32 devices in a mesh: shard: 4 (over y, x), ctx: 2 (over core), tp: 4 (over z).
Axes of the slice: x: 2, y: 2, z: 4, core: 2. Of those that a mesh axis runs over, the one named last changes fastest.
Arguments:
- inputs: bfloat16 [8192, 768], P(('shard', 'ctx', 'tp')), may hold values from -6 to 6
- encoder: bfloat16 [8192, 768], P(('shard', 'ctx', 'tp')), may hold values from -6 to 6
- prefix: int32 [4], P('shard'), may hold values from 204 to 1024
- targets: int32 [8192], P(('shard', 'ctx')), may hold values from 0 to 32127
- cotangent: bfloat16 [8192, 768], P(('shard', 'ctx', 'tp')), may hold values from -6 to 6
- gain_self: bfloat16 [768], P('shard'), may hold values from 0.5 to 1.5
- query_self: bfloat16 [768, 768], P('shard', 'tp'), may hold values from -0.3125 to 0.3125
- key_self: bfloat16 [768, 768], P('shard', 'tp'), may hold values from -0.3125 to 0.3125
- value_self: bfloat16 [768, 768], P('shard', 'tp'), may hold values from -0.21875 to 0.21875
- output_self: bfloat16 [768, 768], P('tp', 'shard'), may hold values from -0.875 to 0.875
- gain_cross: bfloat16 [768], P('shard'), may hold values from 0.5 to 1.5
- query_cross: bfloat16 [768, 768], P('shard', 'tp'), may hold values from -0.3125 to 0.3125
- key_cross: bfloat16 [768, 768], P('shard', 'tp'), may hold values from -0.3125 to 0.3125
- value_cross: bfloat16 [768, 768], P('shard', 'tp'), may hold values from -0.21875 to 0.21875
- output_cross: bfloat16 [768, 768], P('tp', 'shard'), may hold values from -1.25 to 1.25
- gain_hidden: bfloat16 [768], P('shard'), may hold values from 0.5 to 1.5
- gate_weight: bfloat16 [768, 2048], P('shard', 'tp'), may hold values from -0.21875 to 0.21875
- up_weight: bfloat16 [768, 2048], P('shard', 'tp'), may hold values from -0.21875 to 0.21875
- down_weight: bfloat16 [2048, 768], P('tp', 'shard'), may hold values from -0.25 to 0.25
- gain_exit: bfloat16 [768], P('shard'), may hold values from 0.5 to 1.5
- embedding: bfloat16 [32128, 768], P('tp', 'shard'), may hold values from -9 to 9
Outputs:
- layer_output: bfloat16 [8192, 768], P(('shard', 'ctx', 'tp'))
- exit_loss: float32 [8192], P(('shard', 'ctx'))
- inputs_grad: float32 [8192, 768], P(('shard', 'ctx', 'tp'))
- encoder_grad: float32 [8192, 768], P(('shard', 'ctx', 'tp'))
- gain_self_grad: float32 [768], P('shard')
- query_self_grad: float32 [768, 768], P('shard', 'tp')
- key_self_grad: float32 [768, 768], P('shard', 'tp')
- value_self_grad: float32 [768, 768], P('shard', 'tp')
- output_self_grad: float32 [768, 768], P('tp', 'shard')
- gain_cross_grad: float32 [768], P('shard')
- query_cross_grad: float32 [768, 768], P('shard', 'tp')
- key_cross_grad: float32 [768, 768], P('shard', 'tp')
- value_cross_grad: float32 [768, 768], P('shard', 'tp')
- output_cross_grad: float32 [768, 768], P('tp', 'shard')
- gain_hidden_grad: float32 [768], P('shard')
- gate_weight_grad: float32 [768, 2048], P('shard', 'tp')
- up_weight_grad: float32 [768, 2048], P('shard', 'tp')
- down_weight_grad: float32 [2048, 768], P('tp', 'shard')
- gain_exit_grad: float32 [768], P('shard')
- embedding_grad: float32 [32128, 768], P('tp', 'shard')
The draws below stay inside these ranges and needn't reach their ends.
All inputs are finite; a program needn't handle non-finite values.
Results may differ from the reference program's by a relative error of at most 0.028.
Values may be sent and summed in bfloat16 or wider, within the bound.
A program may use at most 256 MiB of HBM per device.

```python
import jax
import jax.numpy as jnp
from jax import lax

D = 768
HEADS = 12
HEAD_DIM = 64
FF = 2048
VOCAB = 32128
LEN = 2048
ENC_LEN = 2048
SEQS = 4
TOKENS = 8192
ENC_TOKENS = 8192


def place_ends(array, rng, smallest, high):
    extent = array.shape
    index_at = [jax.random.randint(jax.random.fold_in(rng, axis), (), 0, extent[axis]) for axis in range(len(extent))]
    array = array.at[tuple(index_at)].set(smallest)
    longest = extent.index(max(extent))
    index_at[longest] = (index_at[longest] + 1) % extent[longest]
    return array.at[tuple(index_at)].set(high)


def steps_of(own_key, dims, cuts, smallest, high):
    level = 1.0
    for position, blocks in cuts:
        steps = jax.random.uniform(jax.random.fold_in(jax.random.fold_in(own_key, 6), position), (blocks,), jnp.float32, smallest / len(cuts), high / len(cuts))
        level = level * jnp.repeat(jnp.exp(steps), dims[position] // blocks).reshape((-1,) + (1,) * (len(dims) - 1 - position))
    return level


def normal_values(own_key, shape, scale, most, cuts=(), kind=jnp.bfloat16):
    values = scale * jax.random.normal(own_key, shape, jnp.float32)
    if cuts:
        values = values * steps_of(own_key, shape, cuts, -0.22, 0.18)
    return jnp.clip(values, -most, most).astype(kind)


def setup_inputs(seed: int = 0) -> dict:
    key_list = jax.random.split(jax.random.key(seed), 22)
    inputs = normal_values(key_list[0], (TOKENS, D), 1.0, 6.0, ((0, 32),))
    encoder = normal_values(key_list[1], (ENC_TOKENS, D), 1.0, 6.0, ((0, 32),))
    prefix = place_ends(jax.random.randint(key_list[2], (SEQS,), LEN // 10, LEN // 2 + 1), jax.random.fold_in(key_list[2], 1), LEN // 10, (LEN // 2 + 1) - 1).astype(jnp.int32)
    targets = place_ends(jax.random.randint(key_list[3], (TOKENS,), 0, VOCAB), jax.random.fold_in(key_list[3], 1), 0, VOCAB - 1).astype(jnp.int32)
    cotangent = normal_values(key_list[4], (TOKENS, D), 1.0, 6.0, ((0, 32),))
    gain_self = jnp.clip(1.0 + 0.1 * jax.random.normal(key_list[5], (D,), jnp.float32), 0.5, 1.5).astype(jnp.bfloat16)
    query_self = normal_values(key_list[6], (D, HEADS * HEAD_DIM), (D // 2) ** -0.5, 0.3125, ((0, 4), (1, 4)))
    key_self = normal_values(key_list[7], (D, HEADS * HEAD_DIM), (D // 2) ** -0.5, 0.3125, ((0, 4), (1, 4)))
    value_self = normal_values(key_list[8], (D, HEADS * HEAD_DIM), D ** -0.5, 0.21875, ((0, 4), (1, 4)))
    output_self = normal_values(key_list[9], (HEADS * HEAD_DIM, D), (HEADS * HEAD_DIM // 16) ** -0.5, 0.875, ((0, 4), (1, 4)))
    gain_cross = jnp.clip(1.0 + 0.1 * jax.random.normal(key_list[10], (D,), jnp.float32), 0.5, 1.5).astype(jnp.bfloat16)
    query_cross = normal_values(key_list[11], (D, HEADS * HEAD_DIM), (D // 2) ** -0.5, 0.3125, ((0, 4), (1, 4)))
    key_cross = normal_values(key_list[12], (D, HEADS * HEAD_DIM), (D // 2) ** -0.5, 0.3125, ((0, 4), (1, 4)))
    value_cross = normal_values(key_list[13], (D, HEADS * HEAD_DIM), D ** -0.5, 0.21875, ((0, 4), (1, 4)))
    output_cross = normal_values(key_list[14], (HEADS * HEAD_DIM, D), (HEADS * HEAD_DIM // 32) ** -0.5, 1.25, ((0, 4), (1, 4)))
    gain_hidden = jnp.clip(1.0 + 0.1 * jax.random.normal(key_list[15], (D,), jnp.float32), 0.5, 1.5).astype(jnp.bfloat16)
    gate_weight = normal_values(key_list[16], (D, FF), D ** -0.5, 0.21875, ((0, 4), (1, 4)))
    up_weight = normal_values(key_list[17], (D, FF), D ** -0.5, 0.21875, ((0, 4), (1, 4)))
    down_weight = normal_values(key_list[18], (FF, D), (FF // 4) ** -0.5, 0.25, ((0, 4), (1, 4)))
    gain_exit = jnp.clip(1.0 + 0.1 * jax.random.normal(key_list[19], (D,), jnp.float32), 0.5, 1.5).astype(jnp.bfloat16)
    embedding = normal_values(key_list[20], (VOCAB, D), 1.5, 9.0, ((0, 4), (1, 4)))
    return {"inputs": inputs, "encoder": encoder, "prefix": prefix, "targets": targets, "cotangent": cotangent, "gain_self": gain_self, "query_self": query_self, "key_self": key_self, "value_self": value_self, "output_self": output_self, "gain_cross": gain_cross, "query_cross": query_cross, "key_cross": key_cross, "value_cross": value_cross, "output_cross": output_cross, "gain_hidden": gain_hidden, "gate_weight": gate_weight, "up_weight": up_weight, "down_weight": down_weight, "gain_exit": gain_exit, "embedding": embedding}


@jax.custom_vjp
def low(v):
    return lax.optimization_barrier(v.astype(jnp.bfloat16)).astype(jnp.float32)

@jax.custom_vjp
def low_back(v):
    return v

def low_keep(v):
    return (low(v), None)

def low_pass(kept, grad):
    return (grad,)

def back_keep(v):
    return (v, None)

def back_low(kept, grad):
    return (low(grad),)
low.defvjp(low_keep, low_pass)
low_back.defvjp(back_keep, back_low)
EPS = 1e-06
MASKED = -1e+30
HIGH = lax.Precision.HIGHEST

def both(value):
    return low(low_back(value))

def product(left, right):
    return jnp.dot(left, right, precision=HIGH)

def rms_scale(hidden, gain):
    return hidden * lax.rsqrt(lax.optimization_barrier(jnp.mean(hidden * hidden, axis=-1, keepdims=True)) + EPS) * gain

def attention(query, keys, values, visible_fn):
    rows = query.shape[0]
    block = min(512, rows)
    query_h = query.reshape(rows // block, block, HEADS, HEAD_DIM)
    keys_h = keys.reshape(keys.shape[0], HEADS, HEAD_DIM)
    values_h = values.reshape(values.shape[0], HEADS, HEAD_DIM)
    starts = jnp.arange(rows // block, dtype=jnp.int32) * block

    def one_block(args):
        part, start = args
        scores = jnp.einsum('qhd,khd->hqk', part, keys_h, precision=HIGH) * HEAD_DIM ** (-0.5)
        scores = low_back(jnp.where(visible_fn(start, block)[None], scores, MASKED))
        probs = low(jax.nn.softmax(scores, axis=-1))
        return jnp.einsum('hqk,khd->qhd', probs, values_h, precision=HIGH)
    result = lax.map(jax.checkpoint(one_block), (query_h, starts))
    return result.reshape(rows, HEADS * HEAD_DIM)

def exit_losses(normed, embedding, targets_seq):
    rows = normed.shape[0]
    block = min(512, rows)

    def one_block(args):
        part, chosen = args
        logits = low_back(product(part, embedding.T) * D ** (-0.5))
        top = lax.optimization_barrier(jnp.max(logits, axis=-1))
        total = top + jnp.log(lax.optimization_barrier(jnp.sum(jnp.exp(logits - top[:, None]), axis=-1)))
        picked = jnp.take_along_axis(logits, chosen[:, None], axis=1)[:, 0]
        return total - picked
    parts = normed.reshape(rows // block, block, D)
    chosen_all = targets_seq.reshape(rows // block, block)
    return lax.map(jax.checkpoint(one_block), (parts, chosen_all)).reshape(rows)

def sequence_layer(weights, inputs_seq, encoder_seq, limit, targets_seq):
    gain_self, query_self, key_self, value_self, output_self, gain_cross, query_cross, key_cross, value_cross, output_cross, gain_hidden, gate_weight, up_weight, down_weight, gain_exit, embedding = weights
    positions = jnp.arange(LEN, dtype=jnp.int32)

    def causal(start, count):
        rows = start + jnp.arange(count, dtype=jnp.int32)
        return (positions[None, :] <= rows[:, None]) | (positions[None, :] < limit)

    def open_all(start, count):
        return jnp.ones((count, ENC_LEN), dtype=jnp.bool_)
    normed1 = low(rms_scale(inputs_seq, gain_self))
    query1 = both(product(normed1, query_self))
    key1 = both(product(normed1, key_self))
    value1 = both(product(normed1, value_self))
    attended1 = both(attention(query1, key1, value1, causal))
    hidden1 = inputs_seq + low_back(product(attended1, output_self))
    normed2 = low(rms_scale(hidden1, gain_cross))
    query2 = both(product(normed2, query_cross))
    key2 = both(product(encoder_seq, key_cross))
    value2 = both(product(encoder_seq, value_cross))
    attended2 = both(attention(query2, key2, value2, open_all))
    hidden2 = hidden1 + low_back(product(attended2, output_cross))
    normed3 = low(rms_scale(hidden2, gain_hidden))
    gate = low_back(product(normed3, gate_weight))
    upper = low_back(product(normed3, up_weight))
    activation = low(jax.nn.gelu(gate, approximate=True) * upper)
    final = hidden2 + low_back(product(activation, down_weight))
    normed4 = low(rms_scale(final, gain_exit))
    losses = exit_losses(normed4, embedding, targets_seq)
    return (final, losses)

def reference(inputs, encoder, prefix, targets, cotangent, gain_self, query_self, key_self, value_self, output_self, gain_cross, query_cross, key_cross, value_cross, output_cross, gain_hidden, gate_weight, up_weight, down_weight, gain_exit, embedding):
    listed = (gain_self, query_self, key_self, value_self, output_self, gain_cross, query_cross, key_cross, value_cross, output_cross, gain_hidden, gate_weight, up_weight, down_weight, gain_exit, embedding)
    weights = tuple((item.astype(jnp.float32) for item in listed))
    inputs_f = inputs.astype(jnp.float32).reshape(SEQS, LEN, D)
    encoder_f = encoder.astype(jnp.float32).reshape(SEQS, ENC_LEN, D)
    targets_s = targets.reshape(SEQS, LEN)

    def whole(weights, inputs_f, encoder_f):

        def per_sequence(args):
            inputs_seq, encoder_seq, limit, targets_seq = args
            return sequence_layer(weights, inputs_seq, encoder_seq, limit, targets_seq)
        return lax.map(jax.checkpoint(per_sequence), (inputs_f, encoder_f, prefix, targets_s))
    (final, losses), pull = jax.vjp(whole, weights, inputs_f, encoder_f)
    grads, inputs_grad, encoder_grad = pull((cotangent.astype(jnp.float32).reshape(SEQS, LEN, D), jnp.ones_like(losses)))
    return (final.reshape(TOKENS, D).astype(jnp.bfloat16), losses.reshape(TOKENS), inputs_grad.reshape(TOKENS, D), encoder_grad.reshape(ENC_TOKENS, D), grads[0], grads[1], grads[2], grads[3], grads[4], grads[5], grads[6], grads[7], grads[8], grads[9], grads[10], grads[11], grads[12], grads[13], grads[14], grads[15])
```

```python
from functools import partial

import jax
import jax.numpy as jnp
from jax import lax
from jax.experimental import pallas as pl
from jax.experimental.pallas import tpu as pltpu
from jax.sharding import PartitionSpec as P

HEAD_DIM = 64
EPS = 1e-06
MASKED = -1e30
BF = jnp.bfloat16
F32 = jnp.float32
VMEM_LIMIT = 58 * 2**20


def attend_kernel(limit_ref, seen_ref, qt_ref, k_ref, vt_ref, o_ref, ot_ref, lse_ref, *, masked, blocks, chunk):
    half = lax.broadcasted_iota(jnp.int32, (2 * HEAD_DIM, 1), 0) // HEAD_DIM
    for head in range(2):
        part = slice(head * HEAD_DIM, (head + 1) * HEAD_DIM)
        for index, (first, count) in enumerate(blocks):
            columns = slice(first, first + count)
            qt = jnp.where(half == head, qt_ref[:, columns], 0).astype(BF)

            def step(i, carry):
                top, total, acc = carry
                start = pl.multiple_of(i * chunk, chunk)
                scores = jnp.dot(k_ref[pl.ds(start, chunk), :], qt, preferred_element_type=F32)
                if masked:
                    key = lax.broadcasted_iota(jnp.int32, (chunk, 1), 0) + start
                    scores = jnp.where(key < seen_ref[:, columns], scores, MASKED)
                new_top = jnp.maximum(top, jnp.max(scores, axis=0, keepdims=True))
                expo = jnp.exp(scores - new_top)
                shrink = jnp.exp(top - new_top)
                total = total * shrink + jnp.sum(expo, axis=0, keepdims=True)
                acc = acc * shrink + jnp.dot(
                    vt_ref[part, pl.ds(start, chunk)], expo.astype(BF), preferred_element_type=F32
                )
                return (new_top, total, acc)

            init = (
                jnp.full((1, count), MASKED, F32),
                jnp.zeros((1, count), F32),
                jnp.zeros((HEAD_DIM, count), F32),
            )
            if masked:
                top, total, acc = lax.fori_loop(0, limit_ref[index], step, init)
            else:
                top, total, acc = lax.fori_loop(0, k_ref.shape[0] // chunk, step, init, unroll=True)
            ot_ref[part, columns] = acc / total
            lse_ref[0, head : head + 1, columns] = top + jnp.log(total)
    o_ref[...] = jnp.transpose(ot_ref[...]).astype(BF)


def attend(limit, seen, qt, keys, values_t, masked, blocks, chunk):
    width, rows = qt.shape
    count = keys.shape[0]
    pairs = width // (2 * HEAD_DIM)
    pair = 2 * HEAD_DIM
    return pl.pallas_call(
        partial(attend_kernel, masked=masked, blocks=blocks, chunk=chunk),
        grid_spec=pltpu.PrefetchScalarGridSpec(
            num_scalar_prefetch=1,
            grid=(pairs,),
            in_specs=[
                pl.BlockSpec((1, rows), lambda p, lim: (0, 0)),
                pl.BlockSpec((pair, rows), lambda p, lim: (p, 0)),
                pl.BlockSpec((count, pair), lambda p, lim: (0, p)),
                pl.BlockSpec((pair, count), lambda p, lim: (p, 0)),
            ],
            out_specs=[
                pl.BlockSpec((rows, pair), lambda p, lim: (0, p)),
                pl.BlockSpec((pair, rows), lambda p, lim: (p, 0)),
                pl.BlockSpec((1, 8, rows), lambda p, lim: (p, 0, 0)),
            ],
        ),
        out_shape=(
            jax.ShapeDtypeStruct((rows, width), BF),
            jax.ShapeDtypeStruct((width, rows), F32),
            jax.ShapeDtypeStruct((pairs, 8, rows), F32),
        ),
        compiler_params=pltpu.CompilerParams(vmem_limit_bytes=VMEM_LIMIT),
        cost_estimate=pl.CostEstimate(
            flops=4 * rows * count * width, transcendentals=rows * count * width // HEAD_DIM,
            bytes_accessed=2 * count * width * 2 + 8 * rows * width,
        ),
        name="attend",
    )(limit, seen, qt, keys, values_t)


def attend_back_kernel(
    limit_ref, seen_ref, qt_ref, q_ref, k_ref, kt_ref, v_ref, do_ref, dot_ref, ot_ref, lse_ref,
    dq_ref, dk_ref, dv_ref, dk_acc, dv_acc, dqt_acc, *, masked, blocks, chunk,
):
    half = lax.broadcasted_iota(jnp.int32, (2 * HEAD_DIM, 1), 0) // HEAD_DIM
    lane = lax.broadcasted_iota(jnp.int32, (1, 2 * HEAD_DIM), 1) // HEAD_DIM
    dk_acc[...] = jnp.zeros_like(dk_acc)
    dv_acc[...] = jnp.zeros_like(dv_acc)
    for head in range(2):
        part = slice(head * HEAD_DIM, (head + 1) * HEAD_DIM)
        for index, (first, count) in enumerate(blocks):
            columns = slice(first, first + count)
            qt = jnp.where(half == head, qt_ref[:, columns], 0).astype(BF)
            dot_t = jnp.where(half == head, dot_ref[:, columns], 0).astype(BF)
            q = jnp.where(lane == head, q_ref[columns, :], 0).astype(BF)
            do = jnp.where(lane == head, do_ref[columns, :], 0).astype(BF)
            inner = jnp.sum(
                dot_ref[part, columns].astype(F32) * ot_ref[part, columns], axis=0, keepdims=True
            )
            lse = lse_ref[0, head : head + 1, columns]

            def step(i, acc):
                start = pl.multiple_of(i * chunk, chunk)
                here = pl.ds(start, chunk)
                scores = jnp.dot(k_ref[here, :], qt, preferred_element_type=F32)
                probs = jnp.exp(scores - lse)
                if masked:
                    key = lax.broadcasted_iota(jnp.int32, (chunk, 1), 0) + start
                    probs = jnp.where(key < seen_ref[:, columns], probs, 0.0)
                grad_probs = jnp.dot(v_ref[here, :], dot_t, preferred_element_type=F32)
                grad_scores = (probs * (grad_probs - inner)).astype(BF)
                dv_acc[here, :] += jnp.dot(probs.astype(BF), do, preferred_element_type=F32)
                dk_acc[here, :] += jnp.dot(grad_scores, q, preferred_element_type=F32)
                return acc + jnp.dot(kt_ref[part, here], grad_scores, preferred_element_type=F32)

            init = jnp.zeros((HEAD_DIM, count), F32)
            if masked:
                acc = lax.fori_loop(0, limit_ref[index], step, init)
            else:
                acc = lax.fori_loop(0, k_ref.shape[0] // chunk, step, init, unroll=True)
            dqt_acc[part, columns] = acc * HEAD_DIM**-0.5
    dq_ref[...] = jnp.transpose(dqt_acc[...]).astype(BF)
    dk_ref[...] = dk_acc[...].astype(BF)
    dv_ref[...] = dv_acc[...].astype(BF)


def attend_back(limit, seen, qt, query, keys, keys_t, values, grad, grad_t, out_t, lse, masked, blocks, chunk):
    width, rows = qt.shape
    count = keys.shape[0]
    pairs = width // (2 * HEAD_DIM)
    pair = 2 * HEAD_DIM
    by_row = pl.BlockSpec((pair, rows), lambda p, lim: (p, 0))
    by_column = pl.BlockSpec((rows, pair), lambda p, lim: (0, p))
    key_spec = pl.BlockSpec((count, pair), lambda p, lim: (0, p))
    return pl.pallas_call(
        partial(attend_back_kernel, masked=masked, blocks=blocks, chunk=chunk),
        grid_spec=pltpu.PrefetchScalarGridSpec(
            num_scalar_prefetch=1,
            grid=(pairs,),
            in_specs=[
                pl.BlockSpec((1, rows), lambda p, lim: (0, 0)),
                by_row,
                by_column,
                key_spec,
                pl.BlockSpec((pair, count), lambda p, lim: (p, 0)),
                key_spec,
                by_column,
                by_row,
                by_row,
                pl.BlockSpec((1, 8, rows), lambda p, lim: (p, 0, 0)),
            ],
            out_specs=[by_column, key_spec, key_spec],
            scratch_shapes=[
                pltpu.VMEM((count, pair), F32),
                pltpu.VMEM((count, pair), F32),
                pltpu.VMEM((pair, rows), F32),
            ],
        ),
        out_shape=(
            jax.ShapeDtypeStruct((rows, width), BF),
            jax.ShapeDtypeStruct((count, width), BF),
            jax.ShapeDtypeStruct((count, width), BF),
        ),
        compiler_params=pltpu.CompilerParams(vmem_limit_bytes=VMEM_LIMIT),
        cost_estimate=pl.CostEstimate(
            flops=10 * rows * count * width, transcendentals=rows * count * width // HEAD_DIM,
            bytes_accessed=5 * count * width * 2 + 14 * rows * width,
        ),
        name="attend_back",
    )(limit, seen, qt, query, keys, keys_t, values, grad, grad_t, out_t, lse)


def head_stats_kernel(pieces_ref, nt_ref, target_ref, stats_ref, emb_ref, *, vocab, block, rows, scale):
    step = pl.program_id(0)
    ids = lax.broadcasted_iota(jnp.int32, (block, 1), 0) + step * block
    emb = jnp.concatenate([pieces_ref[g] for g in range(pieces_ref.shape[0])], axis=1)
    emb = jnp.where(ids < vocab, emb, 0).astype(BF)
    emb_ref[...] = emb

    @pl.when(step == 0)
    def _():
        stats_ref[0:1, :] = jnp.full((1, stats_ref.shape[1]), MASKED, F32)
        stats_ref[1:8, :] = jnp.zeros((7, stats_ref.shape[1]), F32)

    for first in range(0, nt_ref.shape[1], rows):
        columns = slice(first, first + rows)
        logits = jnp.dot(emb, nt_ref[:, columns], preferred_element_type=F32) * scale
        logits = jnp.where(ids < vocab, logits, MASKED)
        hit = (ids == target_ref[:, columns]) & (ids < vocab)
        top = stats_ref[0:1, columns]
        new_top = jnp.maximum(top, jnp.max(logits, axis=0, keepdims=True))
        stats_ref[0:1, columns] = new_top
        stats_ref[1:2, columns] = stats_ref[1:2, columns] * jnp.exp(top - new_top) + jnp.sum(
            jnp.exp(logits - new_top), axis=0, keepdims=True
        )
        stats_ref[2:3, columns] += jnp.sum(jnp.where(hit, logits, 0.0), axis=0, keepdims=True)


def head_stats(pieces, normed_t, target, block, rows):
    groups, vocab, width = pieces.shape
    depth, total = normed_t.shape
    steps = pl.cdiv(vocab, block)
    return pl.pallas_call(
        partial(head_stats_kernel, vocab=vocab, block=block, rows=rows, scale=depth**-0.5),
        grid=(steps,),
        in_specs=[
            pl.BlockSpec((groups, block, width), lambda i: (0, i, 0)),
            pl.BlockSpec((depth, total), lambda i: (0, 0)),
            pl.BlockSpec((1, total), lambda i: (0, 0)),
        ],
        out_specs=[
            pl.BlockSpec((8, total), lambda i: (0, 0)),
            pl.BlockSpec((block, depth), lambda i: (i, 0)),
        ],
        out_shape=(
            jax.ShapeDtypeStruct((8, total), F32),
            jax.ShapeDtypeStruct((steps * block, depth), BF),
        ),
        compiler_params=pltpu.CompilerParams(vmem_limit_bytes=VMEM_LIMIT),
        cost_estimate=pl.CostEstimate(
            flops=2 * vocab * depth * total, transcendentals=vocab * total,
            bytes_accessed=4 * vocab * depth + 2 * depth * total,
        ),
        name="head_stats",
    )(pieces, normed_t, target)


def head_back_kernel(emb_ref, nt_ref, n_ref, target_ref, lse_ref, de_ref, dn_ref, dnt_acc, *, vocab, block, rows, scale):
    step = pl.program_id(0)
    ids = lax.broadcasted_iota(jnp.int32, (block, 1), 0) + step * block
    emb = emb_ref[...]
    emb_t = jnp.transpose(emb)

    @pl.when(step == 0)
    def _():
        dnt_acc[...] = jnp.zeros_like(dnt_acc)

    de = None
    for first in range(0, nt_ref.shape[1], rows):
        columns = slice(first, first + rows)
        logits = jnp.dot(emb, nt_ref[:, columns], preferred_element_type=F32) * scale
        probs = jnp.exp(logits - lse_ref[:, columns])
        probs = jnp.where(ids == target_ref[:, columns], probs - 1.0, probs)
        grad = jnp.where(ids < vocab, probs, 0.0).astype(BF)
        term = jnp.dot(grad, n_ref[columns, :], preferred_element_type=F32)
        de = term if de is None else de + term
        dnt_acc[:, columns] += jnp.dot(emb_t, grad, preferred_element_type=F32)
    de = (de * scale).astype(BF)
    width = de_ref.shape[2]
    for g in range(de_ref.shape[0]):
        de_ref[g] = de[:, g * width : (g + 1) * width]

    @pl.when(step == pl.num_programs(0) - 1)
    def _():
        dn_ref[...] = (jnp.transpose(dnt_acc[...]) * scale).astype(BF)


def head_back(emb, normed_t, normed, target, lse, groups, vocab, block, rows):
    depth, total = normed_t.shape
    steps = pl.cdiv(vocab, block)
    width = depth // groups
    return pl.pallas_call(
        partial(head_back_kernel, vocab=vocab, block=block, rows=rows, scale=depth**-0.5),
        grid=(steps,),
        in_specs=[
            pl.BlockSpec((block, depth), lambda i: (i, 0)),
            pl.BlockSpec((depth, total), lambda i: (0, 0)),
            pl.BlockSpec((total, depth), lambda i: (0, 0)),
            pl.BlockSpec((1, total), lambda i: (0, 0)),
            pl.BlockSpec((1, total), lambda i: (0, 0)),
        ],
        out_specs=[
            pl.BlockSpec((groups, block, width), lambda i: (0, i, 0)),
            pl.BlockSpec((total, depth), lambda i: (0, 0)),
        ],
        out_shape=(
            jax.ShapeDtypeStruct((groups, vocab, width), BF),
            jax.ShapeDtypeStruct((total, depth), BF),
        ),
        scratch_shapes=[pltpu.VMEM((depth, total), F32)],
        compiler_params=pltpu.CompilerParams(vmem_limit_bytes=VMEM_LIMIT),
        cost_estimate=pl.CostEstimate(
            flops=6 * vocab * depth * total, transcendentals=vocab * total,
            bytes_accessed=4 * vocab * depth + 6 * depth * total,
        ),
        name="head_back",
    )(emb, normed_t, normed, target, lse)


def normalize(hidden, gain):
    inverse = lax.rsqrt(jnp.mean(hidden * hidden, axis=-1, keepdims=True) + EPS)
    return (hidden * inverse * gain, inverse)


def norm_back(hidden, inverse, gain, upstream):
    scaled = upstream * gain
    inner = jnp.mean(scaled * hidden, axis=-1, keepdims=True)
    return inverse * scaled - hidden * (inverse * inverse * inverse) * inner


def matmul(left, right):
    return jnp.dot(left, right, preferred_element_type=F32)


def left_t(left, right):
    return jnp.einsum("ra,rb->ab", left, right, preferred_element_type=F32)


def right_t(left, right):
    return jnp.einsum("ra,ba->rb", left, right, preferred_element_type=F32)


def swap(array):
    return lax.ppermute(array, "ctx", [(0, 1), (1, 0)])


def per_device(
    inputs, encoder, prefix, targets, cotangent, gain_self, query_self, key_self, value_self, output_self,
    gain_cross, query_cross, key_cross, value_cross, output_cross, gain_hidden, gate_weight, up_weight,
    down_weight, gain_exit, embedding,
):
    tp = lax.axis_size("tp")
    ctx = lax.axis_size("ctx")
    shards = lax.axis_size("shard")
    assert tp == 4 and ctx == 2
    core = lax.axis_index("ctx")
    place = lax.axis_index("tp")
    rows, depth = inputs.shape
    group = rows * tp
    total = group * ctx
    hb = query_self.shape[1]
    width = 2 * hb
    fb = gate_weight.shape[1]
    pair = rows * ctx

    route_a = []
    route_b = []
    for c in range(2):
        for z in range(4):
            dest = c * 4 + z
            route_a.append(((z % 2) * 4 + 2 * c + z // 2, dest))
            route_b.append(((z % 2) * 4 + 2 * c + 1 - z // 2, dest))
    both = ("ctx", "tp")

    def spread_weights(parts):
        block = jnp.concatenate(parts, axis=1)
        first = lax.ppermute(block, both, route_a)
        second = lax.ppermute(block, both, route_b)
        columns = []
        start = 0
        for piece in parts:
            stop = start + piece.shape[1]
            columns += [first[:, start:stop], second[:, start:stop]]
            start = stop
        return lax.all_gather(jnp.concatenate(columns, axis=1), "shard", axis=0, tiled=True)

    def collect_weights(grad, widths):
        mine = lax.psum_scatter(grad, "shard", scatter_dimension=0, tiled=True)
        first = []
        second = []
        start = 0
        for size in widths:
            first.append(mine[:, start : start + size])
            second.append(mine[:, start + size : start + 2 * size])
            start += 2 * size
        back = lambda route: [(dest, source) for source, dest in route]
        one = lax.ppermute(jnp.concatenate(first, axis=1), both, back(route_a))
        two = lax.ppermute(jnp.concatenate(second, axis=1), both, back(route_b))
        part = (one.astype(F32) + two.astype(F32)).astype(BF)
        whole = part.astype(F32) + swap(part).astype(F32)
        outs = []
        start = 0
        for size in widths:
            outs.append(whole[:, start : start + size])
            start += size
        return outs

    def couple(own, other):
        return jnp.where(
            core == 0, jnp.concatenate([own, other], axis=0), jnp.concatenate([other, own], axis=0)
        )

    gains = lax.all_gather(jnp.stack([gain_self, gain_cross, gain_hidden, gain_exit]), "shard", axis=1, tiled=True)
    gain_one, gain_two, gain_three, gain_four = [gains[i].astype(F32) for i in range(4)]

    own_f = inputs.astype(F32)
    normed1_own, inverse1_own = normalize(own_f, gain_one)
    normed1_own = normed1_own.astype(BF)
    normed1 = lax.all_gather(normed1_own, both, axis=0, tiled=True)
    weights_self = spread_weights([query_self, key_self, value_self, output_self.T])
    encoder_all = lax.all_gather(encoder, both, axis=0, tiled=True)
    weights_cross = spread_weights([query_cross, key_cross, value_cross, output_cross.T])
    weights_ff = spread_weights([gate_weight, up_weight, down_weight.T])
    vocab_half = embedding.shape[0] // ctx
    emb_mine = lax.dynamic_slice_in_dim(embedding, core * vocab_half, vocab_half, axis=0)
    emb_pieces = lax.all_gather(emb_mine, "shard", axis=0)
    if shards != 4:
        emb_pieces = jnp.transpose(emb_pieces, (1, 0, 2)).reshape(1, vocab_half, depth)

    hidden0 = couple(inputs, swap(inputs)).astype(F32)
    cotangent_pair = couple(cotangent, swap(cotangent)).astype(F32)
    targets_all = couple(targets, swap(targets))

    def take_pair(array):
        cut = array.reshape(ctx, group, depth)
        return lax.dynamic_slice_in_dim(cut, place * rows, rows, axis=1).reshape(pair, depth)

    normed1_pair = take_pair(normed1)
    query_w, key_w, value_w, out_w = [weights_self[:, i * width : (i + 1) * width] for i in range(4)]
    scale = HEAD_DIM**-0.5

    def project_q(normed, weight):
        query = matmul(normed, weight).astype(BF) * jnp.asarray(scale, BF)
        return query, query.T

    positions = jnp.concatenate(
        [c * group + place * rows + jnp.arange(rows, dtype=jnp.int32) for c in range(2)]
    )
    limit = prefix[0]
    seen = jnp.maximum(positions + 1, limit)[None, :]
    chunk = 512
    last0 = jnp.maximum((place + 1) * rows, limit)
    last1 = jnp.maximum(group + (place + 1) * rows, limit)
    limits = jnp.stack([(last0 + chunk - 1) // chunk, (last1 + chunk - 1) // chunk]).astype(jnp.int32)
    causal_blocks = ((0, rows), (rows, rows))
    open_blocks = ((0, pair),)

    query1, query1_t = project_q(normed1_pair, query_w)
    key1 = matmul(normed1, key_w).astype(BF)
    value1 = matmul(normed1, value_w).astype(BF)
    attended1, attended1_t, lse1 = attend(
        limits, seen, query1_t, key1, value1.T, True, causal_blocks, chunk
    )

    def add_halves(partial_sum):
        part = partial_sum.astype(BF)
        return partial_sum + swap(part).astype(F32)

    hidden1 = hidden0 + add_halves(right_t(attended1, out_w))
    query2_w, key2_w, value2_w, out2_w = [weights_cross[:, i * width : (i + 1) * width] for i in range(4)]
    key2 = matmul(encoder_all, key2_w).astype(BF)
    value2 = matmul(encoder_all, value2_w).astype(BF)
    normed2, inverse2 = normalize(hidden1, gain_two)
    normed2 = normed2.astype(BF)
    query2, query2_t = project_q(normed2, query2_w)
    attended2, attended2_t, lse2 = attend(
        limits, seen, query2_t, key2, value2.T, False, open_blocks, chunk
    )
    hidden2 = hidden1 + add_halves(right_t(attended2, out2_w))
    normed3, inverse3 = normalize(hidden2, gain_three)
    normed3 = normed3.astype(BF)
    gate_w, up_w, down_w = [weights_ff[:, i * 2 * fb : (i + 1) * 2 * fb] for i in range(3)]
    gate = matmul(normed3, gate_w)
    upper = matmul(normed3, up_w)
    active = jax.nn.gelu(gate, approximate=True)
    product = (active * upper).astype(BF)
    final = hidden2 + add_halves(right_t(product, down_w))
    normed4, inverse4 = normalize(final, gain_four)
    normed4 = normed4.astype(BF)

    def mine(array):
        return lax.dynamic_slice_in_dim(array, core * rows, rows, axis=0)

    final_own = mine(final)
    normed4_all = lax.all_gather(mine(normed4), both, axis=0, tiled=True)
    normed4_t = normed4_all.T
    local_target = (targets_all - (place * embedding.shape[0] + core * vocab_half))[None, :].astype(jnp.int32)
    vblock, rblock = 512, 512
    stats, emb = head_stats(emb_pieces, normed4_t, local_target, vblock, rblock)
    every = lax.all_gather(stats[:3], both, axis=0)
    top = jnp.max(every[:, 0], axis=0)
    summed = jnp.sum(every[:, 1] * jnp.exp(every[:, 0] - top[None]), axis=0)
    picked = jnp.sum(every[:, 2], axis=0)
    logsum = top + jnp.log(summed)
    exit_loss = lax.dynamic_slice_in_dim(logsum - picked, core * group, group, axis=0)
    groups = emb_pieces.shape[0]
    emb_grad, grad_normed4 = head_back(
        emb, normed4_t, normed4_all, local_target, logsum[None, :], groups, vocab_half, vblock, rblock
    )
    if shards != 4:
        emb_grad = jnp.transpose(emb_grad.reshape(vocab_half, shards, depth // shards), (1, 0, 2))
    emb_sum = lax.psum_scatter(
        emb_grad.reshape(shards * vocab_half, depth // shards), "shard", scatter_dimension=0, tiled=True
    )
    embedding_grad = couple(emb_sum, swap(emb_sum)).astype(F32)

    gn4_own = lax.psum_scatter(grad_normed4, both, scatter_dimension=0, tiled=True)
    gn4 = couple(gn4_own, swap(gn4_own)).astype(F32)
    gain4_rows = gn4 * final * inverse4
    grad_final = cotangent_pair + norm_back(final, inverse4, gain_four, gn4)
    grad_final_b = grad_final.astype(BF)
    down_grad = left_t(grad_final_b, product).astype(BF)
    grad_product = matmul(grad_final_b, down_w)
    unused, gelu_pull = jax.vjp(partial(jax.nn.gelu, approximate=True), gate)
    grad_gate = gelu_pull(grad_product * upper)[0].astype(BF)
    grad_upper = (grad_product * active).astype(BF)
    gate_grad = left_t(normed3, grad_gate).astype(BF)
    upper_grad = left_t(normed3, grad_upper).astype(BF)
    ff_grads = collect_weights(jnp.concatenate([gate_grad, upper_grad, down_grad], axis=1), [fb, fb, fb])
    gn3 = add_halves(right_t(grad_gate, gate_w) + right_t(grad_upper, up_w))
    gain3_rows = gn3 * hidden2 * inverse3
    grad_hidden2 = grad_final + norm_back(hidden2, inverse3, gain_three, gn3)
    grad_hidden2_b = grad_hidden2.astype(BF)
    out2_grad = left_t(grad_hidden2_b, attended2).astype(BF)
    grad_attended2 = matmul(grad_hidden2_b, out2_w).astype(BF)
    grad_query2, grad_key2, grad_value2 = attend_back(
        limits, seen, query2_t, query2, key2, key2.T, value2, grad_attended2, grad_attended2.T,
        attended2_t, lse2, False, open_blocks, chunk,
    )
    query2_grad = left_t(normed2, grad_query2).astype(BF)
    key2_grad = left_t(encoder_all, grad_key2).astype(BF)
    value2_grad = left_t(encoder_all, grad_value2).astype(BF)
    cross_grads = collect_weights(
        jnp.concatenate([query2_grad, key2_grad, value2_grad, out2_grad], axis=1), [hb] * 4
    )
    encoder_part = (right_t(grad_key2, key2_w) + right_t(grad_value2, value2_w)).astype(BF)
    encoder_grad = lax.psum_scatter(encoder_part, both, scatter_dimension=0, tiled=True).astype(F32)
    gn2 = add_halves(right_t(grad_query2, query2_w))
    gain2_rows = gn2 * hidden1 * inverse2
    grad_hidden1 = grad_hidden2 + norm_back(hidden1, inverse2, gain_two, gn2)
    grad_hidden1_b = grad_hidden1.astype(BF)
    out_grad = left_t(grad_hidden1_b, attended1).astype(BF)
    grad_attended1 = matmul(grad_hidden1_b, out_w).astype(BF)
    grad_query1, grad_key1, grad_value1 = attend_back(
        limits, seen, query1_t, query1, key1, key1.T, value1, grad_attended1, grad_attended1.T,
        attended1_t, lse1, True, causal_blocks, chunk,
    )
    query_grad = left_t(normed1_pair, grad_query1).astype(BF)
    key_grad = left_t(normed1, grad_key1).astype(BF)
    value_grad = left_t(normed1, grad_value1).astype(BF)
    self_grads = collect_weights(
        jnp.concatenate([query_grad, key_grad, value_grad, out_grad], axis=1), [hb] * 4
    )
    normed1_part = right_t(grad_key1, key_w) + right_t(grad_value1, value_w)
    query_part = right_t(grad_query1, query_w).reshape(ctx, rows, depth)
    cut = normed1_part.reshape(ctx, group, depth)
    old = lax.dynamic_slice_in_dim(cut, place * rows, rows, axis=1)
    cut = lax.dynamic_update_slice_in_dim(cut, old + query_part, place * rows, axis=1)
    gn1 = lax.psum_scatter(
        cut.reshape(total, depth).astype(BF), both, scatter_dimension=0, tiled=True
    ).astype(F32)
    inputs_grad = mine(grad_hidden1) + norm_back(own_f, inverse1_own, gain_one, gn1)
    gain1_sum = jnp.sum(gn1 * own_f * inverse1_own, axis=0)
    gain_sums = jnp.stack(
        [gain1_sum] + [jnp.sum(mine(a), axis=0) for a in (gain2_rows, gain3_rows, gain4_rows)]
    )
    gain_sums = lax.psum(gain_sums, ("shard", "ctx", "tp"))
    part = depth // shards
    gain_grads = lax.dynamic_slice_in_dim(gain_sums, lax.axis_index("shard") * part, part, axis=1)
    return (
        final_own.astype(BF), exit_loss, inputs_grad, encoder_grad,
        gain_grads[0], self_grads[0], self_grads[1], self_grads[2], self_grads[3].T,
        gain_grads[1], cross_grads[0], cross_grads[1], cross_grads[2], cross_grads[3].T,
        gain_grads[2], ff_grads[0], ff_grads[1], ff_grads[2].T,
        gain_grads[3], embedding_grad,
    )


def solution(mesh):
    rows = P(("shard", "ctx", "tp"), None)
    into = P("shard", "tp")
    out = P("tp", "shard")
    gain = P("shard")
    weights = (gain, into, into, into, out, gain, into, into, into, out, gain, into, into, out, gain, out)
    return jax.shard_map(
        per_device,
        mesh=mesh,
        in_specs=(rows, rows, P("shard"), P(("shard", "ctx")), rows) + weights,
        out_specs=(rows, P(("shard", "ctx")), rows, rows) + weights,
        check_vma=False,
    )
```

```python
from functools import partial

import jax
import jax.numpy as jnp
from jax import lax
from jax.experimental import pallas as pl
from jax.experimental.pallas import tpu as pltpu
from jax.sharding import PartitionSpec as P

HEAD_DIM = 64
EPS = 1e-06
MASKED = -1e30
BF = jnp.bfloat16
F32 = jnp.float32
VMEM_LIMIT = 58 * 2**20


def attend_kernel(limit_ref, seen_ref, qt_ref, k_ref, vt_ref, o_ref, ot_ref, lse_ref, *, masked, blocks, chunk):
    half = lax.broadcasted_iota(jnp.int32, (2 * HEAD_DIM, 1), 0) // HEAD_DIM
    for head in range(2):
        part = slice(head * HEAD_DIM, (head + 1) * HEAD_DIM)
        for index, (first, count) in enumerate(blocks):
            columns = slice(first, first + count)
            qt = jnp.where(half == head, qt_ref[:, columns], 0).astype(BF)

            def step(i, carry):
                top, total, acc = carry
                start = pl.multiple_of(i * chunk, chunk)
                scores = jnp.dot(k_ref[pl.ds(start, chunk), :], qt, preferred_element_type=F32)
                if masked:
                    key = lax.broadcasted_iota(jnp.int32, (chunk, 1), 0) + start
                    scores = jnp.where(key < seen_ref[:, columns], scores, MASKED)
                new_top = jnp.maximum(top, jnp.max(scores, axis=0, keepdims=True))
                expo = jnp.exp(scores - new_top)
                shrink = jnp.exp(top - new_top)
                total = total * shrink + jnp.sum(expo, axis=0, keepdims=True)
                acc = acc * shrink + jnp.dot(
                    vt_ref[part, pl.ds(start, chunk)], expo.astype(BF), preferred_element_type=F32
                )
                return (new_top, total, acc)

            init = (
                jnp.full((1, count), MASKED, F32),
                jnp.zeros((1, count), F32),
                jnp.zeros((HEAD_DIM, count), F32),
            )
            if masked:
                top, total, acc = lax.fori_loop(0, limit_ref[index], step, init)
            else:
                top, total, acc = lax.fori_loop(0, k_ref.shape[0] // chunk, step, init, unroll=True)
            ot_ref[part, columns] = acc / total
            lse_ref[0, head : head + 1, columns] = top + jnp.log(total)
    o_ref[...] = jnp.transpose(ot_ref[...]).astype(BF)


def attend(limit, seen, qt, keys, values_t, masked, blocks, chunk):
    width, rows = qt.shape
    count = keys.shape[0]
    pairs = width // (2 * HEAD_DIM)
    pair = 2 * HEAD_DIM
    return pl.pallas_call(
        partial(attend_kernel, masked=masked, blocks=blocks, chunk=chunk),
        grid_spec=pltpu.PrefetchScalarGridSpec(
            num_scalar_prefetch=1,
            grid=(pairs,),
            in_specs=[
                pl.BlockSpec((1, rows), lambda p, lim: (0, 0)),
                pl.BlockSpec((pair, rows), lambda p, lim: (p, 0)),
                pl.BlockSpec((count, pair), lambda p, lim: (0, p)),
                pl.BlockSpec((pair, count), lambda p, lim: (p, 0)),
            ],
            out_specs=[
                pl.BlockSpec((rows, pair), lambda p, lim: (0, p)),
                pl.BlockSpec((pair, rows), lambda p, lim: (p, 0)),
                pl.BlockSpec((1, 8, rows), lambda p, lim: (p, 0, 0)),
            ],
        ),
        out_shape=(
            jax.ShapeDtypeStruct((rows, width), BF),
            jax.ShapeDtypeStruct((width, rows), F32),
            jax.ShapeDtypeStruct((pairs, 8, rows), F32),
        ),
        compiler_params=pltpu.CompilerParams(vmem_limit_bytes=VMEM_LIMIT),
        cost_estimate=pl.CostEstimate(
            flops=4 * rows * count * width, transcendentals=rows * count * width // HEAD_DIM,
            bytes_accessed=2 * count * width * 2 + 8 * rows * width,
        ),
        name="attend",
    )(limit, seen, qt, keys, values_t)


def attend_back_kernel(
    limit_ref, seen_ref, qt_ref, q_ref, k_ref, kt_ref, v_ref, do_ref, dot_ref, ot_ref, lse_ref,
    dq_ref, dk_ref, dv_ref, dk_acc, dv_acc, dqt_acc, *, masked, blocks, chunk,
):
    half = lax.broadcasted_iota(jnp.int32, (2 * HEAD_DIM, 1), 0) // HEAD_DIM
    lane = lax.broadcasted_iota(jnp.int32, (1, 2 * HEAD_DIM), 1) // HEAD_DIM
    dk_acc[...] = jnp.zeros_like(dk_acc)
    dv_acc[...] = jnp.zeros_like(dv_acc)
    for head in range(2):
        part = slice(head * HEAD_DIM, (head + 1) * HEAD_DIM)
        for index, (first, count) in enumerate(blocks):
            columns = slice(first, first + count)
            qt = jnp.where(half == head, qt_ref[:, columns], 0).astype(BF)
            dot_t = jnp.where(half == head, dot_ref[:, columns], 0).astype(BF)
            q = jnp.where(lane == head, q_ref[columns, :], 0).astype(BF)
            do = jnp.where(lane == head, do_ref[columns, :], 0).astype(BF)
            inner = jnp.sum(
                dot_ref[part, columns].astype(F32) * ot_ref[part, columns], axis=0, keepdims=True
            )
            lse = lse_ref[0, head : head + 1, columns]

            def step(i, acc):
                start = pl.multiple_of(i * chunk, chunk)
                here = pl.ds(start, chunk)
                scores = jnp.dot(k_ref[here, :], qt, preferred_element_type=F32)
                probs = jnp.exp(scores - lse)
                if masked:
                    key = lax.broadcasted_iota(jnp.int32, (chunk, 1), 0) + start
                    probs = jnp.where(key < seen_ref[:, columns], probs, 0.0)
                grad_probs = jnp.dot(v_ref[here, :], dot_t, preferred_element_type=F32)
                grad_scores = (probs * (grad_probs - inner)).astype(BF)
                dv_acc[here, :] += jnp.dot(probs.astype(BF), do, preferred_element_type=F32)
                dk_acc[here, :] += jnp.dot(grad_scores, q, preferred_element_type=F32)
                return acc + jnp.dot(kt_ref[part, here], grad_scores, preferred_element_type=F32)

            init = jnp.zeros((HEAD_DIM, count), F32)
            if masked:
                acc = lax.fori_loop(0, limit_ref[index], step, init)
            else:
                acc = lax.fori_loop(0, k_ref.shape[0] // chunk, step, init, unroll=True)
            dqt_acc[part, columns] = acc * HEAD_DIM**-0.5
    dq_ref[...] = jnp.transpose(dqt_acc[...]).astype(BF)
    dk_ref[...] = dk_acc[...].astype(BF)
    dv_ref[...] = dv_acc[...].astype(BF)


def attend_back(limit, seen, qt, query, keys, keys_t, values, grad, grad_t, out_t, lse, masked, blocks, chunk):
    width, rows = qt.shape
    count = keys.shape[0]
    pairs = width // (2 * HEAD_DIM)
    pair = 2 * HEAD_DIM
    by_row = pl.BlockSpec((pair, rows), lambda p, lim: (p, 0))
    by_column = pl.BlockSpec((rows, pair), lambda p, lim: (0, p))
    key_spec = pl.BlockSpec((count, pair), lambda p, lim: (0, p))
    return pl.pallas_call(
        partial(attend_back_kernel, masked=masked, blocks=blocks, chunk=chunk),
        grid_spec=pltpu.PrefetchScalarGridSpec(
            num_scalar_prefetch=1,
            grid=(pairs,),
            in_specs=[
                pl.BlockSpec((1, rows), lambda p, lim: (0, 0)),
                by_row,
                by_column,
                key_spec,
                pl.BlockSpec((pair, count), lambda p, lim: (p, 0)),
                key_spec,
                by_column,
                by_row,
                by_row,
                pl.BlockSpec((1, 8, rows), lambda p, lim: (p, 0, 0)),
            ],
            out_specs=[by_column, key_spec, key_spec],
            scratch_shapes=[
                pltpu.VMEM((count, pair), F32),
                pltpu.VMEM((count, pair), F32),
                pltpu.VMEM((pair, rows), F32),
            ],
        ),
        out_shape=(
            jax.ShapeDtypeStruct((rows, width), BF),
            jax.ShapeDtypeStruct((count, width), BF),
            jax.ShapeDtypeStruct((count, width), BF),
        ),
        compiler_params=pltpu.CompilerParams(vmem_limit_bytes=VMEM_LIMIT),
        cost_estimate=pl.CostEstimate(
            flops=10 * rows * count * width, transcendentals=rows * count * width // HEAD_DIM,
            bytes_accessed=5 * count * width * 2 + 14 * rows * width,
        ),
        name="attend_back",
    )(limit, seen, qt, query, keys, keys_t, values, grad, grad_t, out_t, lse)


def vocab_ids(step, block, vocab):
    row = lax.broadcasted_iota(jnp.int32, (block, 1), 0)
    second = (row >= block // 2).astype(jnp.int32)
    local = row - second * (block // 2) + step * (block // 2)
    return local + second * (vocab // 2), local < vocab // 2


def head_stats_kernel(pieces_ref, nt_ref, target_ref, stats_ref, emb_ref, *, vocab, block, rows, scale):
    step = pl.program_id(0)
    ids, valid = vocab_ids(step, block, vocab)
    width = pieces_ref.shape[2] // 2
    emb = jnp.concatenate(
        [
            jnp.concatenate(
                [pieces_ref[g, :, p * width : (p + 1) * width] for g in range(pieces_ref.shape[0])], axis=1
            )
            for p in range(2)
        ],
        axis=0,
    )
    emb = jnp.where(valid, emb, 0).astype(BF)
    emb_ref[...] = emb

    @pl.when(step == 0)
    def _():
        stats_ref[0:1, :] = jnp.full((1, stats_ref.shape[1]), MASKED, F32)
        stats_ref[1:8, :] = jnp.zeros((7, stats_ref.shape[1]), F32)

    for first in range(0, nt_ref.shape[1], rows):
        columns = slice(first, first + rows)
        logits = jnp.dot(emb, nt_ref[:, columns], preferred_element_type=F32) * scale
        logits = jnp.where(valid, logits, MASKED)
        hit = (ids == target_ref[:, columns]) & valid
        top = stats_ref[0:1, columns]
        new_top = jnp.maximum(top, jnp.max(logits, axis=0, keepdims=True))
        stats_ref[0:1, columns] = new_top
        stats_ref[1:2, columns] = stats_ref[1:2, columns] * jnp.exp(top - new_top) + jnp.sum(
            jnp.exp(logits - new_top), axis=0, keepdims=True
        )
        stats_ref[2:3, columns] += jnp.sum(jnp.where(hit, logits, 0.0), axis=0, keepdims=True)


def head_stats(pieces, normed_t, target, block, rows):
    groups, vocab, width = pieces.shape
    vocab *= 2
    depth, total = normed_t.shape
    steps = pl.cdiv(vocab, block)
    return pl.pallas_call(
        partial(head_stats_kernel, vocab=vocab, block=block, rows=rows, scale=depth**-0.5),
        grid=(steps,),
        in_specs=[
            pl.BlockSpec((groups, block // 2, width), lambda i: (0, i, 0)),
            pl.BlockSpec((depth, total), lambda i: (0, 0)),
            pl.BlockSpec((1, total), lambda i: (0, 0)),
        ],
        out_specs=[
            pl.BlockSpec((8, total), lambda i: (0, 0)),
            pl.BlockSpec((block, depth), lambda i: (i, 0)),
        ],
        out_shape=(
            jax.ShapeDtypeStruct((8, total), F32),
            jax.ShapeDtypeStruct((steps * block, depth), BF),
        ),
        compiler_params=pltpu.CompilerParams(vmem_limit_bytes=VMEM_LIMIT),
        cost_estimate=pl.CostEstimate(
            flops=2 * vocab * depth * total, transcendentals=vocab * total,
            bytes_accessed=4 * vocab * depth + 2 * depth * total,
        ),
        name="head_stats",
    )(pieces, normed_t, target)


def head_back_kernel(emb_ref, nt_ref, n_ref, target_ref, lse_ref, de_ref, dn_ref, dnt_acc, *, vocab, block, rows, scale):
    step = pl.program_id(0)
    ids, valid = vocab_ids(step, block, vocab)
    emb = emb_ref[...]
    emb_t = jnp.transpose(emb)

    @pl.when(step == 0)
    def _():
        dnt_acc[...] = jnp.zeros_like(dnt_acc)

    de = None
    for first in range(0, nt_ref.shape[1], rows):
        columns = slice(first, first + rows)
        logits = jnp.dot(emb, nt_ref[:, columns], preferred_element_type=F32) * scale
        probs = jnp.exp(logits - lse_ref[:, columns])
        probs = jnp.where(ids == target_ref[:, columns], probs - 1.0, probs)
        grad = jnp.where(valid, probs, 0.0).astype(BF)
        term = jnp.dot(grad, n_ref[columns, :], preferred_element_type=F32)
        de = term if de is None else de + term
        dnt_acc[:, columns] += jnp.dot(emb_t, grad, preferred_element_type=F32)
    de = (de * scale).astype(BF)
    width = de_ref.shape[2] // 2
    for g in range(de_ref.shape[0]):
        part = de[:, g * width : (g + 1) * width]
        de_ref[g] = jnp.concatenate([part[: block // 2], part[block // 2 :]], axis=1)

    @pl.when(step == pl.num_programs(0) - 1)
    def _():
        dn_ref[...] = (jnp.transpose(dnt_acc[...]) * scale).astype(BF)


def head_back(emb, normed_t, normed, target, lse, groups, vocab, block, rows):
    depth, total = normed_t.shape
    steps = pl.cdiv(vocab, block)
    width = depth // groups
    return pl.pallas_call(
        partial(head_back_kernel, vocab=vocab, block=block, rows=rows, scale=depth**-0.5),
        grid=(steps,),
        in_specs=[
            pl.BlockSpec((block, depth), lambda i: (i, 0)),
            pl.BlockSpec((depth, total), lambda i: (0, 0)),
            pl.BlockSpec((total, depth), lambda i: (0, 0)),
            pl.BlockSpec((1, total), lambda i: (0, 0)),
            pl.BlockSpec((1, total), lambda i: (0, 0)),
        ],
        out_specs=[
            pl.BlockSpec((groups, block // 2, 2 * width), lambda i: (0, i, 0)),
            pl.BlockSpec((total, depth), lambda i: (0, 0)),
        ],
        out_shape=(
            jax.ShapeDtypeStruct((groups, vocab // 2, 2 * width), BF),
            jax.ShapeDtypeStruct((total, depth), BF),
        ),
        scratch_shapes=[pltpu.VMEM((depth, total), F32)],
        compiler_params=pltpu.CompilerParams(vmem_limit_bytes=VMEM_LIMIT),
        cost_estimate=pl.CostEstimate(
            flops=6 * vocab * depth * total, transcendentals=vocab * total,
            bytes_accessed=4 * vocab * depth + 6 * depth * total,
        ),
        name="head_back",
    )(emb, normed_t, normed, target, lse)


MESH = pl.DeviceIdType.MESH


class Peers:
    def __init__(self):
        self.s, self.c, self.t = (lax.axis_index(name) for name in ("shard", "ctx", "tp"))
        s, c, t = self.s, self.c, self.t
        self.sx = s + 1 - 2 * lax.rem(s, 2)
        self.sy = lax.rem(s + 2, 4)
        self.sd = lax.rem(self.sx + 2, 4)
        self.x = (self.sx, c, t)
        self.y = (self.sy, c, t)
        self.d = (self.sd, c, t)
        self.core = (s, 1 - c, t)
        self.z = [(s, c, lax.rem(t + k, 4)) for k in range(4)]
        self.z_other = [(s, 1 - c, lax.rem(t + k, 4)) for k in range(4)]
        self.group = self.z[1:] + self.z_other
        odd = lax.rem(t, 2)
        self.give = [
            (s, t // 2, 2 * odd + 1 - c),
            (s, t // 2, 2 * (1 - odd) + c),
        ]
        self.back = [
            (s, 1 - odd, 2 * c + t // 2),
            (s, odd, 2 * c + 1 - t // 2),
        ]


def meet(peers):
    barrier = pltpu.get_barrier_semaphore()
    for peer in peers:
        pl.semaphore_signal(barrier, inc=1, device_id=peer, device_id_type=MESH)
    pl.semaphore_wait(barrier, len(peers))


class Sender:
    def __init__(self, sends, arrivals):
        self.sends, self.arrivals, self.count = sends, arrivals, 0
        self.all = []

    def to(self, peer, source, target):
        copy = pltpu.make_async_remote_copy(
            src_ref=source, dst_ref=target, send_sem=self.sends.at[self.count],
            recv_sem=self.arrivals.at[self.count], device_id=peer, device_id_type=MESH,
        )
        self.count += 1
        self.all.append(copy)
        copy.start()
        return copy

    def finish(self):
        for copy in self.all:
            copy.wait_send()


def send_rows(send, me, own, everyone, rows):
    here = everyone.at[pl.ds((me.c * 4 + me.t) * rows, rows)]
    over_z = [send.to(me.z[k], own, here) for k in (1, 2, 3)]
    across = [send.to(me.core, own, here)]
    return over_z, across


def pass_rows(send, me, over_z, across, everyone, rows):
    for k in (1, 2, 3):
        over_z[k - 1].wait_recv()
        there = everyone.at[pl.ds((me.c * 4 + lax.rem(me.t + 4 - k, 4)) * rows, rows)]
        across.append(send.to(me.core, there, there))


def start_kernel(n_ref, e_ref, x_ref, g_ref, t_ref, b0, b1, b2, n_all, e_all, x_pair, g_pair, t_pair, w0, w1, w2, take0, take1, take2, mix0, mix1, mix2, sends, arrivals, local, *, cuts):
    me = Peers()
    meet(me.group + [me.x, me.y])
    send = Sender(sends, arrivals)
    rows = n_ref.shape[0]
    own_rows = pl.ds((me.c * 4 + me.t) * rows, rows)
    locals_ = [
        pltpu.make_async_copy(n_ref, n_all.at[own_rows], local.at[0]),
        pltpu.make_async_copy(e_ref, e_all.at[own_rows], local.at[1]),
    ]
    pairs = []
    for ref, pair in ((x_ref, x_pair), (g_ref, g_pair), (t_ref, t_pair)):
        where = pair.at[pl.ds(me.c * ref.shape[0], ref.shape[0])]
        locals_.append(pltpu.make_async_copy(ref, where, local.at[len(locals_)]))
        pairs.append((ref, where))
    for copy in locals_:
        copy.start()
    bundles = [(b0, take0, mix0, w0), (b1, take1, mix1, w1), (b2, take2, mix2, w2)]

    def give(block, take):
        return [send.to(me.give[i], block, take.at[i]) for i in range(2)]

    given = [give(b0, take0)]
    n_z, n_c = send_rows(send, me, n_ref, n_all, rows)
    given.append(give(b1, take1))
    given.append(give(b2, take2))
    swapped = [send.to(me.core, ref, where) for ref, where in pairs]
    e_z, e_c = send_rows(send, me, e_ref, e_all, rows)
    depth = b0.shape[0]
    half = depth // 2
    mine = pl.ds(me.s * depth, depth)
    over = []
    for i, (block, take, mix, w) in enumerate(bundles):
        for copy in given[i]:
            copy.wait_recv()
        first = take[0]
        second = take[1]
        columns = []
        for start, stop in cuts[i]:
            columns += [first[:, start:stop], second[:, start:stop]]
        mix[...] = jnp.concatenate(columns, axis=1)
        copy = pltpu.make_async_copy(mix, w.at[mine], local.at[len(locals_)])
        copy.start()
        locals_.append(copy)
        over.append((send.to(me.x, mix, w.at[mine]), send.to(me.y, mix, w.at[mine])))
    pass_rows(send, me, n_z, n_c, n_all, rows)
    onward = []
    for i, (block, take, mix, w) in enumerate(bundles):
        to_x, to_y = over[i]
        to_x.wait_recv()
        part = w.at[pl.ds(me.sx * depth, half)]
        onward.append(send.to(me.y, part, part))
        to_y.wait_recv()
        part = w.at[pl.ds(me.sy * depth + half, half)]
        onward.append(send.to(me.x, part, part))
    pass_rows(send, me, e_z, e_c, e_all, rows)
    for copy in onward + n_c + e_c + swapped:
        copy.wait_recv()
    send.finish()
    for copy in locals_:
        copy.wait()


def start_gather(normed, encoder, inputs, cotangent, targets, bundles, cuts):
    rows, depth = normed.shape
    part = bundles[0].shape[0]
    any_space = pl.BlockSpec(memory_space=pl.ANY)
    vmem = pl.BlockSpec(memory_space=pltpu.VMEM)
    return pl.pallas_call(
        partial(start_kernel, cuts=cuts),
        in_specs=[vmem] * 8,
        out_specs=[any_space] * 8,
        out_shape=[jax.ShapeDtypeStruct((8 * rows, depth), BF)] * 2
        + [jax.ShapeDtypeStruct((2 * a.shape[0], a.shape[1]), a.dtype) for a in (inputs, cotangent, targets)]
        + [jax.ShapeDtypeStruct((4 * part, 2 * b.shape[1]), BF) for b in bundles],
        scratch_shapes=[pltpu.VMEM((2,) + b.shape, BF) for b in bundles]
        + [pltpu.VMEM((part, 2 * b.shape[1]), BF) for b in bundles]
        + [pltpu.SemaphoreType.DMA((35,)), pltpu.SemaphoreType.DMA((35,)), pltpu.SemaphoreType.DMA((8,))],
        compiler_params=pltpu.CompilerParams(collective_id=0, has_side_effects=True, vmem_limit_bytes=VMEM_LIMIT),
        name="start_gather",
    )(normed, encoder, inputs, cotangent, targets, *bundles)


def rows_kernel(n_ref, n_all, sends, arrivals, local):
    me = Peers()
    meet(me.z[1:] + [me.core])
    send = Sender(sends, arrivals)
    rows = n_ref.shape[0]
    copy = pltpu.make_async_copy(n_ref, n_all.at[pl.ds((me.c * 4 + me.t) * rows, rows)], local)
    copy.start()
    over_z, across = send_rows(send, me, n_ref, n_all, rows)
    pass_rows(send, me, over_z, across, n_all, rows)
    for arriving in across:
        arriving.wait_recv()
    send.finish()
    copy.wait()


def gather_rows(normed):
    rows, depth = normed.shape
    return pl.pallas_call(
        rows_kernel,
        in_specs=[pl.BlockSpec(memory_space=pltpu.VMEM)],
        out_specs=pl.BlockSpec(memory_space=pl.ANY),
        out_shape=jax.ShapeDtypeStruct((8 * rows, depth), normed.dtype),
        scratch_shapes=[pltpu.SemaphoreType.DMA((8,)), pltpu.SemaphoreType.DMA((8,)), pltpu.SemaphoreType.DMA],
        compiler_params=pltpu.CompilerParams(collective_id=1, has_side_effects=True, vmem_limit_bytes=VMEM_LIMIT),
        name="gather_rows",
    )(normed)


def stats_kernel(stats_ref, out_ref, slots, sends, arrivals):
    me = Peers()
    meet(me.group)
    send = Sender(sends, arrivals)
    here = slots.at[me.c * 4 + me.t]
    slots[me.c * 4 + me.t] = stats_ref[...]
    copies = [send.to(peer, stats_ref, here) for peer in me.group]
    for copy in copies:
        copy.wait_recv()
    top = slots[0, 0:1]
    for i in range(1, 8):
        top = jnp.maximum(top, slots[i, 0:1])
    total = jnp.zeros_like(top)
    picked = jnp.zeros_like(top)
    for i in range(8):
        total += slots[i, 1:2] * jnp.exp(slots[i, 0:1] - top)
        picked += slots[i, 2:3]
    logsum = top + jnp.log(total)
    out_ref[0:1] = logsum
    out_ref[1:2] = logsum - picked
    out_ref[2:8] = jnp.zeros((6, top.shape[1]), F32)
    send.finish()


def combine_stats(stats):
    return pl.pallas_call(
        stats_kernel,
        in_specs=[pl.BlockSpec(memory_space=pltpu.VMEM)],
        out_specs=pl.BlockSpec(memory_space=pltpu.VMEM),
        out_shape=jax.ShapeDtypeStruct(stats.shape, F32),
        scratch_shapes=[pltpu.VMEM((8,) + stats.shape, F32), pltpu.SemaphoreType.DMA((8,)), pltpu.SemaphoreType.DMA((8,))],
        compiler_params=pltpu.CompilerParams(collective_id=2, has_side_effects=True),
        name="combine_stats",
    )(stats)


def settle_first(send, me, part_ref, other, half):
    return send.to(me.core, part_ref.at[pl.ds((1 - me.c) * half, half)], other)


def settle_second(send, me, part_ref, other, summed, landed, rows):
    half = 4 * rows
    for k in range(4):
        start = lax.rem(me.t + k, 4) * rows
        summed[k] = (
            part_ref[pl.ds(me.c * half + start, rows)].astype(F32) + other[pl.ds(start, rows)].astype(F32)
        ).astype(BF)
    return [send.to(me.z[k], summed.at[k], landed.at[k - 1]) for k in (1, 2, 3)]


def settle_third(copies, summed, landed):
    for copy in copies:
        copy.wait_recv()
    return (
        summed[0].astype(F32) + landed[0].astype(F32) + landed[1].astype(F32) + landed[2].astype(F32)
    )


class Planar:
    def __init__(self, send, me, part, first, second, moving, width):
        self.send, self.me, self.part = send, me, part
        self.first, self.second, self.moving = first, second, moving

    def begin(self, chunks):
        me = self.me
        self.chunks = chunks
        self.one = []
        for start, stop, along_x in chunks:
            here = slice(start, stop)
            near, near_block = (me.x, me.sx) if along_x else (me.y, me.sy)
            self.one.append(
                (
                    self.send.to(near, self.part.at[near_block, here], self.first.at[0, here]),
                    self.send.to(near, self.part.at[me.sd, here], self.first.at[1, here]),
                )
            )

    def middle(self):
        me = self.me
        self.two = []
        for (start, stop, along_x), (own, far) in zip(self.chunks, self.one):
            here = slice(start, stop)
            peer, block = (me.y, me.sy) if along_x else (me.x, me.sx)
            far.wait_recv()
            self.moving[here] = (self.part[block, here].astype(F32) + self.first[1, here].astype(F32)).astype(BF)
            self.two.append(self.send.to(peer, self.moving.at[here], self.second.at[here]))
            own.wait_recv()

    def end(self, store):
        me = self.me
        for (start, stop, along_x), copy in zip(self.chunks, self.two):
            here = slice(start, stop)
            copy.wait_recv()
            store(
                here,
                self.part[me.s, here].astype(F32) + self.first[0, here].astype(F32) + self.second[here].astype(F32),
            )


def halves(count, parts, step):
    middle = (count // 2 + step - 1) // step * step
    out = []
    for low, high, along_x in ((0, middle, True), (middle, count, False)):
        size = ((high - low) // parts + step - 1) // step * step
        edges = list(range(low, high, size)) + [high]
        out.append([(a, b, along_x) for a, b in zip(edges[:-1], edges[1:])])
    return [chunk for pair in zip(*out) for chunk in pair]


def middle_kernel(dn_ref, de_ref, gn_ref, eg_ref, other, summed, landed, first, second, moving, sends, arrivals, *, chunks):
    me = Peers()
    meet(me.z[1:] + [me.core, me.x, me.y])
    send = Sender(sends, arrivals)
    rows = landed.shape[1]
    crossing = settle_first(send, me, dn_ref, other, 4 * rows)
    plane = Planar(send, me, de_ref, first, second, moving, None)
    plane.begin(chunks)
    crossing.wait_recv()
    over_z = settle_second(send, me, dn_ref, other, summed, landed, rows)
    plane.middle()
    own = pl.ds(me.c * rows, rows)
    gn_ref[own] = settle_third(over_z, summed, landed).astype(BF)
    share = send.to(me.core, gn_ref.at[own], gn_ref.at[own])
    vocab = de_ref.shape[1]

    def store(here, value):
        eg_ref[pl.ds(me.c * vocab + here.start, here.stop - here.start)] = value.astype(BF)

    plane.end(store)
    mine = pl.ds(me.c * vocab, vocab)
    final = send.to(me.core, eg_ref.at[mine], eg_ref.at[mine])
    share.wait_recv()
    final.wait_recv()
    send.finish()


def middle_scatter(dn, de):
    total, depth = dn.shape
    rows = total // 8
    groups, vocab, width = de.shape
    chunks = halves(vocab, 3, 16)
    count = 1 + 2 * len(chunks) + 3 + len(chunks) + 2
    vmem = pl.BlockSpec(memory_space=pltpu.VMEM)
    return pl.pallas_call(
        partial(middle_kernel, chunks=chunks),
        in_specs=[vmem, vmem],
        out_specs=[vmem, vmem],
        out_shape=[
            jax.ShapeDtypeStruct((2 * rows, depth), BF),
            jax.ShapeDtypeStruct((2 * vocab, width), BF),
        ],
        scratch_shapes=[
            pltpu.VMEM((4 * rows, depth), BF),
            pltpu.VMEM((4, rows, depth), BF),
            pltpu.VMEM((3, rows, depth), BF),
            pltpu.VMEM((2, vocab, width), BF),
            pltpu.VMEM((vocab, width), BF),
            pltpu.VMEM((vocab, width), BF),
            pltpu.SemaphoreType.DMA((count,)),
            pltpu.SemaphoreType.DMA((count,)),
        ],
        compiler_params=pltpu.CompilerParams(collective_id=3, has_side_effects=True, vmem_limit_bytes=VMEM_LIMIT),
        name="middle_scatter",
    )(dn, de)


def tail_kernel(
    dn_ref, g0, g1, f_ref, gains_ref, dn_out, o0, o1, o2, gain_out,
    other, summed, landed, first0, second0, moving0, first1, second1, moving1,
    ab0, ab1, ab2, in0, in1, in2, swap0, swap1, swap2, slots, plane_sum, plane_slots, sends, arrivals, *, cuts, chunks,
):
    me = Peers()
    meet(me.group + [me.x, me.y, me.d])
    send = Sender(sends, arrivals)
    rows = landed.shape[1]
    crossing = settle_first(send, me, dn_ref, other, 4 * rows)
    planes = [
        Planar(send, me, g0, first0, second0, moving0, None),
        Planar(send, me, g1, first1, second1, moving1, None),
    ]
    planes[0].begin(chunks)
    planes[1].begin(chunks)
    slots[me.c * 4 + me.t] = gains_ref[...]
    gain_copies = [send.to(peer, gains_ref, slots.at[me.c * 4 + me.t]) for peer in me.group]

    def split(value, cut, ab):
        for i in range(2):
            ab[i] = jnp.concatenate(
                [value[:, 2 * a + i * (b - a) : 2 * a + (i + 1) * (b - a)] for a, b in cut], axis=1
            ).astype(BF)

    def deliver(ab, landing):
        return [send.to(me.back[i], ab.at[i], landing.at[i]) for i in range(2)]

    split(f_ref[...], cuts[2], ab2)
    third = deliver(ab2, in2)
    crossing.wait_recv()
    over_z = settle_second(send, me, dn_ref, other, summed, landed, rows)
    for copy in gain_copies:
        copy.wait_recv()
    total = slots[0]
    for i in range(1, 8):
        total += slots[i]
    plane_sum[...] = total
    plane_slots[me.s] = total
    plane_copies = [send.to(peer, plane_sum, plane_slots.at[me.s]) for peer in (me.x, me.y, me.d)]
    delivered = []
    for plane, cut, ab, landing, held in (
        (planes[0], cuts[0], ab0, in0, swap0),
        (planes[1], cuts[1], ab1, in1, swap1),
    ):
        plane.middle()

    for plane, cut, ab, landing in ((planes[0], cuts[0], ab0, in0), (planes[1], cuts[1], ab1, in1)):

        def store(here, value):
            for i in range(2):
                ab[i, here] = jnp.concatenate(
                    [value[:, 2 * a + i * (b - a) : 2 * a + (i + 1) * (b - a)] for a, b in cut], axis=1
                ).astype(BF)

        plane.end(store)
        delivered.append(deliver(ab, landing))
    for copy in plane_copies:
        copy.wait_recv()
    gain_out[...] = plane_slots[0] + plane_slots[1] + plane_slots[2] + plane_slots[3]
    shares = []
    for copies, landing, held in ((third, in2, swap2), (delivered[0], in0, swap0), (delivered[1], in1, swap1)):
        for copy in copies:
            copy.wait_recv()
        held[0] = (landing[0].astype(F32) + landing[1].astype(F32)).astype(BF)
        shares.append(send.to(me.core, held.at[0], held.at[1]))
    dn_out[...] = settle_third(over_z, summed, landed)
    for share, held, out in zip(shares, (swap2, swap0, swap1), (o2, o0, o1)):
        share.wait_recv()
        out[...] = held[0].astype(F32) + held[1].astype(F32)
    send.finish()


def tail_scatter(dn, grads, ff, gains, cuts):
    total, depth = dn.shape
    rows = total // 8
    groups, part, width = grads[0].shape
    chunks = halves(part, 1, 16)
    vmem = pl.BlockSpec(memory_space=pltpu.VMEM)
    widths = [width // 2, width // 2, ff.shape[1] // 2]
    scratch = [
        pltpu.VMEM((4 * rows, depth), BF),
        pltpu.VMEM((4, rows, depth), BF),
        pltpu.VMEM((3, rows, depth), BF),
    ]
    for _ in grads:
        scratch += [pltpu.VMEM((2, part, width), BF), pltpu.VMEM((part, width), BF), pltpu.VMEM((part, width), BF)]
    for _ in range(3):
        scratch += [pltpu.VMEM((2, part, w), BF) for w in widths]
    scratch += [
        pltpu.VMEM((8,) + gains.shape, F32),
        pltpu.VMEM(gains.shape, F32),
        pltpu.VMEM((4,) + gains.shape, F32),
        pltpu.SemaphoreType.DMA((48,)),
        pltpu.SemaphoreType.DMA((48,)),
    ]
    return pl.pallas_call(
        partial(tail_kernel, cuts=cuts, chunks=chunks),
        in_specs=[vmem] * 5,
        out_specs=[vmem] * 5,
        out_shape=[jax.ShapeDtypeStruct((rows, depth), F32)]
        + [jax.ShapeDtypeStruct((part, w), F32) for w in widths]
        + [jax.ShapeDtypeStruct(gains.shape, F32)],
        scratch_shapes=scratch,
        compiler_params=pltpu.CompilerParams(collective_id=4, has_side_effects=True, vmem_limit_bytes=VMEM_LIMIT),
        name="tail_scatter",
    )(dn, *grads, ff, gains)


def normalize(hidden, gain):
    inverse = lax.rsqrt(jnp.mean(hidden * hidden, axis=-1, keepdims=True) + EPS)
    return (hidden * inverse * gain, inverse)


def norm_back(hidden, inverse, gain, upstream):
    scaled = upstream * gain
    inner = jnp.mean(scaled * hidden, axis=-1, keepdims=True)
    return inverse * scaled - hidden * (inverse * inverse * inverse) * inner


def matmul(left, right):
    return jnp.dot(left, right, preferred_element_type=F32)


def left_t(left, right):
    return jnp.einsum("ra,rb->ab", left, right, preferred_element_type=F32)


def right_t(left, right):
    return jnp.einsum("ra,ba->rb", left, right, preferred_element_type=F32)


def swap(array):
    return lax.ppermute(array, "ctx", [(0, 1), (1, 0)])


def per_device(
    inputs, encoder, prefix, targets, cotangent, gain_self, query_self, key_self, value_self, output_self,
    gain_cross, query_cross, key_cross, value_cross, output_cross, gain_hidden, gate_weight, up_weight,
    down_weight, gain_exit, embedding,
):
    tp = lax.axis_size("tp")
    ctx = lax.axis_size("ctx")
    shards = lax.axis_size("shard")
    assert tp == 4 and ctx == 2
    core = lax.axis_index("ctx")
    place = lax.axis_index("tp")
    rows, depth = inputs.shape
    group = rows * tp
    total = group * ctx
    hb = query_self.shape[1]
    width = 2 * hb
    fb = gate_weight.shape[1]
    pair = rows * ctx

    route_a = []
    route_b = []
    for c in range(2):
        for z in range(4):
            dest = c * 4 + z
            route_a.append(((z % 2) * 4 + 2 * c + z // 2, dest))
            route_b.append(((z % 2) * 4 + 2 * c + 1 - z // 2, dest))
    both = ("ctx", "tp")

    def spread_weights(parts):
        block = jnp.concatenate(parts, axis=1)
        first = lax.ppermute(block, both, route_a)
        second = lax.ppermute(block, both, route_b)
        columns = []
        start = 0
        for piece in parts:
            stop = start + piece.shape[1]
            columns += [first[:, start:stop], second[:, start:stop]]
            start = stop
        return lax.all_gather(jnp.concatenate(columns, axis=1), "shard", axis=0, tiled=True)

    def collect_weights(grad, widths):
        mine = lax.psum_scatter(grad, "shard", scatter_dimension=0, tiled=True)
        first = []
        second = []
        start = 0
        for size in widths:
            first.append(mine[:, start : start + size])
            second.append(mine[:, start + size : start + 2 * size])
            start += 2 * size
        back = lambda route: [(dest, source) for source, dest in route]
        one = lax.ppermute(jnp.concatenate(first, axis=1), both, back(route_a))
        two = lax.ppermute(jnp.concatenate(second, axis=1), both, back(route_b))
        part = (one.astype(F32) + two.astype(F32)).astype(BF)
        whole = part.astype(F32) + swap(part).astype(F32)
        outs = []
        start = 0
        for size in widths:
            outs.append(whole[:, start : start + size])
            start += size
        return outs

    def couple(own, other):
        return jnp.where(
            core == 0, jnp.concatenate([own, other], axis=0), jnp.concatenate([other, own], axis=0)
        )

    fast = shards == 4
    gains = lax.all_gather(jnp.stack([gain_self, gain_cross, gain_hidden, gain_exit]), "shard", axis=1, tiled=True)
    gain_one, gain_two, gain_three, gain_four = [gains[i].astype(F32) for i in range(4)]

    own_f = inputs.astype(F32)
    normed1_own, inverse1_own = normalize(own_f, gain_one)
    normed1_own = normed1_own.astype(BF)
    parts_self = [query_self, key_self, value_self, output_self.T]
    parts_cross = [query_cross, key_cross, value_cross, output_cross.T]
    parts_ff = [gate_weight, up_weight, down_weight.T]
    cuts = [[(i * w, (i + 1) * w) for i in range(n)] for n, w in ((4, hb), (4, hb), (3, fb))]
    vocab_half = embedding.shape[0] // ctx
    emb_mine = lax.dynamic_slice_in_dim(embedding, core * vocab_half, vocab_half, axis=0)
    emb_mine = jnp.concatenate([emb_mine[: vocab_half // 2], emb_mine[vocab_half // 2 :]], axis=1)
    if fast:
        bundles = [jnp.concatenate(parts, axis=1) for parts in (parts_self, parts_cross, parts_ff)]
        normed1, encoder_all, x_pair, g_pair, t_pair, weights_self, weights_cross, weights_ff = start_gather(
            normed1_own, encoder, inputs, cotangent, targets.reshape(8, group // 8), bundles, cuts
        )
        hidden0 = x_pair.astype(F32)
        cotangent_pair = g_pair.astype(F32)
        targets_all = t_pair.reshape(total)
        emb_mine, normed1 = lax.optimization_barrier((emb_mine, normed1))
        emb_pieces = lax.all_gather(emb_mine, "shard", axis=0)
    else:
        normed1 = lax.all_gather(normed1_own, both, axis=0, tiled=True)
        encoder_all = lax.all_gather(encoder, both, axis=0, tiled=True)
        weights_self, weights_cross, weights_ff = map(spread_weights, (parts_self, parts_cross, parts_ff))
        hidden0 = couple(inputs, swap(inputs)).astype(F32)
        cotangent_pair = couple(cotangent, swap(cotangent)).astype(F32)
        targets_all = couple(targets, swap(targets))
        emb_pieces = lax.all_gather(emb_mine, "shard", axis=0)
        emb_pieces = emb_pieces.reshape(shards, vocab_half // 2, 2, depth // shards)
        emb_pieces = jnp.transpose(emb_pieces, (1, 2, 0, 3)).reshape(1, vocab_half // 2, 2 * depth)

    def take_pair(array):
        cut = array.reshape(ctx, group, depth)
        return lax.dynamic_slice_in_dim(cut, place * rows, rows, axis=1).reshape(pair, depth)

    normed1_pair = take_pair(normed1)
    query_w, key_w, value_w, out_w = [weights_self[:, i * width : (i + 1) * width] for i in range(4)]
    scale = HEAD_DIM**-0.5

    def project_q(normed, weight):
        query = matmul(normed, weight).astype(BF) * jnp.asarray(scale, BF)
        return query, query.T

    positions = jnp.concatenate(
        [c * group + place * rows + jnp.arange(rows, dtype=jnp.int32) for c in range(2)]
    )
    limit = prefix[0]
    seen = jnp.maximum(positions + 1, limit)[None, :]
    chunk = 512
    last0 = jnp.maximum((place + 1) * rows, limit)
    last1 = jnp.maximum(group + (place + 1) * rows, limit)
    limits = jnp.stack([(last0 + chunk - 1) // chunk, (last1 + chunk - 1) // chunk]).astype(jnp.int32)
    causal_blocks = ((0, rows), (rows, rows))
    open_blocks = ((0, pair),)

    query1, query1_t = project_q(normed1_pair, query_w)
    key1 = matmul(normed1, key_w).astype(BF)
    value1 = matmul(normed1, value_w).astype(BF)
    attended1, attended1_t, lse1 = attend(
        limits, seen, query1_t, key1, value1.T, True, causal_blocks, chunk
    )

    def add_halves(partial_sum):
        part = partial_sum.astype(BF)
        return partial_sum + swap(part).astype(F32)

    hidden1 = hidden0 + add_halves(right_t(attended1, out_w))
    query2_w, key2_w, value2_w, out2_w = [weights_cross[:, i * width : (i + 1) * width] for i in range(4)]
    key2 = matmul(encoder_all, key2_w).astype(BF)
    value2 = matmul(encoder_all, value2_w).astype(BF)
    normed2, inverse2 = normalize(hidden1, gain_two)
    normed2 = normed2.astype(BF)
    query2, query2_t = project_q(normed2, query2_w)
    attended2, attended2_t, lse2 = attend(
        limits, seen, query2_t, key2, value2.T, False, open_blocks, chunk
    )
    hidden2 = hidden1 + add_halves(right_t(attended2, out2_w))
    normed3, inverse3 = normalize(hidden2, gain_three)
    normed3 = normed3.astype(BF)
    gate_w, up_w, down_w = [weights_ff[:, i * 2 * fb : (i + 1) * 2 * fb] for i in range(3)]
    gate = matmul(normed3, gate_w)
    upper = matmul(normed3, up_w)
    active = jax.nn.gelu(gate, approximate=True)
    product = (active * upper).astype(BF)
    final = hidden2 + add_halves(right_t(product, down_w))
    normed4, inverse4 = normalize(final, gain_four)
    normed4 = normed4.astype(BF)

    def mine(array):
        return lax.dynamic_slice_in_dim(array, core * rows, rows, axis=0)

    final_own = mine(final)
    if fast:
        normed4_all = gather_rows(mine(normed4))
    else:
        normed4_all = lax.all_gather(mine(normed4), both, axis=0, tiled=True)
    normed4_t = normed4_all.T
    local_target = (targets_all - (place * embedding.shape[0] + core * vocab_half))[None, :].astype(jnp.int32)
    vblock, rblock = 512, 512
    stats, emb = head_stats(emb_pieces, normed4_t, local_target, vblock, rblock)
    if fast:
        combined = combine_stats(stats)
        logsum = combined[0]
        loss = combined[1]
    else:
        every = lax.all_gather(stats[:3], both, axis=0)
        top = jnp.max(every[:, 0], axis=0)
        summed = jnp.sum(every[:, 1] * jnp.exp(every[:, 0] - top[None]), axis=0)
        logsum = top + jnp.log(summed)
        loss = logsum - jnp.sum(every[:, 2], axis=0)
    exit_loss = lax.dynamic_slice_in_dim(loss, core * group, group, axis=0)
    groups = emb_pieces.shape[0]
    emb_grad, grad_normed4 = head_back(
        emb, normed4_t, normed4_all, local_target, logsum[None, :], groups, vocab_half, vblock, rblock
    )
    if fast:
        gn4, emb_sum = middle_scatter(grad_normed4, emb_grad)
        gn4 = gn4.astype(F32)
    else:
        emb_grad = emb_grad.reshape(vocab_half // 2, 2, shards, depth // shards)
        emb_grad = jnp.transpose(emb_grad, (2, 0, 1, 3)).reshape(shards * vocab_half // 2, 2 * depth // shards)
        emb_sum = lax.psum_scatter(emb_grad, "shard", scatter_dimension=0, tiled=True)
        emb_sum = couple(emb_sum, swap(emb_sum))
        gn4_own = lax.psum_scatter(grad_normed4, both, scatter_dimension=0, tiled=True)
        gn4 = couple(gn4_own, swap(gn4_own)).astype(F32)
    emb_sum = emb_sum.reshape(2, vocab_half // 2, 2, depth // shards)
    embedding_grad = jnp.transpose(emb_sum, (0, 2, 1, 3)).reshape(embedding.shape).astype(F32)
    gain4_rows = gn4 * final * inverse4
    grad_final = cotangent_pair + norm_back(final, inverse4, gain_four, gn4)
    grad_final_b = grad_final.astype(BF)
    down_grad = left_t(grad_final_b, product).astype(BF)
    grad_product = matmul(grad_final_b, down_w)
    unused, gelu_pull = jax.vjp(partial(jax.nn.gelu, approximate=True), gate)
    grad_gate = gelu_pull(grad_product * upper)[0].astype(BF)
    grad_upper = (grad_product * active).astype(BF)
    gate_grad = left_t(normed3, grad_gate).astype(BF)
    upper_grad = left_t(normed3, grad_upper).astype(BF)
    ff_part = jnp.concatenate([gate_grad, upper_grad, down_grad], axis=1)
    if fast:
        ff_mine = lax.psum_scatter(ff_part, "shard", scatter_dimension=0, tiled=True)
    gn3 = add_halves(right_t(grad_gate, gate_w) + right_t(grad_upper, up_w))
    gain3_rows = gn3 * hidden2 * inverse3
    grad_hidden2 = grad_final + norm_back(hidden2, inverse3, gain_three, gn3)
    grad_hidden2_b = grad_hidden2.astype(BF)
    out2_grad = left_t(grad_hidden2_b, attended2).astype(BF)
    grad_attended2 = matmul(grad_hidden2_b, out2_w).astype(BF)
    grad_query2, grad_key2, grad_value2 = attend_back(
        limits, seen, query2_t, query2, key2, key2.T, value2, grad_attended2, grad_attended2.T,
        attended2_t, lse2, False, open_blocks, chunk,
    )
    query2_grad = left_t(normed2, grad_query2).astype(BF)
    key2_grad = left_t(encoder_all, grad_key2).astype(BF)
    value2_grad = left_t(encoder_all, grad_value2).astype(BF)
    cross_part = jnp.concatenate([query2_grad, key2_grad, value2_grad, out2_grad], axis=1)
    encoder_part = (right_t(grad_key2, key2_w) + right_t(grad_value2, value2_w)).astype(BF)
    encoder_grad = lax.psum_scatter(encoder_part, both, scatter_dimension=0, tiled=True).astype(F32)
    gn2 = add_halves(right_t(grad_query2, query2_w))
    gain2_rows = gn2 * hidden1 * inverse2
    grad_hidden1 = grad_hidden2 + norm_back(hidden1, inverse2, gain_two, gn2)
    grad_hidden1_b = grad_hidden1.astype(BF)
    out_grad = left_t(grad_hidden1_b, attended1).astype(BF)
    grad_attended1 = matmul(grad_hidden1_b, out_w).astype(BF)
    grad_query1, grad_key1, grad_value1 = attend_back(
        limits, seen, query1_t, query1, key1, key1.T, value1, grad_attended1, grad_attended1.T,
        attended1_t, lse1, True, causal_blocks, chunk,
    )
    query_grad = left_t(normed1_pair, grad_query1).astype(BF)
    key_grad = left_t(normed1, grad_key1).astype(BF)
    value_grad = left_t(normed1, grad_value1).astype(BF)
    self_part = jnp.concatenate([query_grad, key_grad, value_grad, out_grad], axis=1)
    normed1_part = right_t(grad_key1, key_w) + right_t(grad_value1, value_w)
    query_part = right_t(grad_query1, query_w).reshape(ctx, rows, depth)
    cut = normed1_part.reshape(ctx, group, depth)
    old = lax.dynamic_slice_in_dim(cut, place * rows, rows, axis=1)
    cut = lax.dynamic_update_slice_in_dim(cut, old + query_part, place * rows, axis=1)
    cut = cut.reshape(total, depth).astype(BF)

    def gain_rows(gn1):
        gain1_sum = jnp.sum(gn1 * own_f * inverse1_own, axis=0)
        return jnp.stack(
            [gain1_sum] + [jnp.sum(mine(a), axis=0) for a in (gain2_rows, gain3_rows, gain4_rows)]
        )

    if fast:
        blocks = [a.reshape(shards, depth // shards, a.shape[1]) for a in (cross_part, self_part)]
        gain1_part = jnp.sum(cut.astype(F32) * normed1.astype(F32), axis=0) / gain_one
        gains_part = [gain1_part] + [jnp.sum(mine(a), axis=0) for a in (gain2_rows, gain3_rows, gain4_rows)]
        gn1, cross_own, self_own, ff_own, gain_sums = tail_scatter(
            cut, blocks, ff_mine, jnp.stack(gains_part + [jnp.zeros_like(gain1_part)] * 4), [cuts[1], cuts[0], cuts[2]]
        )
        take = lambda own, index: [own[:, a:b] for a, b in cuts[index]]
        self_grads, cross_grads, ff_grads = take(self_own, 0), take(cross_own, 1), take(ff_own, 2)
    else:
        gn1 = lax.psum_scatter(cut, both, scatter_dimension=0, tiled=True).astype(F32)
        ff_grads = collect_weights(ff_part, [fb, fb, fb])
        cross_grads = collect_weights(cross_part, [hb] * 4)
        self_grads = collect_weights(self_part, [hb] * 4)
        gain_sums = lax.psum(gain_rows(gn1), ("shard", "ctx", "tp"))
    inputs_grad = mine(grad_hidden1) + norm_back(own_f, inverse1_own, gain_one, gn1)
    part = depth // shards
    gain_grads = lax.dynamic_slice_in_dim(gain_sums, lax.axis_index("shard") * part, part, axis=1)
    return (
        final_own.astype(BF), exit_loss, inputs_grad, encoder_grad,
        gain_grads[0], self_grads[0], self_grads[1], self_grads[2], self_grads[3].T,
        gain_grads[1], cross_grads[0], cross_grads[1], cross_grads[2], cross_grads[3].T,
        gain_grads[2], ff_grads[0], ff_grads[1], ff_grads[2].T,
        gain_grads[3], embedding_grad,
    )


def solution(mesh):
    rows = P(("shard", "ctx", "tp"), None)
    into = P("shard", "tp")
    out = P("tp", "shard")
    gain = P("shard")
    weights = (gain, into, into, into, out, gain, into, into, into, out, gain, into, into, out, gain, out)
    return jax.shard_map(
        per_device,
        mesh=mesh,
        in_specs=(rows, rows, P("shard"), P(("shard", "ctx")), rows) + weights,
        out_specs=(rows, P(("shard", "ctx")), rows, rows) + weights,
        check_vma=False,
    )
```

```python
from functools import partial

import jax
import jax.numpy as jnp
from jax import lax
from jax.experimental import pallas as pl
from jax.experimental.pallas import tpu as pltpu
from jax.sharding import PartitionSpec as P

HEAD_DIM = 64
EPS = 1e-06
MASKED = -1e30
BF = jnp.bfloat16
F32 = jnp.float32
VMEM_LIMIT = 58 * 2**20


def attend_kernel(limit_ref, seen_ref, q_ref, k_ref, v_ref, o_ref, ot_ref, lse_ref, vt_ref, *, masked, blocks, chunk):
    half = lax.broadcasted_iota(jnp.int32, (2 * HEAD_DIM, 1), 0) // HEAD_DIM
    vt_ref[...] = jnp.transpose(v_ref[...])
    q_t = jnp.transpose(q_ref[...])
    for head in range(2):
        part = slice(head * HEAD_DIM, (head + 1) * HEAD_DIM)
        for index, (first, count) in enumerate(blocks):
            columns = slice(first, first + count)
            qt = jnp.where(half == head, q_t[:, columns], 0).astype(BF)

            def step(i, carry):
                top, total, acc = carry
                start = pl.multiple_of(i * chunk, chunk)
                scores = jnp.dot(k_ref[pl.ds(start, chunk), :], qt, preferred_element_type=F32)
                if masked:
                    key = lax.broadcasted_iota(jnp.int32, (chunk, 1), 0) + start
                    scores = jnp.where(key < seen_ref[:, columns], scores, MASKED)
                new_top = jnp.maximum(top, jnp.max(scores, axis=0, keepdims=True))
                expo = jnp.exp(scores - new_top)
                shrink = jnp.exp(top - new_top)
                total = total * shrink + jnp.sum(expo, axis=0, keepdims=True)
                acc = acc * shrink + jnp.dot(
                    vt_ref[part, pl.ds(start, chunk)], expo.astype(BF), preferred_element_type=F32
                )
                return (new_top, total, acc)

            init = (
                jnp.full((1, count), MASKED, F32),
                jnp.zeros((1, count), F32),
                jnp.zeros((HEAD_DIM, count), F32),
            )
            if masked:
                top, total, acc = lax.fori_loop(0, limit_ref[index], step, init)
            else:
                top, total, acc = lax.fori_loop(0, k_ref.shape[0] // chunk, step, init, unroll=True)
            ot_ref[part, columns] = acc / total
            lse_ref[0, head : head + 1, columns] = top + jnp.log(total)
    o_ref[...] = jnp.transpose(ot_ref[...]).astype(BF)


def attend(limit, seen, query, kv, masked, blocks, chunk):
    rows, width = query.shape
    count = kv.shape[0]
    pair = 2 * HEAD_DIM
    pairs = width // pair
    return pl.pallas_call(
        partial(attend_kernel, masked=masked, blocks=blocks, chunk=chunk),
        grid_spec=pltpu.PrefetchScalarGridSpec(
            num_scalar_prefetch=1,
            grid=(pairs,),
            in_specs=[
                pl.BlockSpec((1, rows), lambda p, lim: (0, 0)),
                pl.BlockSpec((rows, pair), lambda p, lim: (0, p)),
                pl.BlockSpec((count, pair), lambda p, lim: (0, p)),
                pl.BlockSpec((count, pair), lambda p, lim: (0, p + pairs)),
            ],
            out_specs=[
                pl.BlockSpec((rows, pair), lambda p, lim: (0, p)),
                pl.BlockSpec((pair, rows), lambda p, lim: (p, 0)),
                pl.BlockSpec((1, 8, rows), lambda p, lim: (p, 0, 0)),
            ],
            scratch_shapes=[pltpu.VMEM((pair, count), BF)],
        ),
        out_shape=(
            jax.ShapeDtypeStruct((rows, width), BF),
            jax.ShapeDtypeStruct((width, rows), F32),
            jax.ShapeDtypeStruct((pairs, 8, rows), F32),
        ),
        compiler_params=pltpu.CompilerParams(vmem_limit_bytes=VMEM_LIMIT),
        cost_estimate=pl.CostEstimate(
            flops=4 * rows * count * width, transcendentals=rows * count * width // HEAD_DIM,
            bytes_accessed=2 * count * width * 2 + 8 * rows * width,
        ),
        name="attend",
    )(limit, seen, query, kv, kv)


def attend_back_kernel(
    limit_ref, seen_ref, q_ref, k_ref, v_ref, do_ref, ot_ref, lse_ref,
    dq_ref, dk_ref, dv_ref, dk_acc, dv_acc, dqt_acc, kt_ref, *, masked, blocks, chunk,
):
    half = lax.broadcasted_iota(jnp.int32, (2 * HEAD_DIM, 1), 0) // HEAD_DIM
    lane = lax.broadcasted_iota(jnp.int32, (1, 2 * HEAD_DIM), 1) // HEAD_DIM
    kt_ref[...] = jnp.transpose(k_ref[...])
    q_t = jnp.transpose(q_ref[...])
    do_t = jnp.transpose(do_ref[...])
    dk_acc[...] = jnp.zeros_like(dk_acc)
    dv_acc[...] = jnp.zeros_like(dv_acc)
    for head in range(2):
        part = slice(head * HEAD_DIM, (head + 1) * HEAD_DIM)
        for index, (first, count) in enumerate(blocks):
            columns = slice(first, first + count)
            qt = jnp.where(half == head, q_t[:, columns], 0).astype(BF)
            dot_t = jnp.where(half == head, do_t[:, columns], 0).astype(BF)
            q = jnp.where(lane == head, q_ref[columns, :], 0).astype(BF)
            do = jnp.where(lane == head, do_ref[columns, :], 0).astype(BF)
            inner = jnp.sum(
                do_t[part, columns].astype(F32) * ot_ref[part, columns], axis=0, keepdims=True
            )
            lse = lse_ref[0, head : head + 1, columns]

            def step(i, acc):
                start = pl.multiple_of(i * chunk, chunk)
                here = pl.ds(start, chunk)
                scores = jnp.dot(k_ref[here, :], qt, preferred_element_type=F32)
                probs = jnp.exp(scores - lse)
                if masked:
                    key = lax.broadcasted_iota(jnp.int32, (chunk, 1), 0) + start
                    probs = jnp.where(key < seen_ref[:, columns], probs, 0.0)
                grad_probs = jnp.dot(v_ref[here, :], dot_t, preferred_element_type=F32)
                grad_scores = (probs * (grad_probs - inner)).astype(BF)
                dv_acc[here, :] += jnp.dot(probs.astype(BF), do, preferred_element_type=F32)
                dk_acc[here, :] += jnp.dot(grad_scores, q, preferred_element_type=F32)
                return acc + jnp.dot(kt_ref[part, here], grad_scores, preferred_element_type=F32)

            init = jnp.zeros((HEAD_DIM, count), F32)
            if masked:
                acc = lax.fori_loop(0, limit_ref[index], step, init)
            else:
                acc = lax.fori_loop(0, k_ref.shape[0] // chunk, step, init, unroll=True)
            dqt_acc[part, columns] = acc * HEAD_DIM**-0.5
    dq_ref[...] = jnp.transpose(dqt_acc[...]).astype(BF)
    dk_ref[...] = dk_acc[...].astype(BF)
    dv_ref[...] = dv_acc[...].astype(BF)


def attend_back(limit, seen, query, kv, grad, out_t, lse, masked, blocks, chunk):
    rows, width = query.shape
    count = kv.shape[0]
    pair = 2 * HEAD_DIM
    pairs = width // pair
    by_column = pl.BlockSpec((rows, pair), lambda p, lim: (0, p))
    key_spec = pl.BlockSpec((count, pair), lambda p, lim: (0, p))
    return pl.pallas_call(
        partial(attend_back_kernel, masked=masked, blocks=blocks, chunk=chunk),
        grid_spec=pltpu.PrefetchScalarGridSpec(
            num_scalar_prefetch=1,
            grid=(pairs,),
            in_specs=[
                pl.BlockSpec((1, rows), lambda p, lim: (0, 0)),
                by_column,
                key_spec,
                pl.BlockSpec((count, pair), lambda p, lim: (0, p + pairs)),
                by_column,
                pl.BlockSpec((pair, rows), lambda p, lim: (p, 0)),
                pl.BlockSpec((1, 8, rows), lambda p, lim: (p, 0, 0)),
            ],
            out_specs=[by_column, key_spec, key_spec],
            scratch_shapes=[
                pltpu.VMEM((count, pair), F32),
                pltpu.VMEM((count, pair), F32),
                pltpu.VMEM((pair, rows), F32),
                pltpu.VMEM((pair, count), BF),
            ],
        ),
        out_shape=(
            jax.ShapeDtypeStruct((rows, width), BF),
            jax.ShapeDtypeStruct((count, width), BF),
            jax.ShapeDtypeStruct((count, width), BF),
        ),
        compiler_params=pltpu.CompilerParams(vmem_limit_bytes=VMEM_LIMIT),
        cost_estimate=pl.CostEstimate(
            flops=10 * rows * count * width, transcendentals=rows * count * width // HEAD_DIM,
            bytes_accessed=5 * count * width * 2 + 14 * rows * width,
        ),
        name="attend_back",
    )(limit, seen, query, kv, kv, grad, out_t, lse)


def vocab_ids(step, block, vocab):
    row = lax.broadcasted_iota(jnp.int32, (block, 1), 0)
    second = (row >= block // 2).astype(jnp.int32)
    local = row - second * (block // 2) + step * (block // 2)
    valid = local < vocab // 2
    return jnp.where(valid, local + second * (vocab // 2), 2**30), valid


def head_stats_kernel(
    pieces_ref, n_ref, target_ref, stats_ref, emb_ref, expo_ref, tops_ref, nt_ref, run_ref, *, vocab, block, rows, scale
):
    step = pl.program_id(0)
    ids, valid = vocab_ids(step, block, vocab)
    width = pieces_ref.shape[2] // 2
    emb = jnp.concatenate(
        [
            jnp.concatenate(
                [pieces_ref[g, :, p * width : (p + 1) * width] for g in range(pieces_ref.shape[0])], axis=1
            )
            for p in range(2)
        ],
        axis=0,
    )
    emb = jnp.where(valid, emb, 0).astype(BF)
    emb_ref[...] = emb
    total = n_ref.shape[0]

    @pl.when(step == 0)
    def _():
        run_ref[0:1, :] = jnp.full((1, total), MASKED, F32)
        run_ref[1:8, :] = jnp.zeros((7, total), F32)
        for first in range(0, total, rows):
            nt_ref[:, first : first + rows] = jnp.transpose(n_ref[first : first + rows, :])

    for first in range(0, total, rows):
        columns = slice(first, first + rows)
        logits = jnp.dot(emb, nt_ref[:, columns], preferred_element_type=F32) * scale
        logits = jnp.where(valid, logits, MASKED)
        top = run_ref[0:1, columns]
        new_top = jnp.maximum(top, jnp.max(logits, axis=0, keepdims=True))
        expo = jnp.exp(logits - new_top)
        expo_ref[:, columns] = expo.astype(BF)
        run_ref[0:1, columns] = new_top
        run_ref[1:2, columns] = run_ref[1:2, columns] * jnp.exp(top - new_top) + jnp.sum(expo, axis=0, keepdims=True)
        run_ref[2:3, columns] += jnp.sum(jnp.where(ids == target_ref[:, columns], logits, 0.0), axis=0, keepdims=True)
    tops_ref[pl.ds(step, 1), :] = run_ref[0:1, :]

    @pl.when(step == pl.num_programs(0) - 1)
    def _():
        lines = total // 128
        for k in range(3):
            for i in range(lines):
                stats_ref[k * lines + i : k * lines + i + 1, :] = run_ref[k : k + 1, i * 128 : (i + 1) * 128]


def head_stats(pieces, normed, target, block, rows):
    groups, vocab, width = pieces.shape
    vocab *= 2
    total, depth = normed.shape
    steps = pl.cdiv(vocab, block)
    lines = (steps + 7) // 8 * 8
    return pl.pallas_call(
        partial(head_stats_kernel, vocab=vocab, block=block, rows=rows, scale=depth**-0.5),
        grid=(steps,),
        in_specs=[
            pl.BlockSpec((groups, block // 2, width), lambda i: (0, i, 0)),
            pl.BlockSpec((total, depth), lambda i: (0, 0)),
            pl.BlockSpec((1, total), lambda i: (0, 0)),
        ],
        out_specs=[
            pl.BlockSpec((3 * total // 128, 128), lambda i: (0, 0)),
            pl.BlockSpec((block, depth), lambda i: (i, 0)),
            pl.BlockSpec((block, total), lambda i: (i, 0)),
            pl.BlockSpec((lines, total), lambda i: (0, 0)),
        ],
        out_shape=(
            jax.ShapeDtypeStruct((3 * total // 128, 128), F32),
            jax.ShapeDtypeStruct((steps * block, depth), BF),
            jax.ShapeDtypeStruct((steps * block, total), BF),
            jax.ShapeDtypeStruct((lines, total), F32),
        ),
        scratch_shapes=[pltpu.VMEM((depth, total), BF), pltpu.VMEM((8, total), F32)],
        compiler_params=pltpu.CompilerParams(vmem_limit_bytes=VMEM_LIMIT),
        cost_estimate=pl.CostEstimate(
            flops=2 * vocab * depth * total, transcendentals=vocab * total,
            bytes_accessed=4 * vocab * depth + 2 * depth * total + 2 * vocab * total,
        ),
        name="head_stats",
    )(pieces, normed, target)


def head_back_kernel(
    emb_ref, expo_ref, tops_ref, n_ref, target_ref, lse_ref, de_ref, dn_ref, dnt_acc, *, vocab, block, rows, scale
):
    step = pl.program_id(0)
    ids, valid = vocab_ids(step, block, vocab)
    emb_t = jnp.transpose(emb_ref[...])
    factor = jnp.exp(tops_ref[pl.ds(step, 1), :] - lse_ref[...])

    @pl.when(step == 0)
    def _():
        dnt_acc[...] = jnp.zeros_like(dnt_acc)

    de = None
    for first in range(0, n_ref.shape[0], rows):
        columns = slice(first, first + rows)
        probs = expo_ref[:, columns].astype(F32) * factor[:, columns]
        grad = jnp.where(ids == target_ref[:, columns], probs - 1.0, probs).astype(BF)
        term = jnp.dot(grad, n_ref[columns, :], preferred_element_type=F32)
        de = term if de is None else de + term
        dnt_acc[:, columns] += jnp.dot(emb_t, grad, preferred_element_type=F32)
    de = (de * scale).astype(BF)
    width = de_ref.shape[2] // 2
    for g in range(de_ref.shape[0]):
        part = de[:, g * width : (g + 1) * width]
        de_ref[g] = jnp.concatenate([part[: block // 2], part[block // 2 :]], axis=1)

    @pl.when(step == pl.num_programs(0) - 1)
    def _():
        dn_ref[...] = (jnp.transpose(dnt_acc[...]) * scale).astype(BF)


def head_back(emb, expo, tops, normed, target, lse, groups, vocab, block, rows):
    total, depth = normed.shape
    steps = pl.cdiv(vocab, block)
    width = depth // groups
    return pl.pallas_call(
        partial(head_back_kernel, vocab=vocab, block=block, rows=rows, scale=depth**-0.5),
        grid=(steps,),
        in_specs=[
            pl.BlockSpec((block, depth), lambda i: (i, 0)),
            pl.BlockSpec((block, total), lambda i: (i, 0)),
            pl.BlockSpec(tops.shape, lambda i: (0, 0)),
            pl.BlockSpec((total, depth), lambda i: (0, 0)),
            pl.BlockSpec((1, total), lambda i: (0, 0)),
            pl.BlockSpec((1, total), lambda i: (0, 0)),
        ],
        out_specs=[
            pl.BlockSpec((groups, block // 2, 2 * width), lambda i: (0, i, 0)),
            pl.BlockSpec((total, depth), lambda i: (0, 0)),
        ],
        out_shape=(
            jax.ShapeDtypeStruct((groups, steps * block // 2, 2 * width), BF),
            jax.ShapeDtypeStruct((total, depth), BF),
        ),
        scratch_shapes=[pltpu.VMEM((depth, total), F32)],
        compiler_params=pltpu.CompilerParams(vmem_limit_bytes=VMEM_LIMIT),
        cost_estimate=pl.CostEstimate(
            flops=4 * vocab * depth * total, transcendentals=0,
            bytes_accessed=4 * vocab * depth + 6 * depth * total + 2 * vocab * total,
        ),
        name="head_back",
    )(emb, expo, tops, normed, target, lse)


MESH = pl.DeviceIdType.MESH


class Peers:
    def __init__(self):
        self.s, self.c, self.t = (lax.axis_index(name) for name in ("shard", "ctx", "tp"))
        s, c, t = self.s, self.c, self.t
        self.sx = s + 1 - 2 * lax.rem(s, 2)
        self.sy = lax.rem(s + 2, 4)
        self.sd = lax.rem(self.sx + 2, 4)
        self.x = (self.sx, c, t)
        self.y = (self.sy, c, t)
        self.d = (self.sd, c, t)
        self.core = (s, 1 - c, t)
        self.z = [(s, c, lax.rem(t + k, 4)) for k in range(4)]
        self.z_other = [(s, 1 - c, lax.rem(t + k, 4)) for k in range(4)]
        self.group = self.z[1:] + self.z_other


def meet(peers):
    barrier = pltpu.get_barrier_semaphore()
    for peer in peers:
        pl.semaphore_signal(barrier, inc=1, device_id=peer, device_id_type=MESH)
    pl.semaphore_wait(barrier, len(peers))


class Pool:
    def __init__(self, sends, arrivals):
        self.sends, self.arrivals, self.count = sends, arrivals, 0

    def take(self, count):
        first = self.count
        self.count += count
        return first

    def copy(self, index, peer, source, target):
        return pltpu.make_async_remote_copy(
            src_ref=source, dst_ref=target, send_sem=self.sends.at[index],
            recv_sem=self.arrivals.at[index], device_id=peer, device_id_type=MESH,
        )


class Sender:
    def __init__(self, pool):
        self.pool, self.all = pool, []

    def to(self, peer, source, target):
        copy = self.pool.copy(self.pool.take(1), peer, source, target)
        self.all.append(copy)
        copy.start()
        return copy

    def finish(self):
        for copy in self.all:
            copy.wait_send()


class RowLine:
    def __init__(self, pool, me, own, everyone, rows, pieces=2):
        self.pool, self.me, self.own, self.everyone = pool, me, own, everyone
        self.rows, self.pieces, self.sub = rows, pieces, rows // pieces
        self.first = pool.take(13 * pieces)

    def block(self, chip, piece):
        return self.everyone.at[pl.ds((self.me.c * 4 + chip) * self.rows + piece * self.sub, self.sub)]

    def source(self, own, chip, piece):
        return self.own.at[pl.ds(piece * self.sub, self.sub)] if own else self.block(chip, piece)

    def make(self, slot, piece, peer, chip, own=False):
        index = self.first + slot * self.pieces + piece
        return self.pool.copy(index, peer, self.source(own, chip, piece), self.block(chip, piece))

    def right(self, k, piece):
        return self.make(k, piece, self.me.z[1], self.me.t - k, k == 0)

    def left(self, k, piece):
        return self.make(3 + k, piece, self.me.z[3], self.me.t + k, k == 0)

    def across(self, slot, piece, chip, own=False):
        return self.make(6 + slot, piece, self.me.core, chip, own)

    def begin(self):
        t = self.me.t
        for p in range(self.pieces):
            pl.when(t < 3)(lambda: self.right(0, p).start())
            pl.when(t > 0)(lambda: self.left(0, p).start())
        for p in range(self.pieces):
            self.across(0, p, t, True).start()

    def step(self, k):
        t = self.me.t
        for p in range(self.pieces):

            @pl.when(t > k)
            def _():
                chip = t - 1 - k
                self.make(k, p, self.me.z[1], chip).wait_recv()
                if k < 2:
                    pl.when(t < 3)(lambda: self.right(k + 1, p).start())
                self.across(1 + k, p, chip).start()

            @pl.when(t + k < 3)
            def _():
                chip = t + 1 + k
                self.make(3 + k, p, self.me.z[3], chip).wait_recv()
                if k < 2:
                    pl.when(t > 0)(lambda: self.left(k + 1, p).start())
                self.across(4 + k, p, chip).start()

    def finish(self):
        t = self.me.t
        for p in range(self.pieces):
            pl.when(t < 3)(lambda: self.right(0, p).wait_send())
            pl.when(t > 0)(lambda: self.left(0, p).wait_send())
            self.across(0, p, t, True).wait()
            for k in range(3):

                @pl.when(t > k)
                def _():
                    if k < 2:
                        pl.when(t < 3)(lambda: self.right(k + 1, p).wait_send())
                    self.across(1 + k, p, t - 1 - k).wait()

                @pl.when(t + k < 3)
                def _():
                    if k < 2:
                        pl.when(t > 0)(lambda: self.left(k + 1, p).wait_send())
                    self.across(4 + k, p, t + 1 + k).wait()


class BlockLine:
    def __init__(self, pool, me, own, take):
        self.pool, self.me, self.own, self.take = pool, me, own, take
        self.first = pool.take(4)
        self.where = [(me.c + 1, 1 - me.c), (3 * me.c, me.c)]

    def right(self, i):
        here = self.take.at[self.where[i][1]]
        return self.pool.copy(self.first + i, self.me.z[1], here, here)

    def left(self, i):
        here = self.take.at[self.where[i][1]]
        return self.pool.copy(self.first + 2 + i, self.me.z[3], here, here)

    def begin(self):
        t = self.me.t
        for i, (block, slot) in enumerate(self.where):

            @pl.when(t == block)
            def _():
                self.take[slot] = self.own[...]
                pl.when(t < 3)(lambda: self.right(i).start())
                pl.when(t > 0)(lambda: self.left(i).start())

    def arrive(self, distance):
        t = self.me.t
        for i, (block, slot) in enumerate(self.where):

            @pl.when(t - block == distance)
            def _():
                self.right(i).wait_recv()
                pl.when(t < 3)(lambda: self.right(i).start())

            @pl.when(block - t == distance)
            def _():
                self.left(i).wait_recv()
                pl.when(t > 0)(lambda: self.left(i).start())

    def finish(self):
        t = self.me.t
        for i, (block, slot) in enumerate(self.where):
            pl.when((t >= block) & (t < 3))(lambda: self.right(i).wait_send())
            pl.when((t <= block) & (t > 0))(lambda: self.left(i).wait_send())


class SumLine:
    def __init__(self, pool, me, own, coming, going, pieces=2):
        self.pool, self.me, self.own, self.coming, self.going = pool, me, own, coming, going
        self.pieces, self.sub = pieces, own.shape[1] // pieces
        self.first = pool.take(6 * pieces)

    def copy(self, slot, piece, source):
        here = pl.ds(piece * self.sub, self.sub)
        peer = self.me.z[1] if slot < 3 else self.me.z[3]
        return self.pool.copy(
            self.first + slot * self.pieces + piece, peer, source.at[here], self.coming.at[slot, here]
        )

    def dest(self, slot):
        return 3 - slot if slot < 3 else slot - 3

    def direct(self, slot):
        return self.me.t == (0 if slot < 3 else 3)

    def start(self):
        for slot in (0, 3, 1, 4, 2, 5):

            @pl.when(self.direct(slot))
            def _():
                for p in range(self.pieces):
                    self.copy(slot, p, self.own.at[self.dest(slot)]).start()

    passing = ((0, 1), (3, 2), (1, 1), (4, 2), (0, 2), (3, 1))

    def add(self, part):
        for slot, chip in self.passing[2 * part : 2 * part + 2]:

            @pl.when(self.me.t == chip)
            def _():
                for p in range(self.pieces):
                    here = pl.ds(p * self.sub, self.sub)
                    self.copy(slot, p, self.going.at[slot]).wait_recv()
                    self.going[slot, here] = (
                        self.own[self.dest(slot), here].astype(F32) + self.coming[slot, here].astype(F32)
                    ).astype(BF)
                    self.copy(slot, p, self.going.at[slot]).start()

    def result(self, out):
        t = self.me.t
        for slot in range(6):

            @pl.when(t == self.dest(slot))
            def _():
                for p in range(self.pieces):
                    self.copy(slot, p, self.going.at[slot]).wait_recv()

        out[...] = self.own[t].astype(F32)

        @pl.when(t > 0)
        def _():
            out[...] += self.coming[3 - t].astype(F32)

        @pl.when(t < 3)
        def _():
            out[...] += self.coming[3 + t].astype(F32)

    def finish(self):
        for slot in range(6):

            @pl.when(self.direct(slot))
            def _():
                for p in range(self.pieces):
                    self.copy(slot, p, self.own.at[self.dest(slot)]).wait_send()

        for slot, chip in self.passing:

            @pl.when(self.me.t == chip)
            def _():
                for p in range(self.pieces):
                    self.copy(slot, p, self.going.at[slot]).wait_send()


class GradLine:
    def __init__(self, pool, me, own, coming, going, shared):
        self.pool, self.me, self.own, self.coming, self.going, self.shared = pool, me, own, coming, going, shared
        self.first = pool.take(5)
        self.home = me.c == me.t // 2

    def copy(self, slot, source):
        peer = self.me.z[1] if slot < 2 else self.me.z[3]
        return self.pool.copy(self.first + slot, peer, source, self.coming.at[slot])

    def index(self, slot):
        return (1, 0, 0, 1)[slot]

    def block(self, slot):
        return 2 * self.me.c + self.index(slot)

    def direct(self, slot):
        t = self.me.t
        return (t == 0) & (self.block(slot) > 0) if slot < 2 else (t == 3) & (self.block(slot) < 3)

    def start(self):
        for slot in (0, 2, 1, 3):
            pl.when(self.direct(slot))(lambda: self.copy(slot, self.own.at[self.index(slot)]).start())

    passing = ((0, 1), (2, 2), (1, 1), (3, 2), (0, 2), (2, 1))

    def adds(self, slot, chip):
        return (self.me.t == chip) & ((chip < self.block(slot)) if slot < 2 else (chip > self.block(slot)))

    def add(self, part):
        for slot, chip in self.passing[2 * part : 2 * part + 2]:

            @pl.when(self.adds(slot, chip))
            def _():
                self.copy(slot, self.going.at[slot]).wait_recv()
                self.going[slot] = (
                    self.own[self.index(slot)].astype(F32) + self.coming[slot].astype(F32)
                ).astype(BF)
                self.copy(slot, self.going.at[slot]).start()

    def share(self):
        return self.pool.copy(self.first + 4, self.me.core, self.shared, self.shared)

    def settle(self, total):
        t = self.me.t

        for slot in range(4):
            ends = (t == self.block(slot)) & (t > 0 if slot < 2 else t < 3)
            pl.when(ends)(lambda: self.copy(slot, self.going.at[slot]).wait_recv())

        @pl.when(self.home)
        def _():
            j = lax.rem(t, 2)
            total[...] = self.own[j].astype(F32)

            @pl.when(t > 0)
            def _():
                total[...] += self.coming[1 - j].astype(F32)

            @pl.when(t < 3)
            def _():
                total[...] += self.coming[2 + j].astype(F32)

            self.shared[...] = total[...].astype(BF)
            self.share().start()

    def finish(self, out):
        for slot in range(4):
            pl.when(self.direct(slot))(lambda: self.copy(slot, self.own.at[self.index(slot)]).wait_send())
        for slot, chip in self.passing:
            pl.when(self.adds(slot, chip))(lambda: self.copy(slot, self.going.at[slot]).wait_send())
        pl.when(self.home)(lambda: self.share().wait_send())
        pl.when(jnp.logical_not(self.home))(lambda: self.share().wait_recv())
        out[...] = self.shared[...].astype(F32)


def start_kernel(
    gains_ref, x_ref, e_ref, g_ref, t_ref, emb_ref, b0, b1, b2,
    gains_out, n_all, e_all, n_pair, x_pair, g_pair, t_pair, emb_all, w0, w1, mix2,
    gain_slots, n_ref, take0, take1, take2, mix0, mix1, sends, arrivals, local, *, cuts,
):
    me = Peers()
    meet([me.z[1], me.z[3], me.core, me.x, me.y, me.d])
    pool = Pool(sends, arrivals)
    send = Sender(pool)
    rows = x_ref.shape[0]
    locals_ = []

    def copy_here(source, target):
        copy = pltpu.make_async_copy(source, target, local.at[len(locals_)])
        copy.start()
        locals_.append(copy)

    emb_rows = emb_ref.shape[0]
    emb_half = emb_rows // 16 * 8
    copy_here(emb_ref, emb_all.at[me.s])
    emb_x = send.to(me.x, emb_ref, emb_all.at[me.s])
    emb_y = send.to(me.y, emb_ref, emb_all.at[me.s])
    gain_slots[me.s] = gains_ref[...]
    gain_copies = [send.to(peer, gains_ref, gain_slots.at[me.s]) for peer in (me.x, me.y, me.d)]
    bundles = [(b0, take0, mix0), (b1, take1, mix1), (b2, take2, mix2)]
    lines = [BlockLine(pool, me, block, take) for block, take, mix in bundles]

    def interleave(i):
        block, take, mix = bundles[i]
        first = take[0]
        second = take[1]
        columns = []
        for start, stop in cuts[i]:
            columns += [first[:, start:stop], second[:, start:stop]]
        mix[...] = jnp.concatenate(columns, axis=1)

    depth = b0.shape[0]
    half = depth // 2
    mine = pl.ds(me.s * depth, depth)

    def share(i, w):
        mix = bundles[i][2]
        copy_here(mix, w.at[mine])
        return send.to(me.x, mix, w.at[mine]), send.to(me.y, mix, w.at[mine])

    onward = []

    def pass_on(to_x, to_y, x_part, y_part):
        to_x.wait_recv()
        onward.append(send.to(me.y, x_part, x_part))
        to_y.wait_recv()
        onward.append(send.to(me.x, y_part, y_part))

    def pass_weights(over, w):
        pass_on(*over, w.at[pl.ds(me.sx * depth, half)], w.at[pl.ds(me.sy * depth + half, half)])

    lines[0].begin()
    lines[1].begin()
    for copy in gain_copies:
        copy.wait_recv()
    width = x_ref.shape[1] // 4
    gains = jnp.concatenate([gain_slots[i][:, :width] for i in range(4)], axis=1)
    gains_out[...] = gains
    n_ref[...] = normalize(x_ref[...].astype(F32), gains[0:1])[0].astype(BF)
    n_line = RowLine(pool, me, n_ref, n_all, rows)
    e_line = RowLine(pool, me, e_ref, e_all, rows)
    n_line.begin()
    copy_here(n_ref, n_all.at[pl.ds((me.c * 4 + me.t) * rows, rows)])
    copy_here(e_ref, e_all.at[pl.ds((me.c * 4 + me.t) * rows, rows)])
    swapped = []
    for ref, pair in ((n_ref, n_pair), (x_ref, x_pair), (g_ref, g_pair), (t_ref, t_pair)):
        where = pair.at[pl.ds(me.c * ref.shape[0], ref.shape[0])]
        swapped.append(send.to(me.core, ref, where))
        copy_here(ref, where)
    lines[0].arrive(1)
    lines[1].arrive(1)
    lines[0].arrive(2)
    lines[1].arrive(2)
    n_line.step(0)
    lines[0].arrive(3)
    interleave(0)
    over0 = share(0, w0)
    lines[1].arrive(3)
    interleave(1)
    over1 = share(1, w1)
    lines[2].begin()
    e_line.begin()
    n_line.step(1)
    n_line.step(2)
    lines[2].arrive(1)
    e_line.step(0)
    pass_on(
        emb_x, emb_y, emb_all.at[me.sx, pl.ds(0, emb_half)],
        emb_all.at[me.sy, pl.ds(emb_half, emb_rows - emb_half)],
    )
    pass_weights(over0, w0)
    lines[2].arrive(2)
    e_line.step(1)
    pass_weights(over1, w1)
    lines[2].arrive(3)
    e_line.step(2)
    interleave(2)
    for copy in onward + swapped:
        copy.wait_recv()
    for line in lines + [n_line, e_line]:
        line.finish()
    send.finish()
    for copy in locals_:
        copy.wait()


def start_gather(gains, inputs, encoder, cotangent, targets, emb, bundles, cuts):
    rows, depth = inputs.shape
    part = bundles[0].shape[0]
    any_space = pl.BlockSpec(memory_space=pl.ANY)
    vmem = pl.BlockSpec(memory_space=pltpu.VMEM)
    return pl.pallas_call(
        partial(start_kernel, cuts=cuts),
        in_specs=[vmem] * 5 + [any_space] + [vmem] * 3,
        out_specs=[vmem] + [any_space] * 9 + [vmem],
        out_shape=[
            jax.ShapeDtypeStruct((gains.shape[0], depth), F32),
            jax.ShapeDtypeStruct((8 * rows, depth), BF),
            jax.ShapeDtypeStruct((8 * rows, depth), BF),
        ]
        + [jax.ShapeDtypeStruct((2 * a.shape[0], a.shape[1]), a.dtype) for a in (inputs, inputs, cotangent, targets)]
        + [jax.ShapeDtypeStruct((4,) + emb.shape, BF)]
        + [jax.ShapeDtypeStruct((4 * part, 2 * b.shape[1]), BF) for b in bundles[:2]]
        + [jax.ShapeDtypeStruct((part, 2 * bundles[2].shape[1]), BF)],
        scratch_shapes=[pltpu.VMEM((4,) + gains.shape, F32), pltpu.VMEM((rows, depth), BF)]
        + [pltpu.VMEM((2,) + b.shape, BF) for b in bundles]
        + [pltpu.VMEM((part, 2 * b.shape[1]), BF) for b in bundles[:2]]
        + [pltpu.SemaphoreType.DMA((96,)), pltpu.SemaphoreType.DMA((96,)), pltpu.SemaphoreType.DMA((16,))],
        compiler_params=pltpu.CompilerParams(collective_id=0, has_side_effects=True, vmem_limit_bytes=VMEM_LIMIT),
        name="start_gather",
    )(gains, inputs, encoder, cotangent, targets, emb, *bundles)


def rows_kernel(n_ref, n_all, sends, arrivals, local):
    me = Peers()
    meet([me.z[1], me.z[3], me.core])
    rows = n_ref.shape[0]
    copy = pltpu.make_async_copy(n_ref, n_all.at[pl.ds((me.c * 4 + me.t) * rows, rows)], local)
    copy.start()
    line = RowLine(Pool(sends, arrivals), me, n_ref, n_all, rows)
    line.begin()
    for k in range(3):
        line.step(k)
    line.finish()
    copy.wait()


def gather_rows(normed):
    rows, depth = normed.shape
    return pl.pallas_call(
        rows_kernel,
        in_specs=[pl.BlockSpec(memory_space=pltpu.VMEM)],
        out_specs=pl.BlockSpec(memory_space=pl.ANY),
        out_shape=jax.ShapeDtypeStruct((8 * rows, depth), normed.dtype),
        scratch_shapes=[pltpu.SemaphoreType.DMA((26,)), pltpu.SemaphoreType.DMA((26,)), pltpu.SemaphoreType.DMA],
        compiler_params=pltpu.CompilerParams(collective_id=1, has_side_effects=True, vmem_limit_bytes=VMEM_LIMIT),
        name="gather_rows",
    )(normed)


def stats_kernel(stats_ref, out_ref, slots, sends, arrivals):
    me = Peers()
    meet(me.group)
    send = Sender(Pool(sends, arrivals))
    here = slots.at[me.c * 4 + me.t]
    slots[me.c * 4 + me.t] = stats_ref[...]
    copies = [send.to(peer, stats_ref, here) for peer in me.group]
    for copy in copies:
        copy.wait_recv()
    lines = stats_ref.shape[0] // 3
    top = slots[0, 0:lines]
    for i in range(1, 8):
        top = jnp.maximum(top, slots[i, 0:lines])
    total = jnp.zeros_like(top)
    picked = jnp.zeros_like(top)
    for i in range(8):
        total += slots[i, lines : 2 * lines] * jnp.exp(slots[i, 0:lines] - top)
        picked += slots[i, 2 * lines : 3 * lines]
    logsum = top + jnp.log(total)
    out_ref[0] = logsum
    out_ref[1] = logsum - picked
    send.finish()


def combine_stats(stats):
    return pl.pallas_call(
        stats_kernel,
        in_specs=[pl.BlockSpec(memory_space=pltpu.VMEM)],
        out_specs=pl.BlockSpec(memory_space=pltpu.VMEM),
        out_shape=jax.ShapeDtypeStruct((2, stats.shape[0] // 3, stats.shape[1]), F32),
        scratch_shapes=[pltpu.VMEM((8,) + stats.shape, F32), pltpu.SemaphoreType.DMA((8,)), pltpu.SemaphoreType.DMA((8,))],
        compiler_params=pltpu.CompilerParams(collective_id=2, has_side_effects=True),
        name="combine_stats",
    )(stats)


def settle_first(send, me, part_ref, other, half):
    return send.to(me.core, part_ref.at[pl.ds((1 - me.c) * half, half)], other)


def settle_second(me, part_ref, other, summed, rows):
    half = 4 * rows
    for k in range(4):
        summed[k] = (
            part_ref[pl.ds(me.c * half + k * rows, rows)].astype(F32) + other[k * rows : (k + 1) * rows].astype(F32)
        ).astype(BF)


class Planar:
    def __init__(self, send, me, part, first, second, moving, chunks):
        self.send, self.me, self.part = send, me, part
        self.first, self.second, self.moving, self.chunks = first, second, moving, chunks

    def begin(self):
        me = self.me
        self.one = []
        for start, stop, along_x in self.chunks:
            here = slice(start, stop)
            near, near_block = (me.x, me.sx) if along_x else (me.y, me.sy)
            self.one.append(
                (
                    self.send.to(near, self.part.at[me.sd, here], self.first.at[1, here]),
                    self.send.to(near, self.part.at[near_block, here], self.first.at[0, here]),
                )
            )

    def gather(self, i):
        me = self.me
        start, stop, along_x = self.chunks[i]
        here = slice(start, stop)
        self.one[i][0].wait_recv()
        self.moving[here] = (
            self.part[me.sy if along_x else me.sx, here].astype(F32) + self.first[1, here].astype(F32)
        ).astype(BF)
        return here

    def own(self, i):
        start, stop, along_x = self.chunks[i]
        here = slice(start, stop)
        self.one[i][1].wait_recv()
        return self.part[self.me.s, here].astype(F32) + self.first[0, here].astype(F32)

    def go_on(self):
        self.two = []
        for start, stop, along_x in self.chunks:
            here = slice(start, stop)
            self.two.append(
                self.send.to(self.me.y if along_x else self.me.x, self.moving.at[here], self.second.at[here])
            )

    def middle(self):
        for i in range(len(self.chunks)):
            self.gather(i)
        self.go_on()

    def end(self, store):
        for i, copy in enumerate(self.two):
            start, stop, along_x = self.chunks[i]
            here = slice(start, stop)
            copy.wait_recv()
            store(here, self.own(i) + self.second[here].astype(F32))


def halves(count, parts, step):
    middle = (count // 2 + step - 1) // step * step
    out = []
    for low, high, along_x in ((0, middle, True), (middle, count, False)):
        size = ((high - low) // parts + step - 1) // step * step
        edges = list(range(low, high, size)) + [high]
        out.append([(a, b, along_x) for a, b in zip(edges[:-1], edges[1:])])
    return [chunk for pair in zip(*out) for chunk in pair]


def middle_kernel(dn_ref, de_ref, gn_ref, own_ref, move_ref, other, summed, coming, going, total, first, sends, arrivals, *, chunks):
    me = Peers()
    meet([me.z[1], me.z[3], me.core, me.x, me.y])
    pool = Pool(sends, arrivals)
    send = Sender(pool)
    rows = summed.shape[1]
    crossing = settle_first(send, me, dn_ref, other, 4 * rows)
    plane = Planar(send, me, de_ref, first, None, move_ref, chunks)
    plane.begin()
    crossing.wait_recv()
    settle_second(me, dn_ref, other, summed, rows)
    line = SumLine(pool, me, summed, coming, going)
    line.start()
    for part in range(3):
        line.add(part)
    line.result(total)
    own = pl.ds(me.c * rows, rows)
    gn_ref[own] = total[...].astype(BF)
    share = send.to(me.core, gn_ref.at[own], gn_ref.at[own])
    for i in range(len(chunks)):
        here = plane.gather(i)
        own_ref[here] = plane.own(i).astype(BF)
    share.wait_recv()
    line.finish()
    send.finish()


def middle_scatter(dn, de, vocab):
    total, depth = dn.shape
    rows = total // 8
    width = de.shape[2]
    chunks = halves(vocab, 3, 16)
    count = 2 + 12 + 2 * len(chunks)
    vmem = pl.BlockSpec(memory_space=pltpu.VMEM)
    return pl.pallas_call(
        partial(middle_kernel, chunks=chunks),
        in_specs=[vmem] * 2,
        out_specs=[vmem] * 3,
        out_shape=[
            jax.ShapeDtypeStruct((2 * rows, depth), BF),
            jax.ShapeDtypeStruct((vocab, width), BF),
            jax.ShapeDtypeStruct((vocab, width), BF),
        ],
        scratch_shapes=[
            pltpu.VMEM((4 * rows, depth), BF),
            pltpu.VMEM((4, rows, depth), BF),
            pltpu.VMEM((6, rows, depth), BF),
            pltpu.VMEM((6, rows, depth), BF),
            pltpu.VMEM((rows, depth), F32),
            pltpu.VMEM((2, vocab, width), BF),
            pltpu.SemaphoreType.DMA((count,)),
            pltpu.SemaphoreType.DMA((count,)),
        ],
        compiler_params=pltpu.CompilerParams(collective_id=3, has_side_effects=True, vmem_limit_bytes=VMEM_LIMIT),
        name="middle_scatter",
    )(dn, de)


def tail_kernel(
    dn_ref, c0, c1, c2, c3, s0, s1, s2, s3, f_ref, gains_ref, eo_ref, em_ref,
    dn_out, o0, o1, o2, gain_out, eg_out,
    g0, g1, e_second, e_sum, other, summed, coming, going, first0, second0, moving0, first1, second1, moving1,
    ab0, ab1, ab2, in0, in1, in2, out0, out1, out2, held0, held1, held2,
    slots, plane_sum, plane_slots, sends, arrivals, *, cuts, chunks,
):
    me = Peers()
    meet(me.group + [me.x, me.y, me.d])
    pool = Pool(sends, arrivals)
    send = Sender(pool)
    rows = summed.shape[1]
    crossing = settle_first(send, me, dn_ref, other, 4 * rows)
    for i, piece in enumerate((c0, c1, c2, c3)):
        g0[:, :, i * piece.shape[2] : (i + 1) * piece.shape[2]] = piece[...]
    for i, piece in enumerate((s0, s1, s2, s3)):
        g1[:, :, i * piece.shape[2] : (i + 1) * piece.shape[2]] = piece[...]
    planes = [
        Planar(send, me, g0, first0, second0, moving0, chunks),
        Planar(send, me, g1, first1, second1, moving1, chunks),
    ]
    planes[0].begin()
    planes[1].begin()
    slots[me.c * 4 + me.t] = gains_ref[...]
    gain_copies = [send.to(peer, gains_ref, slots.at[me.c * 4 + me.t]) for peer in me.group]

    def split(value, cut):
        return [
            jnp.concatenate([value[:, 2 * a + i * (b - a) : 2 * a + (i + 1) * (b - a)] for a, b in cut], axis=1).astype(BF)
            for i in range(2)
        ]

    ff_line = GradLine(pool, me, ab2, in2, out2, held2)
    lines = [GradLine(pool, me, ab0, in0, out0, held0), GradLine(pool, me, ab1, in1, out1, held1)]
    for i, half in enumerate(split(f_ref[...], cuts[2])):
        ab2[i] = half
    crossing.wait_recv()
    settle_second(me, dn_ref, other, summed, rows)
    row_line = SumLine(pool, me, summed, coming, going)
    ff_line.start()
    row_line.start()
    for part in range(3):
        ff_line.add(part)
        row_line.add(part)
    planes[0].middle()
    planes[1].middle()
    vocab, wide = eo_ref.shape
    e_half = halves(vocab, 1, 16)
    e_copies = [
        send.to(me.y if along_x else me.x, em_ref.at[start:stop], e_second.at[start:stop])
        for start, stop, along_x in e_half
    ]
    for copy in gain_copies:
        copy.wait_recv()
    total = slots[0]
    for i in range(1, 8):
        total += slots[i]
    plane_sum[...] = total
    plane_slots[me.s] = total
    plane_copies = [send.to(peer, plane_sum, plane_slots.at[me.s]) for peer in (me.x, me.y, me.d)]
    for plane, cut, ab, line in ((planes[0], cuts[0], ab0, lines[0]), (planes[1], cuts[1], ab1, lines[1])):

        def store(here, value):
            for i, half in enumerate(split(value, cut)):
                ab[i, here] = half

        plane.end(store)
        line.start()
    for part in range(3):
        lines[0].add(part)
        lines[1].add(part)
    row_line.result(dn_out)
    ff_line.settle(o2)
    for copy in e_copies:
        copy.wait_recv()
    e_sum[me.c] = (eo_ref[...].astype(F32) + e_second[...].astype(F32)).astype(BF)
    e_share = send.to(me.core, e_sum.at[me.c], e_sum.at[me.c])
    for copy in plane_copies:
        copy.wait_recv()
    gain_out[...] = plane_slots[0] + plane_slots[1] + plane_slots[2] + plane_slots[3]
    lines[0].settle(o0)
    e_share.wait_recv()
    for c in range(2):
        for p in range(2):
            first_row = (2 * c + p) * vocab
            eg_out[first_row : first_row + vocab, :] = e_sum[c, :, p * wide // 2 : (p + 1) * wide // 2]
    lines[1].settle(o1)
    for line, out in ((ff_line, o2), (lines[0], o0), (lines[1], o1)):
        line.finish(out)
    row_line.finish()
    send.finish()


def tail_scatter(dn, grads, ff, gains, emb_own, emb_move, cuts):
    total, depth = dn.shape
    rows = total // 8
    groups, part, width = grads[0][0].shape
    width *= 4
    chunks = halves(part, 1, 16)
    vmem = pl.BlockSpec(memory_space=pltpu.VMEM)
    widths = [width // 2, width // 2, ff.shape[1] // 2]
    scratch = [
        pltpu.VMEM((groups, part, width), BF),
        pltpu.VMEM((groups, part, width), BF),
        pltpu.VMEM(emb_own.shape, BF),
        pltpu.VMEM((2,) + emb_own.shape, BF),
        pltpu.VMEM((4 * rows, depth), BF),
        pltpu.VMEM((4, rows, depth), BF),
        pltpu.VMEM((6, rows, depth), BF),
        pltpu.VMEM((6, rows, depth), BF),
    ]
    for _ in grads:
        scratch += [pltpu.VMEM((2, part, width), BF), pltpu.VMEM((part, width), BF), pltpu.VMEM((part, width), BF)]
    for count in (2, 4, 4):
        scratch += [pltpu.VMEM((count, part, w), BF) for w in widths]
    scratch += [pltpu.VMEM((part, w), BF) for w in widths]
    scratch += [
        pltpu.VMEM((8,) + gains.shape, F32),
        pltpu.VMEM(gains.shape, F32),
        pltpu.VMEM((4,) + gains.shape, F32),
        pltpu.SemaphoreType.DMA((64,)),
        pltpu.SemaphoreType.DMA((64,)),
    ]
    return pl.pallas_call(
        partial(tail_kernel, cuts=cuts, chunks=chunks),
        in_specs=[vmem] * 13,
        out_specs=[vmem] * 6,
        out_shape=[jax.ShapeDtypeStruct((rows, depth), F32)]
        + [jax.ShapeDtypeStruct((part, w), F32) for w in widths]
        + [jax.ShapeDtypeStruct(gains.shape, F32)]
        + [jax.ShapeDtypeStruct((4 * emb_own.shape[0], emb_own.shape[1] // 2), BF)],
        scratch_shapes=scratch,
        compiler_params=pltpu.CompilerParams(collective_id=4, has_side_effects=True, vmem_limit_bytes=VMEM_LIMIT),
        name="tail_scatter",
    )(dn, *grads[0], *grads[1], ff, gains, emb_own, emb_move)


def normalize(hidden, gain):
    inverse = lax.rsqrt(jnp.mean(hidden * hidden, axis=-1, keepdims=True) + EPS)
    return (hidden * inverse * gain, inverse)


def norm_back(hidden, inverse, gain, upstream):
    scaled = upstream * gain
    inner = jnp.mean(scaled * hidden, axis=-1, keepdims=True)
    return inverse * scaled - hidden * (inverse * inverse * inverse) * inner


def matmul(left, right):
    return jnp.dot(left, right, preferred_element_type=F32)


def left_t(left, right):
    return jnp.einsum("ra,rb->ab", left, right, preferred_element_type=F32)


def right_t(left, right):
    return jnp.einsum("ra,ba->rb", left, right, preferred_element_type=F32)


def swap(array):
    return lax.ppermute(array, "ctx", [(0, 1), (1, 0)])


def per_device(
    inputs, encoder, prefix, targets, cotangent, gain_self, query_self, key_self, value_self, output_self,
    gain_cross, query_cross, key_cross, value_cross, output_cross, gain_hidden, gate_weight, up_weight,
    down_weight, gain_exit, embedding,
):
    tp = lax.axis_size("tp")
    ctx = lax.axis_size("ctx")
    shards = lax.axis_size("shard")
    assert tp == 4 and ctx == 2
    core = lax.axis_index("ctx")
    place = lax.axis_index("tp")
    rows, depth = inputs.shape
    group = rows * tp
    total = group * ctx
    hb = query_self.shape[1]
    width = 2 * hb
    fb = gate_weight.shape[1]
    pair = rows * ctx

    route_a = []
    route_b = []
    for c in range(2):
        for z in range(4):
            dest = c * 4 + z
            route_a.append(((z % 2) * 4 + 2 * c + z // 2, dest))
            route_b.append(((z % 2) * 4 + 2 * c + 1 - z // 2, dest))
    both = ("ctx", "tp")

    def spread_weights(parts):
        block = jnp.concatenate(parts, axis=1)
        first = lax.ppermute(block, both, route_a)
        second = lax.ppermute(block, both, route_b)
        columns = []
        start = 0
        for piece in parts:
            stop = start + piece.shape[1]
            columns += [first[:, start:stop], second[:, start:stop]]
            start = stop
        return lax.all_gather(jnp.concatenate(columns, axis=1), "shard", axis=0, tiled=True)

    def collect_weights(grad, widths):
        mine = lax.psum_scatter(grad, "shard", scatter_dimension=0, tiled=True)
        first = []
        second = []
        start = 0
        for size in widths:
            first.append(mine[:, start : start + size])
            second.append(mine[:, start + size : start + 2 * size])
            start += 2 * size
        back = lambda route: [(dest, source) for source, dest in route]
        one = lax.ppermute(jnp.concatenate(first, axis=1), both, back(route_a))
        two = lax.ppermute(jnp.concatenate(second, axis=1), both, back(route_b))
        part = (one.astype(F32) + two.astype(F32)).astype(BF)
        whole = part.astype(F32) + swap(part).astype(F32)
        outs = []
        start = 0
        for size in widths:
            outs.append(whole[:, start : start + size])
            start += size
        return outs

    def couple(own, other):
        return jnp.where(
            core == 0, jnp.concatenate([own, other], axis=0), jnp.concatenate([other, own], axis=0)
        )

    fast = shards == 4
    own_f = inputs.astype(F32)
    parts_self = [query_self, key_self, value_self, output_self.T]
    parts_cross = [query_cross, key_cross, value_cross, output_cross.T]
    parts_ff = [gate_weight, up_weight, down_weight.T]
    gain_parts = jnp.stack([gain_self, gain_cross, gain_hidden, gain_exit])
    cuts = [[(i * w, (i + 1) * w) for i in range(n)] for n, w in ((4, hb), (4, hb), (3, fb))]
    vocab_half = embedding.shape[0] // ctx
    emb_mine = lax.dynamic_slice_in_dim(embedding, core * vocab_half, vocab_half, axis=0)
    emb_mine = jnp.concatenate([emb_mine[: vocab_half // 2], emb_mine[vocab_half // 2 :]], axis=1)

    def take_pair(array):
        cut = array.reshape(ctx, group, depth)
        return lax.dynamic_slice_in_dim(cut, place * rows, rows, axis=1).reshape(pair, depth)

    if fast:
        bundles = [jnp.concatenate(parts, axis=1) for parts in (parts_self, parts_cross, parts_ff)]
        spare = -(depth // shards) % 128
        gain_block = jnp.pad(gain_parts.astype(F32), ((0, 4), (0, spare)))
        (
            gains, normed1, encoder_all, normed1_pair, x_pair, g_pair, t_pair, emb_pieces, weights_self, weights_cross,
            ff_mix,
        ) = start_gather(
            gain_block, inputs, encoder, cotangent, targets.reshape(8, group // 8), emb_mine, bundles, cuts
        )
        hidden0 = x_pair.astype(F32)
        cotangent_pair = g_pair.astype(F32)
        targets_all = t_pair.reshape(total)
        weights_ff = lax.all_gather(ff_mix, "shard", axis=0, tiled=True)
    else:
        gains = lax.all_gather(gain_parts, "shard", axis=1, tiled=True).astype(F32)
        normed1_own = normalize(own_f, gains[0])[0].astype(BF)
        normed1 = lax.all_gather(normed1_own, both, axis=0, tiled=True)
        normed1_pair = take_pair(normed1)
        encoder_all = lax.all_gather(encoder, both, axis=0, tiled=True)
        weights_self, weights_cross, weights_ff = map(spread_weights, (parts_self, parts_cross, parts_ff))
        hidden0 = couple(inputs, swap(inputs)).astype(F32)
        cotangent_pair = couple(cotangent, swap(cotangent)).astype(F32)
        targets_all = couple(targets, swap(targets))
        emb_pieces = lax.all_gather(emb_mine, "shard", axis=0)
        emb_pieces = emb_pieces.reshape(shards, vocab_half // 2, 2, depth // shards)
        emb_pieces = jnp.transpose(emb_pieces, (1, 2, 0, 3)).reshape(1, vocab_half // 2, 2 * depth)

    gain_one, gain_two, gain_three, gain_four = [gains[i] for i in range(4)]
    inverse1_own = normalize(own_f, gain_one)[1]
    query_w, key_w, value_w, out_w = [weights_self[:, i * width : (i + 1) * width] for i in range(4)]
    scale = HEAD_DIM**-0.5

    def project_q(normed, weight):
        return matmul(normed, weight).astype(BF) * jnp.asarray(scale, BF)

    positions = jnp.concatenate(
        [c * group + place * rows + jnp.arange(rows, dtype=jnp.int32) for c in range(2)]
    )
    limit = prefix[0]
    seen = jnp.maximum(positions + 1, limit)[None, :]
    chunk = 512
    last0 = jnp.maximum((place + 1) * rows, limit)
    last1 = jnp.maximum(group + (place + 1) * rows, limit)
    limits = jnp.stack([(last0 + chunk - 1) // chunk, (last1 + chunk - 1) // chunk]).astype(jnp.int32)
    causal_blocks = ((0, rows), (rows, rows))
    open_blocks = ((0, pair),)

    query1 = project_q(normed1_pair, query_w)
    kv1 = matmul(normed1, weights_self[:, width : 3 * width]).astype(BF)
    attended1, attended1_t, lse1 = attend(limits, seen, query1, kv1, True, causal_blocks, chunk)

    def add_halves(partial_sum):
        part = partial_sum.astype(BF)
        return partial_sum + swap(part).astype(F32)

    hidden1 = hidden0 + add_halves(right_t(attended1, out_w))
    query2_w, key2_w, value2_w, out2_w = [weights_cross[:, i * width : (i + 1) * width] for i in range(4)]
    kv2 = matmul(encoder_all, weights_cross[:, width : 3 * width]).astype(BF)
    normed2, inverse2 = normalize(hidden1, gain_two)
    normed2 = normed2.astype(BF)
    query2 = project_q(normed2, query2_w)
    attended2, attended2_t, lse2 = attend(limits, seen, query2, kv2, False, open_blocks, chunk)
    hidden2 = hidden1 + add_halves(right_t(attended2, out2_w))
    normed3, inverse3 = normalize(hidden2, gain_three)
    normed3 = normed3.astype(BF)
    gate_w, up_w, down_w = [weights_ff[:, i * 2 * fb : (i + 1) * 2 * fb] for i in range(3)]
    gate = matmul(normed3, gate_w)
    upper = matmul(normed3, up_w)
    active = jax.nn.gelu(gate, approximate=True)
    product = (active * upper).astype(BF)
    final = hidden2 + add_halves(right_t(product, down_w))
    normed4, inverse4 = normalize(final, gain_four)
    normed4 = normed4.astype(BF)

    def mine(array):
        return lax.dynamic_slice_in_dim(array, core * rows, rows, axis=0)

    final_own = mine(final)
    if fast:
        normed4_all = gather_rows(mine(normed4))
    else:
        normed4_all = lax.all_gather(mine(normed4), both, axis=0, tiled=True)
    local_target = (targets_all - (place * embedding.shape[0] + core * vocab_half))[None, :].astype(jnp.int32)
    vblock, rblock = 512, 512
    stats, emb, expo, tops = head_stats(emb_pieces, normed4_all, local_target, vblock, rblock)
    if fast:
        combined = combine_stats(stats)
        logsum = combined[0].reshape(total)
        loss = combined[1].reshape(total)
    else:
        every = lax.all_gather(stats.reshape(3, total), both, axis=0)
        top = jnp.max(every[:, 0], axis=0)
        summed = jnp.sum(every[:, 1] * jnp.exp(every[:, 0] - top[None]), axis=0)
        logsum = top + jnp.log(summed)
        loss = logsum - jnp.sum(every[:, 2], axis=0)
    exit_loss = lax.dynamic_slice_in_dim(loss, core * group, group, axis=0)
    groups = emb_pieces.shape[0]
    emb_grad, grad_normed4 = head_back(
        emb, expo, tops, normed4_all, local_target, logsum[None, :], groups, vocab_half, vblock, rblock
    )
    if fast:
        gn4, emb_own, emb_move = middle_scatter(grad_normed4, emb_grad, vocab_half // 2)
        gn4 = gn4.astype(F32)
    else:
        emb_grad = emb_grad[0, : vocab_half // 2].reshape(vocab_half // 2, 2, shards, depth // shards)
        emb_grad = jnp.transpose(emb_grad, (2, 0, 1, 3)).reshape(shards * vocab_half // 2, 2 * depth // shards)
        emb_sum = lax.psum_scatter(emb_grad, "shard", scatter_dimension=0, tiled=True)
        gn4_own = lax.psum_scatter(grad_normed4, both, scatter_dimension=0, tiled=True)
        gn4 = couple(gn4_own, swap(gn4_own)).astype(F32)
    gain4_rows = gn4 * final * inverse4
    grad_final = cotangent_pair + norm_back(final, inverse4, gain_four, gn4)
    grad_final_b = grad_final.astype(BF)
    down_grad = left_t(grad_final_b, product).astype(BF)
    grad_product = matmul(grad_final_b, down_w)
    unused, gelu_pull = jax.vjp(partial(jax.nn.gelu, approximate=True), gate)
    grad_gate = gelu_pull(grad_product * upper)[0].astype(BF)
    grad_upper = (grad_product * active).astype(BF)
    gate_grad = left_t(normed3, grad_gate).astype(BF)
    upper_grad = left_t(normed3, grad_upper).astype(BF)
    ff_part = jnp.concatenate([gate_grad, upper_grad, down_grad], axis=1)
    gn3 = add_halves(right_t(grad_gate, gate_w) + right_t(grad_upper, up_w))
    gain3_rows = gn3 * hidden2 * inverse3
    grad_hidden2 = grad_final + norm_back(hidden2, inverse3, gain_three, gn3)
    grad_hidden2_b = grad_hidden2.astype(BF)
    out2_grad = left_t(grad_hidden2_b, attended2).astype(BF)
    grad_attended2 = matmul(grad_hidden2_b, out2_w).astype(BF)
    if fast:
        ff_mine = lax.psum_scatter(ff_part, "shard", scatter_dimension=0, tiled=True)
    grad_query2, grad_key2, grad_value2 = attend_back(
        limits, seen, query2, kv2, grad_attended2, attended2_t, lse2, False, open_blocks, chunk
    )
    query2_grad = left_t(normed2, grad_query2).astype(BF)
    key2_grad = left_t(encoder_all, grad_key2).astype(BF)
    value2_grad = left_t(encoder_all, grad_value2).astype(BF)
    cross_parts = [query2_grad, key2_grad, value2_grad, out2_grad]
    encoder_part = (right_t(grad_key2, key2_w) + right_t(grad_value2, value2_w)).astype(BF)
    if fast:
        encoder_part, ff_mine = lax.optimization_barrier((encoder_part, ff_mine))
    encoder_grad = lax.psum_scatter(encoder_part, both, scatter_dimension=0, tiled=True).astype(F32)
    gn2 = add_halves(right_t(grad_query2, query2_w))
    gain2_rows = gn2 * hidden1 * inverse2
    grad_hidden1 = grad_hidden2 + norm_back(hidden1, inverse2, gain_two, gn2)
    grad_hidden1_b = grad_hidden1.astype(BF)
    out_grad = left_t(grad_hidden1_b, attended1).astype(BF)
    grad_attended1 = matmul(grad_hidden1_b, out_w).astype(BF)
    grad_query1, grad_key1, grad_value1 = attend_back(
        limits, seen, query1, kv1, grad_attended1, attended1_t, lse1, True, causal_blocks, chunk
    )
    query_grad = left_t(normed1_pair, grad_query1).astype(BF)
    key_grad = left_t(normed1, grad_key1).astype(BF)
    value_grad = left_t(normed1, grad_value1).astype(BF)
    self_parts = [query_grad, key_grad, value_grad, out_grad]
    normed1_part = right_t(grad_key1, key_w) + right_t(grad_value1, value_w)
    query_part = right_t(grad_query1, query_w).reshape(ctx, rows, depth)
    cut = normed1_part.reshape(ctx, group, depth)
    old = lax.dynamic_slice_in_dim(cut, place * rows, rows, axis=1)
    cut = lax.dynamic_update_slice_in_dim(cut, old + query_part, place * rows, axis=1)
    cut = cut.reshape(total, depth).astype(BF)

    def gain_rows(gn1):
        gain1_sum = jnp.sum(gn1 * own_f * inverse1_own, axis=0)
        return jnp.stack(
            [gain1_sum] + [jnp.sum(mine(a), axis=0) for a in (gain2_rows, gain3_rows, gain4_rows)]
        )

    if fast:
        blocks = [
            [a.reshape(shards, depth // shards, a.shape[1]) for a in parts] for parts in (cross_parts, self_parts)
        ]
        cut, encoder_grad = lax.optimization_barrier((cut, encoder_grad))
        gain1_part = jnp.sum(cut.astype(F32) * normed1.astype(F32), axis=0) / gain_one
        gains_part = [gain1_part] + [jnp.sum(mine(a), axis=0) for a in (gain2_rows, gain3_rows, gain4_rows)]
        gain_pad = jnp.stack(gains_part + [jnp.zeros_like(gain1_part)] * 4)
        gn1, cross_own, self_own, ff_own, gain_sums, embedding_grad = tail_scatter(
            cut, blocks, ff_mine, gain_pad, emb_own, emb_move, [cuts[1], cuts[0], cuts[2]]
        )
        embedding_grad = embedding_grad.astype(F32)
        take = lambda own, index: [own[:, a:b] for a, b in cuts[index]]
        self_grads, cross_grads, ff_grads = take(self_own, 0), take(cross_own, 1), take(ff_own, 2)
    else:
        emb_other = swap(emb_sum)
        emb_halves = [jnp.where(core == 0, emb_sum, emb_other), jnp.where(core == 0, emb_other, emb_sum)]
        slim = depth // shards
        embedding_grad = jnp.concatenate(
            [half[:, p * slim : (p + 1) * slim] for half in emb_halves for p in range(2)], axis=0
        ).astype(F32)
        gn1 = lax.psum_scatter(cut, both, scatter_dimension=0, tiled=True).astype(F32)
        ff_grads = collect_weights(ff_part, [fb, fb, fb])
        cross_grads = collect_weights(jnp.concatenate(cross_parts, axis=1), [hb] * 4)
        self_grads = collect_weights(jnp.concatenate(self_parts, axis=1), [hb] * 4)
        gain_sums = lax.psum(gain_rows(gn1), ("shard", "ctx", "tp"))
    inputs_grad = mine(grad_hidden1) + norm_back(own_f, inverse1_own, gain_one, gn1)
    part = depth // shards
    gain_grads = lax.dynamic_slice_in_dim(gain_sums, lax.axis_index("shard") * part, part, axis=1)
    return (
        final_own.astype(BF), exit_loss, inputs_grad, encoder_grad,
        gain_grads[0], self_grads[0], self_grads[1], self_grads[2], self_grads[3].T,
        gain_grads[1], cross_grads[0], cross_grads[1], cross_grads[2], cross_grads[3].T,
        gain_grads[2], ff_grads[0], ff_grads[1], ff_grads[2].T,
        gain_grads[3], embedding_grad,
    )


def solution(mesh):
    rows = P(("shard", "ctx", "tp"), None)
    into = P("shard", "tp")
    out = P("tp", "shard")
    gain = P("shard")
    weights = (gain, into, into, into, out, gain, into, into, into, out, gain, into, into, out, gain, out)
    return jax.shard_map(
        per_device,
        mesh=mesh,
        in_specs=(rows, rows, P("shard"), P(("shard", "ctx")), rows) + weights,
        out_specs=(rows, P(("shard", "ctx")), rows, rows) + weights,
        check_vma=False,
    )
```

```python
from functools import partial

import jax
import jax.numpy as jnp
from jax import lax
from jax.experimental import pallas as pl
from jax.experimental.pallas import tpu as pltpu
from jax.sharding import PartitionSpec as P

HEAD_DIM = 64
EPS = 1e-06
MASKED = -1e30
BF = jnp.bfloat16
F32 = jnp.float32
VMEM_LIMIT = 58 * 2**20


def attend_kernel(seen_ref, q_ref, k_ref, v_ref, o_ref, ot_ref, lse_ref, vt_ref, *, tiles):
    half = lax.broadcasted_iota(jnp.int32, (2 * HEAD_DIM, 1), 0) // HEAD_DIM
    vt_ref[...] = jnp.transpose(v_ref[...])
    q_t = jnp.transpose(q_ref[...])
    for head in range(2):
        part = slice(head * HEAD_DIM, (head + 1) * HEAD_DIM)
        state = None
        for rows, keys, masked in tiles:
            qt = jnp.where(half == head, q_t[:, rows[0] : rows[1]], 0).astype(BF)
            scores = jnp.dot(k_ref[keys[0] : keys[1], :], qt, preferred_element_type=F32)
            if masked:
                key = lax.broadcasted_iota(jnp.int32, (keys[1] - keys[0], 1), 0) + keys[0]
                scores = jnp.where(key < seen_ref[:, rows[0] : rows[1]], scores, MASKED)
            top = jnp.max(scores, axis=0, keepdims=True)
            if state is not None:
                base, old_top, old_total, old_acc = state
                cut = slice(rows[0] - base, rows[1] - base)
                top = jnp.maximum(top, old_top[:, cut])
                shrink = jnp.exp(old_top[:, cut] - top)
            expo = jnp.exp(scores - top)
            total = jnp.sum(expo, axis=0, keepdims=True)
            acc = jnp.dot(vt_ref[part, keys[0] : keys[1]], expo.astype(BF), preferred_element_type=F32)
            if state is not None:
                total += old_total[:, cut] * shrink
                acc += old_acc[:, cut] * shrink
            state = (rows[0], top, total, acc)
            ot_ref[part, rows[0] : rows[1]] = acc / total
            lse_ref[0, head : head + 1, rows[0] : rows[1]] = top + jnp.log(total)
    o_ref[...] = jnp.transpose(ot_ref[...]).astype(BF)


def attend(seen, query, kv, tiles):
    rows, width = query.shape
    count = kv.shape[0]
    pair = 2 * HEAD_DIM
    pairs = width // pair
    return pl.pallas_call(
        partial(attend_kernel, tiles=tiles),
        grid=(pairs,),
        in_specs=[
            pl.BlockSpec((1, rows), lambda p: (0, 0)),
            pl.BlockSpec((rows, pair), lambda p: (0, p)),
            pl.BlockSpec((count, pair), lambda p: (0, p)),
            pl.BlockSpec((count, pair), lambda p: (0, p + pairs)),
        ],
        out_specs=[
            pl.BlockSpec((rows, pair), lambda p: (0, p)),
            pl.BlockSpec((pair, rows), lambda p: (p, 0)),
            pl.BlockSpec((1, 8, rows), lambda p: (p, 0, 0)),
        ],
        scratch_shapes=[pltpu.VMEM((pair, count), BF)],
        out_shape=(
            jax.ShapeDtypeStruct((rows, width), BF),
            jax.ShapeDtypeStruct((width, rows), F32),
            jax.ShapeDtypeStruct((pairs, 8, rows), F32),
        ),
        compiler_params=pltpu.CompilerParams(vmem_limit_bytes=VMEM_LIMIT),
        cost_estimate=pl.CostEstimate(
            flops=4 * rows * count * width, transcendentals=rows * count * width // HEAD_DIM,
            bytes_accessed=2 * count * width * 2 + 8 * rows * width,
        ),
        name="attend",
    )(seen, query, kv, kv)


def attend_back_kernel(
    seen_ref, q_ref, k_ref, v_ref, do_ref, ot_ref, lse_ref, dq_ref, dk_ref, dv_ref, dk_acc, dv_acc, dqt_acc, kt_ref, *, tiles
):
    half = lax.broadcasted_iota(jnp.int32, (2 * HEAD_DIM, 1), 0) // HEAD_DIM
    lane = lax.broadcasted_iota(jnp.int32, (1, 2 * HEAD_DIM), 1) // HEAD_DIM
    kt_ref[...] = jnp.transpose(k_ref[...])
    q_t = jnp.transpose(q_ref[...])
    do_t = jnp.transpose(do_ref[...])
    dqt_acc[...] = jnp.zeros_like(dqt_acc)
    done = []
    for head in range(2):
        part = slice(head * HEAD_DIM, (head + 1) * HEAD_DIM)
        inner_all = jnp.sum(do_t[part].astype(F32) * ot_ref[part], axis=0, keepdims=True)
        for rows, keys, masked in tiles:
            cut = slice(rows[0], rows[1])
            here = slice(keys[0], keys[1])
            qt = jnp.where(half == head, q_t[:, cut], 0).astype(BF)
            dot_t = jnp.where(half == head, do_t[:, cut], 0).astype(BF)
            q = jnp.where(lane == head, q_ref[cut, :], 0).astype(BF)
            do = jnp.where(lane == head, do_ref[cut, :], 0).astype(BF)
            scores = jnp.dot(k_ref[here, :], qt, preferred_element_type=F32)
            probs = jnp.exp(scores - lse_ref[0, head : head + 1, cut])
            if masked:
                key = lax.broadcasted_iota(jnp.int32, (keys[1] - keys[0], 1), 0) + keys[0]
                probs = jnp.where(key < seen_ref[:, cut], probs, 0.0)
            grad_probs = jnp.dot(v_ref[here, :], dot_t, preferred_element_type=F32)
            grad_scores = (probs * (grad_probs - inner_all[:, cut])).astype(BF)
            dv = jnp.dot(probs.astype(BF), do, preferred_element_type=F32)
            dk = jnp.dot(grad_scores, q, preferred_element_type=F32)
            if keys in done:
                dv_acc[here, :] += dv
                dk_acc[here, :] += dk
            else:
                dv_acc[here, :] = dv
                dk_acc[here, :] = dk
                done.append(keys)
            dqt_acc[part, cut] += jnp.dot(kt_ref[part, here], grad_scores, preferred_element_type=F32)
    dq_ref[...] = jnp.transpose(dqt_acc[...] * HEAD_DIM**-0.5).astype(BF)
    dk_ref[...] = dk_acc[...].astype(BF)
    dv_ref[...] = dv_acc[...].astype(BF)


def attend_back(seen, query, kv, grad, out_t, lse, tiles):
    rows, width = query.shape
    count = kv.shape[0]
    pair = 2 * HEAD_DIM
    pairs = width // pair
    by_column = pl.BlockSpec((rows, pair), lambda p: (0, p))
    key_spec = pl.BlockSpec((count, pair), lambda p: (0, p))
    return pl.pallas_call(
        partial(attend_back_kernel, tiles=tiles),
        grid=(pairs,),
        in_specs=[
            pl.BlockSpec((1, rows), lambda p: (0, 0)),
            by_column,
            key_spec,
            pl.BlockSpec((count, pair), lambda p: (0, p + pairs)),
            by_column,
            pl.BlockSpec((pair, rows), lambda p: (p, 0)),
            pl.BlockSpec((1, 8, rows), lambda p: (p, 0, 0)),
        ],
        out_specs=[by_column, key_spec, key_spec],
        scratch_shapes=[
            pltpu.VMEM((count, pair), F32),
            pltpu.VMEM((count, pair), F32),
            pltpu.VMEM((pair, rows), F32),
            pltpu.VMEM((pair, count), BF),
        ],
        out_shape=(
            jax.ShapeDtypeStruct((rows, width), BF),
            jax.ShapeDtypeStruct((count, width), BF),
            jax.ShapeDtypeStruct((count, width), BF),
        ),
        compiler_params=pltpu.CompilerParams(vmem_limit_bytes=VMEM_LIMIT),
        cost_estimate=pl.CostEstimate(
            flops=10 * rows * count * width, transcendentals=rows * count * width // HEAD_DIM,
            bytes_accessed=5 * count * width * 2 + 14 * rows * width,
        ),
        name="attend_back",
    )(seen, query, kv, kv, grad, out_t, lse)


def vocab_ids(step, block, vocab):
    ids = lax.broadcasted_iota(jnp.int32, (block, 1), 0) + step * block
    valid = ids < vocab
    return jnp.where(valid, ids, 2**30), valid


def head_stats_kernel(emb_ref, n_ref, target_ref, stats_ref, expo_ref, tops_ref, nt_ref, run_ref, *, vocab, block, rows, scale):
    step = pl.program_id(0)
    ids, valid = vocab_ids(step, block, vocab)
    emb = jnp.transpose(emb_ref[...])
    total = n_ref.shape[0]

    @pl.when(step == 0)
    def _():
        run_ref[0:1, :] = jnp.full((1, total), MASKED, F32)
        run_ref[1:8, :] = jnp.zeros((7, total), F32)
        for first in range(0, total, rows):
            nt_ref[:, first : first + rows] = jnp.transpose(n_ref[first : first + rows, :])

    for first in range(0, total, rows):
        columns = slice(first, first + rows)
        logits = jnp.dot(emb, nt_ref[:, columns], preferred_element_type=F32) * scale
        logits = jnp.where(valid, logits, MASKED)
        top = run_ref[0:1, columns]
        new_top = jnp.maximum(top, jnp.max(logits, axis=0, keepdims=True))
        expo = jnp.exp(logits - new_top)
        expo_ref[:, columns] = expo.astype(BF)
        run_ref[0:1, columns] = new_top
        run_ref[1:2, columns] = run_ref[1:2, columns] * jnp.exp(top - new_top) + jnp.sum(expo, axis=0, keepdims=True)
        run_ref[2:3, columns] += jnp.sum(jnp.where(ids == target_ref[:, columns], logits, 0.0), axis=0, keepdims=True)
    tops_ref[pl.ds(step, 1), :] = run_ref[0:1, :]

    @pl.when(step == pl.num_programs(0) - 1)
    def _():
        lines = total // 128
        for k in range(3):
            for i in range(lines):
                stats_ref[k * lines + i : k * lines + i + 1, :] = run_ref[k : k + 1, i * 128 : (i + 1) * 128]


def head_stats(emb_t, normed, target, vocab, block, rows):
    total, depth = normed.shape
    steps = emb_t.shape[1] // block
    lines = (steps + 7) // 8 * 8
    return pl.pallas_call(
        partial(head_stats_kernel, vocab=vocab, block=block, rows=rows, scale=depth**-0.5),
        grid=(steps,),
        in_specs=[
            pl.BlockSpec((depth, block), lambda i: (0, i)),
            pl.BlockSpec((total, depth), lambda i: (0, 0)),
            pl.BlockSpec((1, total), lambda i: (0, 0)),
        ],
        out_specs=[
            pl.BlockSpec((3 * total // 128, 128), lambda i: (0, 0)),
            pl.BlockSpec((block, total), lambda i: (i, 0)),
            pl.BlockSpec((lines, total), lambda i: (0, 0)),
        ],
        out_shape=(
            jax.ShapeDtypeStruct((3 * total // 128, 128), F32),
            jax.ShapeDtypeStruct((steps * block, total), BF),
            jax.ShapeDtypeStruct((lines, total), F32),
        ),
        scratch_shapes=[pltpu.VMEM((depth, total), BF), pltpu.VMEM((8, total), F32)],
        compiler_params=pltpu.CompilerParams(vmem_limit_bytes=VMEM_LIMIT),
        cost_estimate=pl.CostEstimate(
            flops=2 * vocab * depth * total, transcendentals=vocab * total,
            bytes_accessed=2 * vocab * depth + 2 * depth * total + 2 * vocab * total,
        ),
        name="head_stats",
    )(emb_t, normed, target)


def head_back_kernel(
    emb_ref, expo_ref, tops_ref, n_ref, target_ref, lse_ref, de_ref, dn_ref, dnt_acc, *, vocab, block, rows, scale
):
    step = pl.program_id(0)
    ids, valid = vocab_ids(step, block, vocab)
    factor = jnp.exp(tops_ref[pl.ds(step, 1), :] - lse_ref[...])

    @pl.when(step == 0)
    def _():
        dnt_acc[...] = jnp.zeros_like(dnt_acc)

    de = None
    for first in range(0, n_ref.shape[0], rows):
        columns = slice(first, first + rows)
        probs = expo_ref[:, columns].astype(F32) * factor[:, columns]
        grad = jnp.where(ids == target_ref[:, columns], probs - 1.0, probs).astype(BF)
        term = jnp.dot(grad, n_ref[columns, :], preferred_element_type=F32)
        de = term if de is None else de + term
        dnt_acc[:, columns] += jnp.dot(emb_ref[...], grad, preferred_element_type=F32)
    de_ref[...] = jnp.transpose((de * scale).astype(BF))

    @pl.when(step == pl.num_programs(0) - 1)
    def _():
        dn_ref[...] = (jnp.transpose(dnt_acc[...]) * scale).astype(BF)


def head_back(emb_t, expo, tops, normed, target, lse, vocab, block, rows):
    total, depth = normed.shape
    steps = emb_t.shape[1] // block
    return pl.pallas_call(
        partial(head_back_kernel, vocab=vocab, block=block, rows=rows, scale=depth**-0.5),
        grid=(steps,),
        in_specs=[
            pl.BlockSpec((depth, block), lambda i: (0, i)),
            pl.BlockSpec((block, total), lambda i: (i, 0)),
            pl.BlockSpec(tops.shape, lambda i: (0, 0)),
            pl.BlockSpec((total, depth), lambda i: (0, 0)),
            pl.BlockSpec((1, total), lambda i: (0, 0)),
            pl.BlockSpec((1, total), lambda i: (0, 0)),
        ],
        out_specs=[
            pl.BlockSpec((depth, block), lambda i: (0, i)),
            pl.BlockSpec((total, depth), lambda i: (0, 0)),
        ],
        out_shape=(
            jax.ShapeDtypeStruct(emb_t.shape, BF),
            jax.ShapeDtypeStruct((total, depth), BF),
        ),
        scratch_shapes=[pltpu.VMEM((depth, total), F32)],
        compiler_params=pltpu.CompilerParams(vmem_limit_bytes=VMEM_LIMIT),
        cost_estimate=pl.CostEstimate(
            flops=4 * vocab * depth * total, transcendentals=0,
            bytes_accessed=4 * vocab * depth + 6 * depth * total + 2 * vocab * total,
        ),
        name="head_back",
    )(emb_t, expo, tops, normed, target, lse)


MESH = pl.DeviceIdType.MESH


class Peers:
    def __init__(self):
        self.s, self.c, self.t = (lax.axis_index(name) for name in ("shard", "ctx", "tp"))
        s, c, t = self.s, self.c, self.t
        self.sx = s + 1 - 2 * lax.rem(s, 2)
        self.sy = lax.rem(s + 2, 4)
        self.sd = lax.rem(self.sx + 2, 4)
        self.x = (self.sx, c, t)
        self.y = (self.sy, c, t)
        self.d = (self.sd, c, t)
        self.core = (s, 1 - c, t)
        self.z = [(s, c, lax.rem(t + k, 4)) for k in range(4)]
        self.z_other = [(s, 1 - c, lax.rem(t + k, 4)) for k in range(4)]
        self.group = self.z[1:] + self.z_other


def meet(peers):
    barrier = pltpu.get_barrier_semaphore()
    for peer in peers:
        pl.semaphore_signal(barrier, inc=1, device_id=peer, device_id_type=MESH)
    pl.semaphore_wait(barrier, len(peers))


class Pool:
    def __init__(self, sends, arrivals):
        self.sends, self.arrivals, self.count = sends, arrivals, 0

    def take(self, count):
        first = self.count
        self.count += count
        return first

    def copy(self, index, peer, source, target):
        return pltpu.make_async_remote_copy(
            src_ref=source, dst_ref=target, send_sem=self.sends.at[index],
            recv_sem=self.arrivals.at[index], device_id=peer, device_id_type=MESH,
        )


class Sender:
    def __init__(self, pool):
        self.pool, self.all = pool, []

    def to(self, peer, source, target):
        copy = self.pool.copy(self.pool.take(1), peer, source, target)
        self.all.append(copy)
        copy.start()
        return copy

    def finish(self):
        for copy in self.all:
            copy.wait_send()


class RowLine:
    def __init__(self, pool, me, own, everyone, rows, pieces=2):
        self.pool, self.me, self.own, self.everyone = pool, me, own, everyone
        self.rows, self.pieces, self.sub = rows, pieces, rows // pieces
        self.first = pool.take(13 * pieces)

    def block(self, chip, piece):
        return self.everyone.at[pl.ds((self.me.c * 4 + chip) * self.rows + piece * self.sub, self.sub)]

    def source(self, own, chip, piece):
        return self.own.at[pl.ds(piece * self.sub, self.sub)] if own else self.block(chip, piece)

    def make(self, slot, piece, peer, chip, own=False):
        index = self.first + slot * self.pieces + piece
        return self.pool.copy(index, peer, self.source(own, chip, piece), self.block(chip, piece))

    def right(self, k, piece):
        return self.make(k, piece, self.me.z[1], self.me.t - k, k == 0)

    def left(self, k, piece):
        return self.make(3 + k, piece, self.me.z[3], self.me.t + k, k == 0)

    def across(self, slot, piece, chip, own=False):
        return self.make(6 + slot, piece, self.me.core, chip, own)

    def begin(self):
        t = self.me.t
        for p in range(self.pieces):
            pl.when(t < 3)(lambda: self.right(0, p).start())
            pl.when(t > 0)(lambda: self.left(0, p).start())
        for p in range(self.pieces):
            self.across(0, p, t, True).start()

    def step(self, k):
        t = self.me.t
        for p in range(self.pieces):

            @pl.when(t > k)
            def _():
                chip = t - 1 - k
                self.make(k, p, self.me.z[1], chip).wait_recv()
                if k < 2:
                    pl.when(t < 3)(lambda: self.right(k + 1, p).start())
                self.across(1 + k, p, chip).start()

            @pl.when(t + k < 3)
            def _():
                chip = t + 1 + k
                self.make(3 + k, p, self.me.z[3], chip).wait_recv()
                if k < 2:
                    pl.when(t > 0)(lambda: self.left(k + 1, p).start())
                self.across(4 + k, p, chip).start()

    def finish(self):
        t = self.me.t
        for p in range(self.pieces):
            pl.when(t < 3)(lambda: self.right(0, p).wait_send())
            pl.when(t > 0)(lambda: self.left(0, p).wait_send())
            self.across(0, p, t, True).wait()
            for k in range(3):

                @pl.when(t > k)
                def _():
                    if k < 2:
                        pl.when(t < 3)(lambda: self.right(k + 1, p).wait_send())
                    self.across(1 + k, p, t - 1 - k).wait()

                @pl.when(t + k < 3)
                def _():
                    if k < 2:
                        pl.when(t > 0)(lambda: self.left(k + 1, p).wait_send())
                    self.across(4 + k, p, t + 1 + k).wait()


class BlockLine:
    def __init__(self, pool, me, own, take):
        self.pool, self.me, self.own, self.take = pool, me, own, take
        self.first = pool.take(4)
        self.where = [(me.c + 1, 1 - me.c), (3 * me.c, me.c)]

    def right(self, i):
        here = self.take.at[self.where[i][1]]
        return self.pool.copy(self.first + i, self.me.z[1], here, here)

    def left(self, i):
        here = self.take.at[self.where[i][1]]
        return self.pool.copy(self.first + 2 + i, self.me.z[3], here, here)

    def begin(self):
        t = self.me.t
        for i, (block, slot) in enumerate(self.where):

            @pl.when(t == block)
            def _():
                self.take[slot] = self.own[...]
                pl.when(t < 3)(lambda: self.right(i).start())
                pl.when(t > 0)(lambda: self.left(i).start())

    def arrive(self, distance):
        t = self.me.t
        for i, (block, slot) in enumerate(self.where):

            @pl.when(t - block == distance)
            def _():
                self.right(i).wait_recv()
                pl.when(t < 3)(lambda: self.right(i).start())

            @pl.when(block - t == distance)
            def _():
                self.left(i).wait_recv()
                pl.when(t > 0)(lambda: self.left(i).start())

    def finish(self):
        t = self.me.t
        for i, (block, slot) in enumerate(self.where):
            pl.when((t >= block) & (t < 3))(lambda: self.right(i).wait_send())
            pl.when((t <= block) & (t > 0))(lambda: self.left(i).wait_send())


class SumLine:
    def __init__(self, pool, me, own, coming, going, pieces=2):
        self.pool, self.me, self.own, self.coming, self.going = pool, me, own, coming, going
        self.pieces, self.sub = pieces, own.shape[1] // pieces
        self.first = pool.take(6 * pieces)

    def copy(self, slot, piece, source):
        here = pl.ds(piece * self.sub, self.sub)
        peer = self.me.z[1] if slot < 3 else self.me.z[3]
        return self.pool.copy(
            self.first + slot * self.pieces + piece, peer, source.at[here], self.coming.at[slot, here]
        )

    def dest(self, slot):
        return 3 - slot if slot < 3 else slot - 3

    def direct(self, slot):
        return self.me.t == (0 if slot < 3 else 3)

    def start(self):
        for slot in (0, 3, 1, 4, 2, 5):

            @pl.when(self.direct(slot))
            def _():
                for p in range(self.pieces):
                    self.copy(slot, p, self.own.at[self.dest(slot)]).start()

    passing = ((0, 1), (3, 2), (1, 1), (4, 2), (0, 2), (3, 1))

    def add(self, part):
        for slot, chip in self.passing[2 * part : 2 * part + 2]:

            @pl.when(self.me.t == chip)
            def _():
                for p in range(self.pieces):
                    here = pl.ds(p * self.sub, self.sub)
                    self.copy(slot, p, self.going.at[slot]).wait_recv()
                    self.going[slot, here] = (
                        self.own[self.dest(slot), here].astype(F32) + self.coming[slot, here].astype(F32)
                    ).astype(BF)
                    self.copy(slot, p, self.going.at[slot]).start()

    def result(self, out):
        t = self.me.t
        for slot in range(6):

            @pl.when(t == self.dest(slot))
            def _():
                for p in range(self.pieces):
                    self.copy(slot, p, self.going.at[slot]).wait_recv()

        out[...] = self.own[t].astype(F32)

        @pl.when(t > 0)
        def _():
            out[...] += self.coming[3 - t].astype(F32)

        @pl.when(t < 3)
        def _():
            out[...] += self.coming[3 + t].astype(F32)

    def finish(self):
        for slot in range(6):

            @pl.when(self.direct(slot))
            def _():
                for p in range(self.pieces):
                    self.copy(slot, p, self.own.at[self.dest(slot)]).wait_send()

        for slot, chip in self.passing:

            @pl.when(self.me.t == chip)
            def _():
                for p in range(self.pieces):
                    self.copy(slot, p, self.going.at[slot]).wait_send()


class GradLine:
    def __init__(self, pool, me, own, coming, going, shared):
        self.pool, self.me, self.own, self.coming, self.going, self.shared = pool, me, own, coming, going, shared
        self.first = pool.take(5)
        self.home = me.c == me.t // 2

    def copy(self, slot, source):
        peer = self.me.z[1] if slot < 2 else self.me.z[3]
        return self.pool.copy(self.first + slot, peer, source, self.coming.at[slot])

    def index(self, slot):
        return (1, 0, 0, 1)[slot]

    def block(self, slot):
        return 2 * self.me.c + self.index(slot)

    def direct(self, slot):
        t = self.me.t
        return (t == 0) & (self.block(slot) > 0) if slot < 2 else (t == 3) & (self.block(slot) < 3)

    def start(self):
        for slot in (0, 2, 1, 3):
            pl.when(self.direct(slot))(lambda: self.copy(slot, self.own.at[self.index(slot)]).start())

    passing = ((0, 1), (2, 2), (1, 1), (3, 2), (0, 2), (2, 1))

    def adds(self, slot, chip):
        return (self.me.t == chip) & ((chip < self.block(slot)) if slot < 2 else (chip > self.block(slot)))

    def add(self, part):
        for slot, chip in self.passing[2 * part : 2 * part + 2]:

            @pl.when(self.adds(slot, chip))
            def _():
                self.copy(slot, self.going.at[slot]).wait_recv()
                self.going[slot] = (
                    self.own[self.index(slot)].astype(F32) + self.coming[slot].astype(F32)
                ).astype(BF)
                self.copy(slot, self.going.at[slot]).start()

    def share(self):
        return self.pool.copy(self.first + 4, self.me.core, self.shared, self.shared)

    def settle(self, total):
        t = self.me.t

        for slot in range(4):
            ends = (t == self.block(slot)) & (t > 0 if slot < 2 else t < 3)
            pl.when(ends)(lambda: self.copy(slot, self.going.at[slot]).wait_recv())

        @pl.when(self.home)
        def _():
            j = lax.rem(t, 2)
            total[...] = self.own[j].astype(F32)

            @pl.when(t > 0)
            def _():
                total[...] += self.coming[1 - j].astype(F32)

            @pl.when(t < 3)
            def _():
                total[...] += self.coming[2 + j].astype(F32)

            self.shared[...] = total[...].astype(BF)
            self.share().start()

    def finish(self):
        for slot in range(4):
            pl.when(self.direct(slot))(lambda: self.copy(slot, self.own.at[self.index(slot)]).wait_send())
        for slot, chip in self.passing:
            pl.when(self.adds(slot, chip))(lambda: self.copy(slot, self.going.at[slot]).wait_send())
        pl.when(self.home)(lambda: self.share().wait_send())
        pl.when(jnp.logical_not(self.home))(lambda: self.share().wait_recv())


def start_kernel(
    gains_ref, x_ref, e_ref, g_ref, t_ref, b0, b1, b2, gains_out, n_all, e_all, n_pair, x_pair, g_pair, t_pair, w0, w1, mix2,
    gain_slots, n_ref, take0, take1, take2, mix0, mix1, sends, arrivals, local, *, cuts,
):
    me = Peers()
    meet([me.z[1], me.z[3], me.core, me.x, me.y, me.d])
    pool = Pool(sends, arrivals)
    send = Sender(pool)
    rows = x_ref.shape[0]
    locals_ = []

    def copy_here(source, target):
        copy = pltpu.make_async_copy(source, target, local.at[len(locals_)])
        copy.start()
        locals_.append(copy)

    gain_slots[me.s] = gains_ref[...]
    gain_copies = [send.to(peer, gains_ref, gain_slots.at[me.s]) for peer in (me.x, me.y, me.d)]
    bundles = [(b0, take0, mix0), (b1, take1, mix1), (b2, take2, mix2)]
    lines = [BlockLine(pool, me, block, take) for block, take, mix in bundles]

    def interleave(i):
        block, take, mix = bundles[i]
        first = take[0]
        second = take[1]
        columns = []
        for start, stop in cuts[i]:
            columns += [first[:, start:stop], second[:, start:stop]]
        mix[...] = jnp.concatenate(columns, axis=1)

    depth = b0.shape[0]
    half = depth // 2
    mine = pl.ds(me.s * depth, depth)

    def share(i, w):
        mix = bundles[i][2]
        copy_here(mix, w.at[mine])
        return send.to(me.x, mix, w.at[mine]), send.to(me.y, mix, w.at[mine])

    onward = []

    def pass_on(to_x, to_y, x_part, y_part):
        to_x.wait_recv()
        onward.append(send.to(me.y, x_part, x_part))
        to_y.wait_recv()
        onward.append(send.to(me.x, y_part, y_part))

    def pass_weights(over, w):
        pass_on(*over, w.at[pl.ds(me.sx * depth, half)], w.at[pl.ds(me.sy * depth + half, half)])

    lines[0].begin()
    lines[1].begin()
    for copy in gain_copies:
        copy.wait_recv()
    width = x_ref.shape[1] // 4
    gains = jnp.concatenate([gain_slots[i][:, :width] for i in range(4)], axis=1)
    gains_out[...] = gains
    n_ref[...] = normalize(x_ref[...].astype(F32), gains[0:1])[0].astype(BF)
    n_line = RowLine(pool, me, n_ref, n_all, rows)
    e_line = RowLine(pool, me, e_ref, e_all, rows)
    n_line.begin()
    copy_here(n_ref, n_all.at[pl.ds((me.c * 4 + me.t) * rows, rows)])
    copy_here(e_ref, e_all.at[pl.ds((me.c * 4 + me.t) * rows, rows)])
    swapped = []
    for ref, pair in ((n_ref, n_pair), (x_ref, x_pair), (g_ref, g_pair), (t_ref, t_pair)):
        where = pair.at[pl.ds(me.c * ref.shape[0], ref.shape[0])]
        swapped.append(send.to(me.core, ref, where))
        copy_here(ref, where)
    lines[0].arrive(1)
    lines[1].arrive(1)
    lines[0].arrive(2)
    lines[1].arrive(2)
    n_line.step(0)
    lines[0].arrive(3)
    interleave(0)
    over0 = share(0, w0)
    lines[1].arrive(3)
    interleave(1)
    over1 = share(1, w1)
    lines[2].begin()
    e_line.begin()
    n_line.step(1)
    n_line.step(2)
    lines[2].arrive(1)
    e_line.step(0)
    pass_weights(over0, w0)
    lines[2].arrive(2)
    e_line.step(1)
    pass_weights(over1, w1)
    lines[2].arrive(3)
    e_line.step(2)
    interleave(2)
    for copy in onward + swapped:
        copy.wait_recv()
    for line in lines + [n_line, e_line]:
        line.finish()
    send.finish()
    for copy in locals_:
        copy.wait()


def start_gather(gains, inputs, encoder, cotangent, targets, bundles, cuts):
    rows, depth = inputs.shape
    part = bundles[0].shape[0]
    any_space = pl.BlockSpec(memory_space=pl.ANY)
    vmem = pl.BlockSpec(memory_space=pltpu.VMEM)
    return pl.pallas_call(
        partial(start_kernel, cuts=cuts),
        in_specs=[vmem] * 8,
        out_specs=[vmem] + [any_space] * 8 + [vmem],
        out_shape=[
            jax.ShapeDtypeStruct((gains.shape[0], depth), F32),
            jax.ShapeDtypeStruct((8 * rows, depth), BF),
            jax.ShapeDtypeStruct((8 * rows, depth), BF),
        ]
        + [jax.ShapeDtypeStruct((2 * a.shape[0], a.shape[1]), a.dtype) for a in (inputs, inputs, cotangent, targets)]
        + [jax.ShapeDtypeStruct((4 * part, 2 * b.shape[1]), BF) for b in bundles[:2]]
        + [jax.ShapeDtypeStruct((part, 2 * bundles[2].shape[1]), BF)],
        scratch_shapes=[pltpu.VMEM((4,) + gains.shape, F32), pltpu.VMEM((rows, depth), BF)]
        + [pltpu.VMEM((2,) + b.shape, BF) for b in bundles]
        + [pltpu.VMEM((part, 2 * b.shape[1]), BF) for b in bundles[:2]]
        + [pltpu.SemaphoreType.DMA((96,)), pltpu.SemaphoreType.DMA((96,)), pltpu.SemaphoreType.DMA((16,))],
        compiler_params=pltpu.CompilerParams(collective_id=0, has_side_effects=True, vmem_limit_bytes=VMEM_LIMIT),
        name="start_gather",
    )(gains, inputs, encoder, cotangent, targets, *bundles)


def rows_kernel(n_ref, n_all, sends, arrivals, local):
    me = Peers()
    meet([me.z[1], me.z[3], me.core])
    rows = n_ref.shape[0]
    copy = pltpu.make_async_copy(n_ref, n_all.at[pl.ds((me.c * 4 + me.t) * rows, rows)], local)
    copy.start()
    line = RowLine(Pool(sends, arrivals), me, n_ref, n_all, rows)
    line.begin()
    for k in range(3):
        line.step(k)
    line.finish()
    copy.wait()


def gather_rows(normed):
    rows, depth = normed.shape
    return pl.pallas_call(
        rows_kernel,
        in_specs=[pl.BlockSpec(memory_space=pltpu.VMEM)],
        out_specs=pl.BlockSpec(memory_space=pl.ANY),
        out_shape=jax.ShapeDtypeStruct((8 * rows, depth), normed.dtype),
        scratch_shapes=[pltpu.SemaphoreType.DMA((26,)), pltpu.SemaphoreType.DMA((26,)), pltpu.SemaphoreType.DMA],
        compiler_params=pltpu.CompilerParams(collective_id=1, has_side_effects=True, vmem_limit_bytes=VMEM_LIMIT),
        name="gather_rows",
    )(normed)


def stats_kernel(stats_ref, out_ref, slots, sends, arrivals):
    me = Peers()
    meet(me.group)
    send = Sender(Pool(sends, arrivals))
    here = slots.at[me.c * 4 + me.t]
    slots[me.c * 4 + me.t] = stats_ref[...]
    copies = [send.to(peer, stats_ref, here) for peer in me.group]
    for copy in copies:
        copy.wait_recv()
    lines = stats_ref.shape[0] // 3
    top = slots[0, 0:lines]
    for i in range(1, 8):
        top = jnp.maximum(top, slots[i, 0:lines])
    total = jnp.zeros_like(top)
    picked = jnp.zeros_like(top)
    for i in range(8):
        total += slots[i, lines : 2 * lines] * jnp.exp(slots[i, 0:lines] - top)
        picked += slots[i, 2 * lines : 3 * lines]
    logsum = top + jnp.log(total)
    out_ref[0] = logsum
    out_ref[1] = logsum - picked
    send.finish()


def combine_stats(stats):
    return pl.pallas_call(
        stats_kernel,
        in_specs=[pl.BlockSpec(memory_space=pltpu.VMEM)],
        out_specs=pl.BlockSpec(memory_space=pltpu.VMEM),
        out_shape=jax.ShapeDtypeStruct((2, stats.shape[0] // 3, stats.shape[1]), F32),
        scratch_shapes=[pltpu.VMEM((8,) + stats.shape, F32), pltpu.SemaphoreType.DMA((8,)), pltpu.SemaphoreType.DMA((8,))],
        compiler_params=pltpu.CompilerParams(collective_id=2, has_side_effects=True),
        name="combine_stats",
    )(stats)


def settle_first(send, me, part_ref, other, half):
    return send.to(me.core, part_ref.at[pl.ds((1 - me.c) * half, half)], other)


def settle_second(me, part_ref, other, summed, rows):
    half = 4 * rows
    for k in range(4):
        summed[k] = (
            part_ref[pl.ds(me.c * half + k * rows, rows)].astype(F32) + other[k * rows : (k + 1) * rows].astype(F32)
        ).astype(BF)


class Planar:
    def __init__(self, send, me, part, first, second, moving, chunks):
        self.send, self.me, self.part = send, me, part
        self.first, self.second, self.moving, self.chunks = first, second, moving, chunks

    def begin(self):
        me = self.me
        self.one = []
        for start, stop, along_x in self.chunks:
            here = slice(start, stop)
            near, near_block = (me.x, me.sx) if along_x else (me.y, me.sy)
            self.one.append(
                (
                    self.send.to(near, self.part.at[me.sd, here], self.first.at[1, here]),
                    self.send.to(near, self.part.at[near_block, here], self.first.at[0, here]),
                )
            )

    def gather(self, i):
        me = self.me
        start, stop, along_x = self.chunks[i]
        here = slice(start, stop)
        self.one[i][0].wait_recv()
        self.moving[here] = (
            self.part[me.sy if along_x else me.sx, here].astype(F32) + self.first[1, here].astype(F32)
        ).astype(BF)
        return here

    def own(self, i):
        start, stop, along_x = self.chunks[i]
        here = slice(start, stop)
        self.one[i][1].wait_recv()
        return self.part[self.me.s, here].astype(F32) + self.first[0, here].astype(F32)

    def go_on(self):
        self.two = []
        for start, stop, along_x in self.chunks:
            here = slice(start, stop)
            self.two.append(
                self.send.to(self.me.y if along_x else self.me.x, self.moving.at[here], self.second.at[here])
            )

    def middle(self):
        for i in range(len(self.chunks)):
            self.gather(i)
        self.go_on()

    def end(self, store):
        for i, copy in enumerate(self.two):
            start, stop, along_x = self.chunks[i]
            here = slice(start, stop)
            copy.wait_recv()
            store(here, self.own(i) + self.second[here].astype(F32))


def halves(count, parts, step):
    middle = (count // 2 + step - 1) // step * step
    out = []
    for low, high, along_x in ((0, middle, True), (middle, count, False)):
        size = ((high - low) // parts + step - 1) // step * step
        edges = list(range(low, high, size)) + [high]
        out.append([(a, b, along_x) for a, b in zip(edges[:-1], edges[1:])])
    return [chunk for pair in zip(*out) for chunk in pair]


def middle_kernel(dn_ref, de_ref, gn_ref, own_ref, move_ref, other, summed, coming, going, total, first, sends, arrivals, *, chunks):
    me = Peers()
    meet([me.z[1], me.z[3], me.core, me.x, me.y])
    pool = Pool(sends, arrivals)
    send = Sender(pool)
    rows = summed.shape[1]
    crossing = settle_first(send, me, dn_ref, other, 4 * rows)
    plane = Planar(send, me, de_ref, first, None, move_ref, chunks)
    crossing.wait_recv()
    settle_second(me, dn_ref, other, summed, rows)
    line = SumLine(pool, me, summed, coming, going)
    line.start()
    plane.begin()
    for part in range(3):
        line.add(part)
    line.result(total)
    own = pl.ds(me.c * rows, rows)
    gn_ref[own] = total[...].astype(BF)
    share = send.to(me.core, gn_ref.at[own], gn_ref.at[own])
    for i in range(len(chunks)):
        here = plane.gather(i)
        own_ref[here] = plane.own(i).astype(BF)
    share.wait_recv()
    line.finish()
    send.finish()


def middle_scatter(dn, de):
    total, depth = dn.shape
    rows = total // 8
    groups, part, wide = de.shape
    chunks = halves(part, 3, 16)
    count = 14 + 2 * len(chunks)
    vmem = pl.BlockSpec(memory_space=pltpu.VMEM)
    return pl.pallas_call(
        partial(middle_kernel, chunks=chunks),
        in_specs=[vmem] * 2,
        out_specs=[vmem] * 3,
        out_shape=[
            jax.ShapeDtypeStruct((2 * rows, depth), BF),
            jax.ShapeDtypeStruct((part, wide), BF),
            jax.ShapeDtypeStruct((part, wide), BF),
        ],
        scratch_shapes=[
            pltpu.VMEM((4 * rows, depth), BF),
            pltpu.VMEM((4, rows, depth), BF),
            pltpu.VMEM((6, rows, depth), BF),
            pltpu.VMEM((6, rows, depth), BF),
            pltpu.VMEM((rows, depth), F32),
            pltpu.VMEM((2, part, wide), BF),
            pltpu.SemaphoreType.DMA((count,)),
            pltpu.SemaphoreType.DMA((count,)),
        ],
        compiler_params=pltpu.CompilerParams(collective_id=3, has_side_effects=True, vmem_limit_bytes=VMEM_LIMIT),
        name="middle_scatter",
    )(dn, de)


def tail_kernel(
    dn_ref, c0, c1, c2, c3, s0, s1, s2, s3, f_ref, gains_ref, eo_ref, em_ref,
    dn_out, held0, held1, held2, gain_out, e_sum, g0, g1, e_second, other, summed, coming, going, first0, second0, moving0, first1, second1, moving1,
    ab0, ab1, ab2, in0, in1, in2, out0, out1, out2, sum0, sum1, sum2, slots, plane_sum, plane_slots, sends, arrivals, *, cuts, chunks,
):
    me = Peers()
    meet(me.group + [me.x, me.y, me.d])
    pool = Pool(sends, arrivals)
    send = Sender(pool)
    rows = summed.shape[1]
    crossing = settle_first(send, me, dn_ref, other, 4 * rows)
    for i, piece in enumerate((c0, c1, c2, c3)):
        g0[:, :, i * piece.shape[2] : (i + 1) * piece.shape[2]] = piece[...]
    for i, piece in enumerate((s0, s1, s2, s3)):
        g1[:, :, i * piece.shape[2] : (i + 1) * piece.shape[2]] = piece[...]
    planes = [
        Planar(send, me, g0, first0, second0, moving0, chunks),
        Planar(send, me, g1, first1, second1, moving1, chunks),
    ]
    planes[0].begin()
    planes[1].begin()
    slots[me.c * 4 + me.t] = gains_ref[...]
    gain_copies = [send.to(peer, gains_ref, slots.at[me.c * 4 + me.t]) for peer in me.group]

    def split(value, cut):
        return [
            jnp.concatenate([value[:, 2 * a + i * (b - a) : 2 * a + (i + 1) * (b - a)] for a, b in cut], axis=1).astype(BF)
            for i in range(2)
        ]

    ff_line = GradLine(pool, me, ab2, in2, out2, held2)
    lines = [GradLine(pool, me, ab0, in0, out0, held0), GradLine(pool, me, ab1, in1, out1, held1)]
    for i, half in enumerate(split(f_ref[...], cuts[2])):
        ab2[i] = half
    crossing.wait_recv()
    settle_second(me, dn_ref, other, summed, rows)
    row_line = SumLine(pool, me, summed, coming, going)
    ff_line.start()
    row_line.start()
    for part in range(3):
        ff_line.add(part)
        row_line.add(part)
    planes[0].middle()
    planes[1].middle()
    e_copies = [
        send.to(me.y if along_x else me.x, em_ref.at[start:stop], e_second.at[start:stop])
        for start, stop, along_x in halves(eo_ref.shape[0], 1, 16)
    ]
    for copy in gain_copies:
        copy.wait_recv()
    total = slots[0]
    for i in range(1, 8):
        total += slots[i]
    plane_sum[...] = total
    plane_slots[me.s] = total
    plane_copies = [send.to(peer, plane_sum, plane_slots.at[me.s]) for peer in (me.x, me.y, me.d)]
    for plane, cut, ab, line in ((planes[0], cuts[0], ab0, lines[0]), (planes[1], cuts[1], ab1, lines[1])):

        def store(here, value):
            for i, half in enumerate(split(value, cut)):
                ab[i, here] = half

        plane.end(store)
        line.start()
    for part in range(3):
        lines[0].add(part)
        lines[1].add(part)
    row_line.result(dn_out)
    ff_line.settle(sum2)
    for copy in e_copies:
        copy.wait_recv()
    e_sum[me.c] = (eo_ref[...].astype(F32) + e_second[...].astype(F32)).astype(BF)
    e_share = send.to(me.core, e_sum.at[me.c], e_sum.at[me.c])
    for copy in plane_copies:
        copy.wait_recv()
    gain_out[...] = plane_slots[0] + plane_slots[1] + plane_slots[2] + plane_slots[3]
    lines[0].settle(sum0)
    lines[1].settle(sum1)
    for line in (ff_line, lines[0], lines[1]):
        line.finish()
    e_share.wait_recv()
    row_line.finish()
    send.finish()


def tail_scatter(dn, grads, ff, gains, emb_own, emb_move, cuts):
    total, depth = dn.shape
    rows = total // 8
    groups, part, width = grads[0][0].shape
    width *= 4
    chunks = halves(part, 1, 16)
    vmem = pl.BlockSpec(memory_space=pltpu.VMEM)
    widths = [width // 2, width // 2, ff.shape[1] // 2]
    scratch = [
        pltpu.VMEM((groups, part, width), BF),
        pltpu.VMEM((groups, part, width), BF),
        pltpu.VMEM(emb_own.shape, BF),
        pltpu.VMEM((4 * rows, depth), BF),
        pltpu.VMEM((4, rows, depth), BF),
        pltpu.VMEM((6, rows, depth), BF),
        pltpu.VMEM((6, rows, depth), BF),
    ]
    for _ in grads:
        scratch += [pltpu.VMEM((2, part, width), BF), pltpu.VMEM((part, width), BF), pltpu.VMEM((part, width), BF)]
    for count in (2, 4, 4):
        scratch += [pltpu.VMEM((count, part, w), BF) for w in widths]
    scratch += [pltpu.VMEM((part, w), F32) for w in widths]
    scratch += [
        pltpu.VMEM((8,) + gains.shape, F32),
        pltpu.VMEM(gains.shape, F32),
        pltpu.VMEM((4,) + gains.shape, F32),
        pltpu.SemaphoreType.DMA((64,)),
        pltpu.SemaphoreType.DMA((64,)),
    ]
    return pl.pallas_call(
        partial(tail_kernel, cuts=cuts, chunks=chunks),
        in_specs=[vmem] * 13,
        out_specs=[vmem] * 6,
        out_shape=[jax.ShapeDtypeStruct((rows, depth), F32)]
        + [jax.ShapeDtypeStruct((part, w), BF) for w in widths]
        + [jax.ShapeDtypeStruct(gains.shape, F32), jax.ShapeDtypeStruct((2,) + emb_own.shape, BF)],
        scratch_shapes=scratch,
        compiler_params=pltpu.CompilerParams(collective_id=4, has_side_effects=True, vmem_limit_bytes=VMEM_LIMIT),
        name="tail_scatter",
    )(dn, *grads[0], *grads[1], ff, gains, emb_own, emb_move)


def finish_kernel(
    emb_ref, self_ref, cross_ref, ff_ref, x_ref, gh_ref, gn_ref, gain_ref, eg_ref, dx_ref, *outs
):
    half = eg_ref.shape[1] // 2
    for c in range(2):
        eg_ref[:, c * half : (c + 1) * half] = emb_ref[c, :, :half].astype(F32)
    x = x_ref[...].astype(F32)
    inverse = lax.rsqrt(jnp.mean(x * x, axis=-1, keepdims=True) + EPS)
    dx_ref[...] = gh_ref[...] + norm_back(x, inverse, gain_ref[...], gn_ref[...])
    index = 0
    for ref, count in ((self_ref, 4), (cross_ref, 4), (ff_ref, 3)):
        size = ref.shape[1] // count
        for k in range(count):
            outs[index][...] = ref[:, k * size : (k + 1) * size].astype(F32)
            index += 1


def finish(emb, own_self, own_cross, own_ff, x, grad_hidden, gn, gain, vocab):
    part, width = own_self.shape
    shapes = []
    for total, count in ((width, 4), (width, 4), (own_ff.shape[1], 3)):
        shapes += [(part, total // count)] * count
    ins = (emb, own_self, own_cross, own_ff, x, grad_hidden, gn, gain)
    vmem = pl.BlockSpec(memory_space=pltpu.VMEM)
    return pl.pallas_call(
        finish_kernel,
        in_specs=[vmem] * len(ins),
        out_specs=[vmem] * (2 + len(shapes)),
        out_shape=[jax.ShapeDtypeStruct((part, vocab), F32), jax.ShapeDtypeStruct(x.shape, F32)]
        + [jax.ShapeDtypeStruct(shape, F32) for shape in shapes],
        compiler_params=pltpu.CompilerParams(vmem_limit_bytes=VMEM_LIMIT),
        name="finish",
    )(*ins)


def normalize(hidden, gain):
    inverse = lax.rsqrt(jnp.mean(hidden * hidden, axis=-1, keepdims=True) + EPS)
    return (hidden * inverse * gain, inverse)


def norm_back(hidden, inverse, gain, upstream):
    scaled = upstream * gain
    inner = jnp.mean(scaled * hidden, axis=-1, keepdims=True)
    return inverse * scaled - hidden * (inverse * inverse * inverse) * inner


def matmul(left, right):
    return jnp.dot(left, right, preferred_element_type=F32)


def left_t(left, right):
    return jnp.einsum("ra,rb->ab", left, right, preferred_element_type=F32)


def right_t(left, right):
    return jnp.einsum("ra,ba->rb", left, right, preferred_element_type=F32)


def swap(array):
    return lax.ppermute(array, "ctx", [(0, 1), (1, 0)])


def per_device(
    inputs, encoder, prefix, targets, cotangent, gain_self, query_self, key_self, value_self, output_self,
    gain_cross, query_cross, key_cross, value_cross, output_cross, gain_hidden, gate_weight, up_weight,
    down_weight, gain_exit, embedding,
):
    tp = lax.axis_size("tp")
    ctx = lax.axis_size("ctx")
    shards = lax.axis_size("shard")
    assert tp == 4 and ctx == 2
    core = lax.axis_index("ctx")
    place = lax.axis_index("tp")
    rows, depth = inputs.shape
    group = rows * tp
    total = group * ctx
    hb = query_self.shape[1]
    width = 2 * hb
    fb = gate_weight.shape[1]
    pair = rows * ctx

    route_a = []
    route_b = []
    for c in range(2):
        for z in range(4):
            dest = c * 4 + z
            route_a.append(((z % 2) * 4 + 2 * c + z // 2, dest))
            route_b.append(((z % 2) * 4 + 2 * c + 1 - z // 2, dest))
    both = ("ctx", "tp")

    def spread_weights(parts):
        block = jnp.concatenate(parts, axis=1)
        first = lax.ppermute(block, both, route_a)
        second = lax.ppermute(block, both, route_b)
        columns = []
        start = 0
        for piece in parts:
            stop = start + piece.shape[1]
            columns += [first[:, start:stop], second[:, start:stop]]
            start = stop
        return lax.all_gather(jnp.concatenate(columns, axis=1), "shard", axis=0, tiled=True)

    def collect_weights(grad, widths):
        mine = lax.psum_scatter(grad, "shard", scatter_dimension=0, tiled=True)
        first = []
        second = []
        start = 0
        for size in widths:
            first.append(mine[:, start : start + size])
            second.append(mine[:, start + size : start + 2 * size])
            start += 2 * size
        back = lambda route: [(dest, source) for source, dest in route]
        one = lax.ppermute(jnp.concatenate(first, axis=1), both, back(route_a))
        two = lax.ppermute(jnp.concatenate(second, axis=1), both, back(route_b))
        part = (one.astype(F32) + two.astype(F32)).astype(BF)
        whole = part.astype(F32) + swap(part).astype(F32)
        outs = []
        start = 0
        for size in widths:
            outs.append(whole[:, start : start + size])
            start += size
        return outs

    def couple(own, other):
        return jnp.where(
            core == 0, jnp.concatenate([own, other], axis=0), jnp.concatenate([other, own], axis=0)
        )

    fast = shards == 4
    own_f = inputs.astype(F32)
    parts_self = [query_self, key_self, value_self, output_self.T]
    parts_cross = [query_cross, key_cross, value_cross, output_cross.T]
    parts_ff = [gate_weight, up_weight, down_weight.T]
    gain_parts = jnp.stack([gain_self, gain_cross, gain_hidden, gain_exit])
    cuts = [[(i * w, (i + 1) * w) for i in range(n)] for n, w in ((4, hb), (4, hb), (3, fb))]
    vocab_half = embedding.shape[0] // ctx
    vblock, rblock = 512, 512
    emb_mine = lax.dynamic_slice_in_dim(embedding.T, core * vocab_half, vocab_half, axis=1)
    emb_mine = jnp.pad(emb_mine, ((0, 0), (0, -vocab_half % vblock)))
    emb_t = lax.all_gather(emb_mine, "shard", axis=0, tiled=True)

    def take_pair(array):
        cut = array.reshape(ctx, group, depth)
        return lax.dynamic_slice_in_dim(cut, place * rows, rows, axis=1).reshape(pair, depth)

    if fast:
        bundles = [jnp.concatenate(parts, axis=1) for parts in (parts_self, parts_cross, parts_ff)]
        spare = -(depth // shards) % 128
        gain_block = jnp.pad(gain_parts.astype(F32), ((0, 4), (0, spare)))
        (
            gains, normed1, encoder_all, normed1_pair, x_pair, g_pair, t_pair, weights_self, weights_cross, ff_mix,
        ) = start_gather(
            gain_block, inputs, encoder, cotangent, targets.reshape(8, group // 8), bundles, cuts
        )
        hidden0 = x_pair.astype(F32)
        cotangent_pair = g_pair.astype(F32)
        targets_all = t_pair.reshape(total)
        ff_mix, emb_t = lax.optimization_barrier((ff_mix, emb_t))
        weights_ff = lax.all_gather(ff_mix, "shard", axis=0, tiled=True)
    else:
        gains = lax.all_gather(gain_parts, "shard", axis=1, tiled=True).astype(F32)
        normed1_own = normalize(own_f, gains[0])[0].astype(BF)
        normed1 = lax.all_gather(normed1_own, both, axis=0, tiled=True)
        normed1_pair = take_pair(normed1)
        encoder_all = lax.all_gather(encoder, both, axis=0, tiled=True)
        weights_self, weights_cross, weights_ff = map(spread_weights, (parts_self, parts_cross, parts_ff))
        hidden0 = couple(inputs, swap(inputs)).astype(F32)
        cotangent_pair = couple(cotangent, swap(cotangent)).astype(F32)
        targets_all = couple(targets, swap(targets))

    gain_one, gain_two, gain_three, gain_four = [gains[i] for i in range(4)]
    inverse1_own = normalize(own_f, gain_one)[1]
    query_w, key_w, value_w, out_w = [weights_self[:, i * width : (i + 1) * width] for i in range(4)]
    scale = HEAD_DIM**-0.5

    def project_q(normed, weight):
        return matmul(normed, weight).astype(BF) * jnp.asarray(scale, BF)

    positions = jnp.concatenate(
        [c * group + place * rows + jnp.arange(rows, dtype=jnp.int32) for c in range(2)]
    )
    limit = prefix[0]
    seen = jnp.maximum(positions + 1, limit)[None, :]
    causal_tiles = (((0, pair), (0, group), True), ((rows, pair), (group, total), True))
    open_tiles = (((0, pair), (0, total), False),)

    query1 = project_q(normed1_pair, query_w)
    kv1 = matmul(normed1, weights_self[:, width : 3 * width]).astype(BF)
    attended1, attended1_t, lse1 = attend(seen, query1, kv1, causal_tiles)

    def add_halves(partial_sum):
        part = partial_sum.astype(BF)
        return partial_sum + swap(part).astype(F32)

    hidden1 = hidden0 + add_halves(right_t(attended1, out_w))
    query2_w, key2_w, value2_w, out2_w = [weights_cross[:, i * width : (i + 1) * width] for i in range(4)]
    kv2 = matmul(encoder_all, weights_cross[:, width : 3 * width]).astype(BF)
    normed2, inverse2 = normalize(hidden1, gain_two)
    normed2 = normed2.astype(BF)
    query2 = project_q(normed2, query2_w)
    attended2, attended2_t, lse2 = attend(seen, query2, kv2, open_tiles)
    hidden2 = hidden1 + add_halves(right_t(attended2, out2_w))
    normed3, inverse3 = normalize(hidden2, gain_three)
    normed3 = normed3.astype(BF)
    gate_w, up_w, down_w = [weights_ff[:, i * 2 * fb : (i + 1) * 2 * fb] for i in range(3)]
    gate = matmul(normed3, gate_w)
    upper = matmul(normed3, up_w)
    active = jax.nn.gelu(gate, approximate=True)
    product = (active * upper).astype(BF)
    final = hidden2 + add_halves(right_t(product, down_w))
    normed4, inverse4 = normalize(final, gain_four)
    normed4 = normed4.astype(BF)

    def mine(array):
        return lax.dynamic_slice_in_dim(array, core * rows, rows, axis=0)

    final_own = mine(final)
    if fast:
        normed4_all = gather_rows(mine(normed4))
    else:
        normed4_all = lax.all_gather(mine(normed4), both, axis=0, tiled=True)
    local_target = (targets_all - (place * embedding.shape[0] + core * vocab_half))[None, :].astype(jnp.int32)
    stats, expo, tops = head_stats(emb_t, normed4_all, local_target, vocab_half, vblock, rblock)
    if fast:
        combined = combine_stats(stats)
        logsum = combined[0].reshape(total)
        loss = combined[1].reshape(total)
    else:
        every = lax.all_gather(stats.reshape(3, total), both, axis=0)
        top = jnp.max(every[:, 0], axis=0)
        summed = jnp.sum(every[:, 1] * jnp.exp(every[:, 0] - top[None]), axis=0)
        logsum = top + jnp.log(summed)
        loss = logsum - jnp.sum(every[:, 2], axis=0)
    exit_loss = lax.dynamic_slice_in_dim(loss, core * group, group, axis=0)
    emb_grad, grad_normed4 = head_back(
        emb_t, expo, tops, normed4_all, local_target, logsum[None, :], vocab_half, vblock, rblock
    )
    if fast:
        gn4, emb_own, emb_move = middle_scatter(grad_normed4, emb_grad.reshape(shards, depth // shards, -1))
        gn4 = gn4.astype(F32)
    else:
        emb_sum = lax.psum_scatter(emb_grad, "shard", scatter_dimension=0, tiled=True)
        emb_other = swap(emb_sum)
        gn4_own = lax.psum_scatter(grad_normed4, both, scatter_dimension=0, tiled=True)
        gn4 = couple(gn4_own, swap(gn4_own)).astype(F32)
    gain4_rows = gn4 * final * inverse4
    grad_final = cotangent_pair + norm_back(final, inverse4, gain_four, gn4)
    grad_final_b = grad_final.astype(BF)
    down_grad = left_t(grad_final_b, product).astype(BF)
    grad_product = matmul(grad_final_b, down_w)
    unused, gelu_pull = jax.vjp(partial(jax.nn.gelu, approximate=True), gate)
    grad_gate = gelu_pull(grad_product * upper)[0].astype(BF)
    grad_upper = (grad_product * active).astype(BF)
    gate_grad = left_t(normed3, grad_gate).astype(BF)
    upper_grad = left_t(normed3, grad_upper).astype(BF)
    ff_part = jnp.concatenate([gate_grad, upper_grad, down_grad], axis=1)
    gn3 = add_halves(right_t(grad_gate, gate_w) + right_t(grad_upper, up_w))
    gain3_rows = gn3 * hidden2 * inverse3
    grad_hidden2 = grad_final + norm_back(hidden2, inverse3, gain_three, gn3)
    grad_hidden2_b = grad_hidden2.astype(BF)
    out2_grad = left_t(grad_hidden2_b, attended2).astype(BF)
    grad_attended2 = matmul(grad_hidden2_b, out2_w).astype(BF)
    if fast:
        ff_mine = lax.psum_scatter(ff_part, "shard", scatter_dimension=0, tiled=True)
    grad_query2, grad_key2, grad_value2 = attend_back(
        seen, query2, kv2, grad_attended2, attended2_t, lse2, open_tiles
    )
    query2_grad = left_t(normed2, grad_query2).astype(BF)
    key2_grad = left_t(encoder_all, grad_key2).astype(BF)
    value2_grad = left_t(encoder_all, grad_value2).astype(BF)
    cross_parts = [query2_grad, key2_grad, value2_grad, out2_grad]
    encoder_part = (right_t(grad_key2, key2_w) + right_t(grad_value2, value2_w)).astype(BF)
    if fast:
        encoder_part, ff_mine = lax.optimization_barrier((encoder_part, ff_mine))
    encoder_grad = lax.psum_scatter(encoder_part, both, scatter_dimension=0, tiled=True).astype(F32)
    gn2 = add_halves(right_t(grad_query2, query2_w))
    gain2_rows = gn2 * hidden1 * inverse2
    grad_hidden1 = grad_hidden2 + norm_back(hidden1, inverse2, gain_two, gn2)
    grad_hidden1_b = grad_hidden1.astype(BF)
    out_grad = left_t(grad_hidden1_b, attended1).astype(BF)
    grad_attended1 = matmul(grad_hidden1_b, out_w).astype(BF)
    grad_query1, grad_key1, grad_value1 = attend_back(
        seen, query1, kv1, grad_attended1, attended1_t, lse1, causal_tiles
    )
    query_grad = left_t(normed1_pair, grad_query1).astype(BF)
    key_grad = left_t(normed1, grad_key1).astype(BF)
    value_grad = left_t(normed1, grad_value1).astype(BF)
    self_parts = [query_grad, key_grad, value_grad, out_grad]
    normed1_part = right_t(grad_key1, key_w) + right_t(grad_value1, value_w)
    query_part = right_t(grad_query1, query_w).reshape(ctx, rows, depth)
    cut = normed1_part.reshape(ctx, group, depth)
    old = lax.dynamic_slice_in_dim(cut, place * rows, rows, axis=1)
    cut = lax.dynamic_update_slice_in_dim(cut, old + query_part, place * rows, axis=1)
    cut = cut.reshape(total, depth).astype(BF)

    def gain_rows(gn1):
        gain1_sum = jnp.sum(gn1 * own_f * inverse1_own, axis=0)
        return jnp.stack(
            [gain1_sum] + [jnp.sum(mine(a), axis=0) for a in (gain2_rows, gain3_rows, gain4_rows)]
        )

    if fast:
        blocks = [
            [a.reshape(shards, depth // shards, a.shape[1]) for a in parts] for parts in (cross_parts, self_parts)
        ]
        gain1_part = jnp.sum(cut.astype(F32) * normed1.astype(F32), axis=0) / gain_one
        gains_part = [gain1_part] + [jnp.sum(mine(a), axis=0) for a in (gain2_rows, gain3_rows, gain4_rows)]
        gain_pad = jnp.stack(gains_part + [jnp.zeros_like(gain1_part)] * 4)
        gn1, cross_own, self_own, ff_own, gain_sums, emb_sums = tail_scatter(
            cut, blocks, ff_mine, gain_pad, emb_own, emb_move, [cuts[1], cuts[0], cuts[2]]
        )
        embedding_grad, inputs_grad, *weight_grads = finish(
            emb_sums, self_own, cross_own, ff_own, inputs, mine(grad_hidden1), gn1, gain_one[None],
            embedding.shape[0],
        )
    else:
        emb_halves = [jnp.where(core == 0, a, b)[:, :vocab_half] for a, b in ((emb_sum, emb_other), (emb_other, emb_sum))]
        embedding_grad = jnp.concatenate(emb_halves, axis=1).astype(F32)
        gn1 = lax.psum_scatter(cut, both, scatter_dimension=0, tiled=True).astype(F32)
        ff_grads = collect_weights(ff_part, [fb, fb, fb])
        cross_grads = collect_weights(jnp.concatenate(cross_parts, axis=1), [hb] * 4)
        self_grads = collect_weights(jnp.concatenate(self_parts, axis=1), [hb] * 4)
        gain_sums = lax.psum(gain_rows(gn1), ("shard", "ctx", "tp"))
        inputs_grad = mine(grad_hidden1) + norm_back(own_f, inverse1_own, gain_one, gn1)
        weight_grads = []
        for grads in (self_grads, cross_grads, ff_grads):
            weight_grads += grads
    part = depth // shards
    gain_grads = lax.dynamic_slice_in_dim(gain_sums, lax.axis_index("shard") * part, part, axis=1)
    return (
        final_own.astype(BF), exit_loss, inputs_grad, encoder_grad,
        gain_grads[0], *weight_grads[:3], weight_grads[3].T, gain_grads[1], *weight_grads[4:7], weight_grads[7].T,
        gain_grads[2], *weight_grads[8:10], weight_grads[10].T, gain_grads[3], embedding_grad.T,
    )


def solution(mesh):
    rows = P(("shard", "ctx", "tp"), None)
    into = P("shard", "tp")
    out = P("tp", "shard")
    gain = P("shard")
    weights = (gain, into, into, into, out, gain, into, into, into, out, gain, into, into, out, gain, out)
    return jax.shard_map(
        per_device,
        mesh=mesh,
        in_specs=(rows, rows, P("shard"), P(("shard", "ctx")), rows) + weights,
        out_specs=(rows, P(("shard", "ctx")), rows, rows) + weights,
        check_vma=False,
    )
```

```python
from functools import partial

import jax
import jax.numpy as jnp
from jax import lax
from jax.experimental import pallas as pl
from jax.experimental.pallas import tpu as pltpu
from jax.sharding import PartitionSpec as P

HEAD_DIM = 64
EPS = 1e-06
MASKED = -1e30
BF = jnp.bfloat16
F32 = jnp.float32
VMEM_LIMIT = 58 * 2**20


def attend_kernel(seen_ref, q_ref, k_ref, v_ref, o_ref, ot_ref, lse_ref, vt_ref, *, tiles):
    half = lax.broadcasted_iota(jnp.int32, (2 * HEAD_DIM, 1), 0) // HEAD_DIM
    vt_ref[...] = jnp.transpose(v_ref[...])
    q_t = jnp.transpose(q_ref[...])
    for head in range(2):
        part = slice(head * HEAD_DIM, (head + 1) * HEAD_DIM)
        state = None
        for rows, keys, masked in tiles:
            qt = jnp.where(half == head, q_t[:, rows[0] : rows[1]], 0).astype(BF)
            scores = jnp.dot(k_ref[keys[0] : keys[1], :], qt, preferred_element_type=F32)
            if masked:
                key = lax.broadcasted_iota(jnp.int32, (keys[1] - keys[0], 1), 0) + keys[0]
                scores = jnp.where(key < seen_ref[:, rows[0] : rows[1]], scores, MASKED)
            top = jnp.max(scores, axis=0, keepdims=True)
            if state is not None:
                base, old_top, old_total, old_acc = state
                cut = slice(rows[0] - base, rows[1] - base)
                top = jnp.maximum(top, old_top[:, cut])
                shrink = jnp.exp(old_top[:, cut] - top)
            expo = jnp.exp(scores - top)
            total = jnp.sum(expo, axis=0, keepdims=True)
            acc = jnp.dot(vt_ref[part, keys[0] : keys[1]], expo.astype(BF), preferred_element_type=F32)
            if state is not None:
                total += old_total[:, cut] * shrink
                acc += old_acc[:, cut] * shrink
            state = (rows[0], top, total, acc)
            ot_ref[part, rows[0] : rows[1]] = acc / total
            lse_ref[0, head : head + 1, rows[0] : rows[1]] = top + jnp.log(total)
    o_ref[...] = jnp.transpose(ot_ref[...]).astype(BF)


def attend(seen, query, kv, tiles):
    rows, width = query.shape
    count = kv.shape[0]
    pair = 2 * HEAD_DIM
    pairs = width // pair
    return pl.pallas_call(
        partial(attend_kernel, tiles=tiles),
        grid=(pairs,),
        in_specs=[
            pl.BlockSpec((1, rows), lambda p: (0, 0)),
            pl.BlockSpec((rows, pair), lambda p: (0, p)),
            pl.BlockSpec((count, pair), lambda p: (0, p)),
            pl.BlockSpec((count, pair), lambda p: (0, p + pairs)),
        ],
        out_specs=[
            pl.BlockSpec((rows, pair), lambda p: (0, p)),
            pl.BlockSpec((pair, rows), lambda p: (p, 0)),
            pl.BlockSpec((1, 8, rows), lambda p: (p, 0, 0)),
        ],
        scratch_shapes=[pltpu.VMEM((pair, count), BF)],
        out_shape=(
            jax.ShapeDtypeStruct((rows, width), BF),
            jax.ShapeDtypeStruct((width, rows), F32),
            jax.ShapeDtypeStruct((pairs, 8, rows), F32),
        ),
        compiler_params=pltpu.CompilerParams(vmem_limit_bytes=VMEM_LIMIT),
        cost_estimate=pl.CostEstimate(
            flops=4 * rows * count * width, transcendentals=rows * count * width // HEAD_DIM,
            bytes_accessed=2 * count * width * 2 + 8 * rows * width,
        ),
        name="attend",
    )(seen, query, kv, kv)


def attend_back_kernel(
    seen_ref, q_ref, k_ref, v_ref, do_ref, ot_ref, lse_ref, dq_ref, dk_ref, dv_ref, dk_acc, dv_acc, dqt_acc, kt_ref, *, tiles
):
    half = lax.broadcasted_iota(jnp.int32, (2 * HEAD_DIM, 1), 0) // HEAD_DIM
    lane = lax.broadcasted_iota(jnp.int32, (1, 2 * HEAD_DIM), 1) // HEAD_DIM
    kt_ref[...] = jnp.transpose(k_ref[...])
    q_t = jnp.transpose(q_ref[...])
    do_t = jnp.transpose(do_ref[...])
    dqt_acc[...] = jnp.zeros_like(dqt_acc)
    done = []
    for head in range(2):
        part = slice(head * HEAD_DIM, (head + 1) * HEAD_DIM)
        inner_all = jnp.sum(do_t[part].astype(F32) * ot_ref[part], axis=0, keepdims=True)
        for rows, keys, masked in tiles:
            cut = slice(rows[0], rows[1])
            here = slice(keys[0], keys[1])
            qt = jnp.where(half == head, q_t[:, cut], 0).astype(BF)
            dot_t = jnp.where(half == head, do_t[:, cut], 0).astype(BF)
            q = jnp.where(lane == head, q_ref[cut, :], 0).astype(BF)
            do = jnp.where(lane == head, do_ref[cut, :], 0).astype(BF)
            scores = jnp.dot(k_ref[here, :], qt, preferred_element_type=F32)
            probs = jnp.exp(scores - lse_ref[0, head : head + 1, cut])
            if masked:
                key = lax.broadcasted_iota(jnp.int32, (keys[1] - keys[0], 1), 0) + keys[0]
                probs = jnp.where(key < seen_ref[:, cut], probs, 0.0)
            grad_probs = jnp.dot(v_ref[here, :], dot_t, preferred_element_type=F32)
            grad_scores = (probs * (grad_probs - inner_all[:, cut])).astype(BF)
            dv = jnp.dot(probs.astype(BF), do, preferred_element_type=F32)
            dk = jnp.dot(grad_scores, q, preferred_element_type=F32)
            if keys in done:
                dv_acc[here, :] += dv
                dk_acc[here, :] += dk
            else:
                dv_acc[here, :] = dv
                dk_acc[here, :] = dk
                done.append(keys)
            dqt_acc[part, cut] += jnp.dot(kt_ref[part, here], grad_scores, preferred_element_type=F32)
    dq_ref[...] = jnp.transpose(dqt_acc[...] * HEAD_DIM**-0.5).astype(BF)
    dk_ref[...] = dk_acc[...].astype(BF)
    dv_ref[...] = dv_acc[...].astype(BF)


def attend_back(seen, query, kv, grad, out_t, lse, tiles):
    rows, width = query.shape
    count = kv.shape[0]
    pair = 2 * HEAD_DIM
    pairs = width // pair
    by_column = pl.BlockSpec((rows, pair), lambda p: (0, p))
    key_spec = pl.BlockSpec((count, pair), lambda p: (0, p))
    return pl.pallas_call(
        partial(attend_back_kernel, tiles=tiles),
        grid=(pairs,),
        in_specs=[
            pl.BlockSpec((1, rows), lambda p: (0, 0)),
            by_column,
            key_spec,
            pl.BlockSpec((count, pair), lambda p: (0, p + pairs)),
            by_column,
            pl.BlockSpec((pair, rows), lambda p: (p, 0)),
            pl.BlockSpec((1, 8, rows), lambda p: (p, 0, 0)),
        ],
        out_specs=[by_column, key_spec, key_spec],
        scratch_shapes=[
            pltpu.VMEM((count, pair), F32),
            pltpu.VMEM((count, pair), F32),
            pltpu.VMEM((pair, rows), F32),
            pltpu.VMEM((pair, count), BF),
        ],
        out_shape=(
            jax.ShapeDtypeStruct((rows, width), BF),
            jax.ShapeDtypeStruct((count, width), BF),
            jax.ShapeDtypeStruct((count, width), BF),
        ),
        compiler_params=pltpu.CompilerParams(vmem_limit_bytes=VMEM_LIMIT),
        cost_estimate=pl.CostEstimate(
            flops=10 * rows * count * width, transcendentals=rows * count * width // HEAD_DIM,
            bytes_accessed=5 * count * width * 2 + 14 * rows * width,
        ),
        name="attend_back",
    )(seen, query, kv, kv, grad, out_t, lse)


def vocab_ids(step, block, vocab):
    ids = lax.broadcasted_iota(jnp.int32, (block, 1), 0) + step * block
    valid = ids < vocab
    return jnp.where(valid, ids, 2**30), valid


def head_stats_kernel(emb_ref, n_ref, target_ref, stats_ref, expo_ref, tops_ref, nt_ref, run_ref, *, vocab, block, rows, scale):
    step = pl.program_id(0)
    ids, valid = vocab_ids(step, block, vocab)
    emb = jnp.transpose(emb_ref[...])
    total = n_ref.shape[0]

    @pl.when(step == 0)
    def _():
        run_ref[0:1, :] = jnp.full((1, total), MASKED, F32)
        run_ref[1:8, :] = jnp.zeros((7, total), F32)
        for first in range(0, total, rows):
            nt_ref[:, first : first + rows] = jnp.transpose(n_ref[first : first + rows, :])

    for first in range(0, total, rows):
        columns = slice(first, first + rows)
        logits = jnp.dot(emb, nt_ref[:, columns], preferred_element_type=F32) * scale
        logits = jnp.where(valid, logits, MASKED)
        top = run_ref[0:1, columns]
        new_top = jnp.maximum(top, jnp.max(logits, axis=0, keepdims=True))
        expo = jnp.exp(logits - new_top)
        expo_ref[:, columns] = expo.astype(BF)
        run_ref[0:1, columns] = new_top
        run_ref[1:2, columns] = run_ref[1:2, columns] * jnp.exp(top - new_top) + jnp.sum(expo, axis=0, keepdims=True)
        run_ref[2:3, columns] += jnp.sum(jnp.where(ids == target_ref[:, columns], logits, 0.0), axis=0, keepdims=True)
    tops_ref[pl.ds(step, 1), :] = run_ref[0:1, :]

    @pl.when(step == pl.num_programs(0) - 1)
    def _():
        lines = total // 128
        for k in range(3):
            for i in range(lines):
                stats_ref[k * lines + i : k * lines + i + 1, :] = run_ref[k : k + 1, i * 128 : (i + 1) * 128]


def head_stats(emb_t, normed, target, vocab, block, rows):
    total, depth = normed.shape
    steps = emb_t.shape[1] // block
    lines = (steps + 7) // 8 * 8
    return pl.pallas_call(
        partial(head_stats_kernel, vocab=vocab, block=block, rows=rows, scale=depth**-0.5),
        grid=(steps,),
        in_specs=[
            pl.BlockSpec((depth, block), lambda i: (0, i)),
            pl.BlockSpec((total, depth), lambda i: (0, 0)),
            pl.BlockSpec((1, total), lambda i: (0, 0)),
        ],
        out_specs=[
            pl.BlockSpec((3 * total // 128, 128), lambda i: (0, 0)),
            pl.BlockSpec((block, total), lambda i: (i, 0)),
            pl.BlockSpec((lines, total), lambda i: (0, 0)),
        ],
        out_shape=(
            jax.ShapeDtypeStruct((3 * total // 128, 128), F32),
            jax.ShapeDtypeStruct((steps * block, total), BF),
            jax.ShapeDtypeStruct((lines, total), F32),
        ),
        scratch_shapes=[pltpu.VMEM((depth, total), BF), pltpu.VMEM((8, total), F32)],
        compiler_params=pltpu.CompilerParams(vmem_limit_bytes=VMEM_LIMIT),
        cost_estimate=pl.CostEstimate(
            flops=2 * vocab * depth * total, transcendentals=vocab * total,
            bytes_accessed=2 * vocab * depth + 2 * depth * total + 2 * vocab * total,
        ),
        name="head_stats",
    )(emb_t, normed, target)


def head_back_kernel(
    emb_ref, expo_ref, tops_ref, n_ref, target_ref, lse_ref, de_ref, dn_ref, dnt_acc, *, vocab, block, rows, scale
):
    step = pl.program_id(0)
    ids, valid = vocab_ids(step, block, vocab)
    factor = jnp.exp(tops_ref[pl.ds(step, 1), :] - lse_ref[...])

    @pl.when(step == 0)
    def _():
        dnt_acc[...] = jnp.zeros_like(dnt_acc)

    de = None
    for first in range(0, n_ref.shape[0], rows):
        columns = slice(first, first + rows)
        probs = expo_ref[:, columns].astype(F32) * factor[:, columns]
        grad = jnp.where(ids == target_ref[:, columns], probs - 1.0, probs).astype(BF)
        term = jnp.dot(grad, n_ref[columns, :], preferred_element_type=F32)
        de = term if de is None else de + term
        dnt_acc[:, columns] += jnp.dot(emb_ref[...], grad, preferred_element_type=F32)
    de_ref[...] = jnp.transpose((de * scale).astype(BF))

    @pl.when(step == pl.num_programs(0) - 1)
    def _():
        dn_ref[...] = (jnp.transpose(dnt_acc[...]) * scale).astype(BF)


def head_back(emb_t, expo, tops, normed, target, lse, vocab, block, rows):
    total, depth = normed.shape
    steps = emb_t.shape[1] // block
    return pl.pallas_call(
        partial(head_back_kernel, vocab=vocab, block=block, rows=rows, scale=depth**-0.5),
        grid=(steps,),
        in_specs=[
            pl.BlockSpec((depth, block), lambda i: (0, i)),
            pl.BlockSpec((block, total), lambda i: (i, 0)),
            pl.BlockSpec(tops.shape, lambda i: (0, 0)),
            pl.BlockSpec((total, depth), lambda i: (0, 0)),
            pl.BlockSpec((1, total), lambda i: (0, 0)),
            pl.BlockSpec((1, total), lambda i: (0, 0)),
        ],
        out_specs=[
            pl.BlockSpec((depth, block), lambda i: (0, i)),
            pl.BlockSpec((total, depth), lambda i: (0, 0)),
        ],
        out_shape=(
            jax.ShapeDtypeStruct(emb_t.shape, BF),
            jax.ShapeDtypeStruct((total, depth), BF),
        ),
        scratch_shapes=[pltpu.VMEM((depth, total), F32)],
        compiler_params=pltpu.CompilerParams(vmem_limit_bytes=VMEM_LIMIT),
        cost_estimate=pl.CostEstimate(
            flops=4 * vocab * depth * total, transcendentals=0,
            bytes_accessed=4 * vocab * depth + 6 * depth * total + 2 * vocab * total,
        ),
        name="head_back",
    )(emb_t, expo, tops, normed, target, lse)


MESH = pl.DeviceIdType.MESH


class Peers:
    def __init__(self):
        self.s, self.c, self.t = (lax.axis_index(name) for name in ("shard", "ctx", "tp"))
        s, c, t = self.s, self.c, self.t
        self.sx = s + 1 - 2 * lax.rem(s, 2)
        self.sy = lax.rem(s + 2, 4)
        self.sd = lax.rem(self.sx + 2, 4)
        self.x = (self.sx, c, t)
        self.y = (self.sy, c, t)
        self.d = (self.sd, c, t)
        self.core = (s, 1 - c, t)
        self.z = [(s, c, lax.rem(t + k, 4)) for k in range(4)]
        self.z_other = [(s, 1 - c, lax.rem(t + k, 4)) for k in range(4)]
        self.group = self.z[1:] + self.z_other


def meet(peers):
    barrier = pltpu.get_barrier_semaphore()
    for peer in peers:
        pl.semaphore_signal(barrier, inc=1, device_id=peer, device_id_type=MESH)
    pl.semaphore_wait(barrier, len(peers))


class Pool:
    def __init__(self, sends, arrivals):
        self.sends, self.arrivals, self.count = sends, arrivals, 0

    def take(self, count):
        first = self.count
        self.count += count
        return first

    def copy(self, index, peer, source, target):
        return pltpu.make_async_remote_copy(
            src_ref=source, dst_ref=target, send_sem=self.sends.at[index],
            recv_sem=self.arrivals.at[index], device_id=peer, device_id_type=MESH,
        )


class Sender:
    def __init__(self, pool):
        self.pool, self.all = pool, []

    def to(self, peer, source, target):
        copy = self.pool.copy(self.pool.take(1), peer, source, target)
        self.all.append(copy)
        copy.start()
        return copy

    def finish(self):
        for copy in self.all:
            copy.wait_send()


class RowLine:
    def __init__(self, pool, me, own, everyone, rows, pieces=2):
        self.pool, self.me, self.own, self.everyone = pool, me, own, everyone
        self.rows, self.pieces, self.sub = rows, pieces, rows // pieces
        self.first = pool.take(13 * pieces)

    def block(self, chip, piece):
        return self.everyone.at[pl.ds((self.me.c * 4 + chip) * self.rows + piece * self.sub, self.sub)]

    def source(self, own, chip, piece):
        return self.own.at[pl.ds(piece * self.sub, self.sub)] if own else self.block(chip, piece)

    def make(self, slot, piece, peer, chip, own=False):
        index = self.first + slot * self.pieces + piece
        return self.pool.copy(index, peer, self.source(own, chip, piece), self.block(chip, piece))

    def right(self, k, piece):
        return self.make(k, piece, self.me.z[1], self.me.t - k, k == 0)

    def left(self, k, piece):
        return self.make(3 + k, piece, self.me.z[3], self.me.t + k, k == 0)

    def across(self, slot, piece, chip, own=False):
        return self.make(6 + slot, piece, self.me.core, chip, own)

    def begin(self):
        t = self.me.t
        for p in range(self.pieces):
            pl.when(t < 3)(lambda: self.right(0, p).start())
            pl.when(t > 0)(lambda: self.left(0, p).start())
        for p in range(self.pieces):
            self.across(0, p, t, True).start()

    def step(self, k):
        t = self.me.t
        for p in range(self.pieces):

            @pl.when(t > k)
            def _():
                chip = t - 1 - k
                self.make(k, p, self.me.z[1], chip).wait_recv()
                if k < 2:
                    pl.when(t < 3)(lambda: self.right(k + 1, p).start())
                self.across(1 + k, p, chip).start()

            @pl.when(t + k < 3)
            def _():
                chip = t + 1 + k
                self.make(3 + k, p, self.me.z[3], chip).wait_recv()
                if k < 2:
                    pl.when(t > 0)(lambda: self.left(k + 1, p).start())
                self.across(4 + k, p, chip).start()

    def finish(self):
        t = self.me.t
        for p in range(self.pieces):
            pl.when(t < 3)(lambda: self.right(0, p).wait_send())
            pl.when(t > 0)(lambda: self.left(0, p).wait_send())
            self.across(0, p, t, True).wait()
            for k in range(3):

                @pl.when(t > k)
                def _():
                    if k < 2:
                        pl.when(t < 3)(lambda: self.right(k + 1, p).wait_send())
                    self.across(1 + k, p, t - 1 - k).wait()

                @pl.when(t + k < 3)
                def _():
                    if k < 2:
                        pl.when(t > 0)(lambda: self.left(k + 1, p).wait_send())
                    self.across(4 + k, p, t + 1 + k).wait()


class BlockLine:
    def __init__(self, pool, me, own, take, pieces=2):
        self.pool, self.me, self.own, self.take = pool, me, own, take
        self.pieces, self.sub = pieces, own.shape[0] // pieces
        self.first = pool.take(4 * pieces)
        self.where = [(me.c + 1, 1 - me.c), (3 * me.c, me.c)]

    def make(self, lane, i, piece, peer):
        here = self.take.at[self.where[i][1], pl.ds(piece * self.sub, self.sub)]
        return self.pool.copy(self.first + (2 * lane + i) * self.pieces + piece, peer, here, here)

    def right(self, i, piece):
        return self.make(0, i, piece, self.me.z[1])

    def left(self, i, piece):
        return self.make(1, i, piece, self.me.z[3])

    def begin(self):
        t = self.me.t
        for i, (block, slot) in enumerate(self.where):

            @pl.when(t == block)
            def _():
                self.take[slot] = self.own[...]
                for p in range(self.pieces):
                    pl.when(t < 3)(lambda: self.right(i, p).start())
                    pl.when(t > 0)(lambda: self.left(i, p).start())

    def arrive(self, distance):
        t = self.me.t
        for i, (block, slot) in enumerate(self.where):

            @pl.when(t - block == distance)
            def _():
                for p in range(self.pieces):
                    self.right(i, p).wait_recv()
                    pl.when(t < 3)(lambda: self.right(i, p).start())

            @pl.when(block - t == distance)
            def _():
                for p in range(self.pieces):
                    self.left(i, p).wait_recv()
                    pl.when(t > 0)(lambda: self.left(i, p).start())

    def finish(self):
        t = self.me.t
        for i, (block, slot) in enumerate(self.where):
            for p in range(self.pieces):
                pl.when((t >= block) & (t < 3))(lambda: self.right(i, p).wait_send())
                pl.when((t <= block) & (t > 0))(lambda: self.left(i, p).wait_send())


class SumLine:
    def __init__(self, pool, me, own, coming, going, pieces=2):
        self.pool, self.me, self.own, self.coming, self.going = pool, me, own, coming, going
        self.pieces, self.sub = pieces, own.shape[1] // pieces
        self.first = pool.take(6 * pieces)

    def copy(self, slot, piece, source):
        here = pl.ds(piece * self.sub, self.sub)
        peer = self.me.z[1] if slot < 3 else self.me.z[3]
        return self.pool.copy(
            self.first + slot * self.pieces + piece, peer, source.at[here], self.coming.at[slot, here]
        )

    def dest(self, slot):
        return 3 - slot if slot < 3 else slot - 3

    def direct(self, slot):
        return self.me.t == (0 if slot < 3 else 3)

    def start(self):
        for slot in (0, 3, 1, 4, 2, 5):

            @pl.when(self.direct(slot))
            def _():
                for p in range(self.pieces):
                    self.copy(slot, p, self.own.at[self.dest(slot)]).start()

    passing = ((0, 1), (3, 2), (1, 1), (4, 2), (0, 2), (3, 1))

    def add(self, part):
        for slot, chip in self.passing[2 * part : 2 * part + 2]:

            @pl.when(self.me.t == chip)
            def _():
                for p in range(self.pieces):
                    here = pl.ds(p * self.sub, self.sub)
                    self.copy(slot, p, self.going.at[slot]).wait_recv()
                    self.going[slot, here] = (
                        self.own[self.dest(slot), here].astype(F32) + self.coming[slot, here].astype(F32)
                    ).astype(BF)
                    self.copy(slot, p, self.going.at[slot]).start()

    def result(self, out):
        t = self.me.t
        for slot in range(6):

            @pl.when(t == self.dest(slot))
            def _():
                for p in range(self.pieces):
                    self.copy(slot, p, self.going.at[slot]).wait_recv()

        out[...] = self.own[t].astype(F32)

        @pl.when(t > 0)
        def _():
            out[...] += self.coming[3 - t].astype(F32)

        @pl.when(t < 3)
        def _():
            out[...] += self.coming[3 + t].astype(F32)

    def finish(self):
        for slot in range(6):

            @pl.when(self.direct(slot))
            def _():
                for p in range(self.pieces):
                    self.copy(slot, p, self.own.at[self.dest(slot)]).wait_send()

        for slot, chip in self.passing:

            @pl.when(self.me.t == chip)
            def _():
                for p in range(self.pieces):
                    self.copy(slot, p, self.going.at[slot]).wait_send()


class GradLine:
    def __init__(self, pool, me, own, coming, going, shared, pieces=2):
        self.pool, self.me, self.own, self.coming, self.going, self.shared = pool, me, own, coming, going, shared
        self.pieces, self.sub = pieces, own.shape[1] // pieces
        self.first = pool.take(4 * pieces + 1)
        self.home = me.c == me.t // 2

    def here(self, piece):
        return pl.ds(piece * self.sub, self.sub)

    def copy(self, slot, source, piece):
        peer = self.me.z[1] if slot < 2 else self.me.z[3]
        here = self.here(piece)
        return self.pool.copy(
            self.first + slot * self.pieces + piece, peer, source.at[here], self.coming.at[slot, here]
        )

    def index(self, slot):
        return (1, 0, 0, 1)[slot]

    def block(self, slot):
        return 2 * self.me.c + self.index(slot)

    def direct(self, slot):
        t = self.me.t
        return (t == 0) & (self.block(slot) > 0) if slot < 2 else (t == 3) & (self.block(slot) < 3)

    def start(self):
        for slot in (0, 2, 1, 3):
            for p in range(self.pieces):
                pl.when(self.direct(slot))(lambda: self.copy(slot, self.own.at[self.index(slot)], p).start())

    passing = ((0, 1), (2, 2), (1, 1), (3, 2), (0, 2), (2, 1))

    def adds(self, slot, chip):
        return (self.me.t == chip) & ((chip < self.block(slot)) if slot < 2 else (chip > self.block(slot)))

    def add(self, part):
        for slot, chip in self.passing[2 * part : 2 * part + 2]:

            @pl.when(self.adds(slot, chip))
            def _():
                for p in range(self.pieces):
                    here = self.here(p)
                    self.copy(slot, self.going.at[slot], p).wait_recv()
                    self.going[slot, here] = (
                        self.own[self.index(slot), here].astype(F32) + self.coming[slot, here].astype(F32)
                    ).astype(BF)
                    self.copy(slot, self.going.at[slot], p).start()

    def share(self):
        return self.pool.copy(self.first + 4 * self.pieces, self.me.core, self.shared, self.shared)

    def settle(self, total):
        t = self.me.t

        for slot in range(4):
            ends = (t == self.block(slot)) & (t > 0 if slot < 2 else t < 3)
            for p in range(self.pieces):
                pl.when(ends)(lambda: self.copy(slot, self.going.at[slot], p).wait_recv())

        @pl.when(self.home)
        def _():
            j = lax.rem(t, 2)
            total[...] = self.own[j].astype(F32)

            @pl.when(t > 0)
            def _():
                total[...] += self.coming[1 - j].astype(F32)

            @pl.when(t < 3)
            def _():
                total[...] += self.coming[2 + j].astype(F32)

            self.shared[...] = total[...].astype(BF)
            self.share().start()

    def finish(self):
        for slot in range(4):
            for p in range(self.pieces):
                pl.when(self.direct(slot))(lambda: self.copy(slot, self.own.at[self.index(slot)], p).wait_send())
        for slot, chip in self.passing:
            for p in range(self.pieces):
                pl.when(self.adds(slot, chip))(lambda: self.copy(slot, self.going.at[slot], p).wait_send())
        pl.when(self.home)(lambda: self.share().wait_send())
        pl.when(jnp.logical_not(self.home))(lambda: self.share().wait_recv())


def start_kernel(
    gains_ref, x_ref, e_ref, g_ref, t_ref, b0, b1, b2, gains_out, n_all, e_all, n_pair, x_pair, g_pair, t_pair, w0, w1, mix2,
    gain_slots, n_ref, take0, take1, take2, mix0, mix1, sends, arrivals, local, *, cuts,
):
    me = Peers()
    meet([me.z[1], me.z[3], me.core, me.x, me.y, me.d])
    pool = Pool(sends, arrivals)
    send = Sender(pool)
    rows = x_ref.shape[0]
    locals_ = []

    def copy_here(source, target):
        copy = pltpu.make_async_copy(source, target, local.at[len(locals_)])
        copy.start()
        locals_.append(copy)

    gain_slots[me.s] = gains_ref[...]
    gain_copies = [send.to(peer, gains_ref, gain_slots.at[me.s]) for peer in (me.x, me.y, me.d)]
    bundles = [(b0, take0, mix0), (b1, take1, mix1), (b2, take2, mix2)]
    lines = [BlockLine(pool, me, block, take) for block, take, mix in bundles]

    def interleave(i):
        block, take, mix = bundles[i]
        first = take[0]
        second = take[1]
        columns = []
        for start, stop in cuts[i]:
            columns += [first[:, start:stop], second[:, start:stop]]
        mix[...] = jnp.concatenate(columns, axis=1)

    depth = b0.shape[0]
    half = depth // 2
    mine = pl.ds(me.s * depth, depth)

    def share(i, w):
        mix = bundles[i][2]
        copy_here(mix, w.at[mine])
        return send.to(me.x, mix, w.at[mine]), send.to(me.y, mix, w.at[mine])

    onward = []

    def pass_on(to_x, to_y, x_part, y_part):
        to_x.wait_recv()
        onward.append(send.to(me.y, x_part, x_part))
        to_y.wait_recv()
        onward.append(send.to(me.x, y_part, y_part))

    def pass_weights(over, w):
        pass_on(*over, w.at[pl.ds(me.sx * depth, half)], w.at[pl.ds(me.sy * depth + half, half)])

    lines[0].begin()
    lines[1].begin()
    for copy in gain_copies:
        copy.wait_recv()
    width = x_ref.shape[1] // 4
    gains = jnp.concatenate([gain_slots[i][:, :width] for i in range(4)], axis=1)
    gains_out[...] = gains
    n_ref[...] = normalize(x_ref[...].astype(F32), gains[0:1])[0].astype(BF)
    n_line = RowLine(pool, me, n_ref, n_all, rows)
    e_line = RowLine(pool, me, e_ref, e_all, rows)
    n_line.begin()
    copy_here(n_ref, n_all.at[pl.ds((me.c * 4 + me.t) * rows, rows)])
    copy_here(e_ref, e_all.at[pl.ds((me.c * 4 + me.t) * rows, rows)])
    swapped = []
    for ref, pair in ((n_ref, n_pair), (x_ref, x_pair), (g_ref, g_pair), (t_ref, t_pair)):
        where = pair.at[pl.ds(me.c * ref.shape[0], ref.shape[0])]
        swapped.append(send.to(me.core, ref, where))
        copy_here(ref, where)
    lines[0].arrive(1)
    lines[1].arrive(1)
    lines[0].arrive(2)
    lines[1].arrive(2)
    n_line.step(0)
    lines[0].arrive(3)
    interleave(0)
    over0 = share(0, w0)
    lines[1].arrive(3)
    interleave(1)
    over1 = share(1, w1)
    lines[2].begin()
    e_line.begin()
    n_line.step(1)
    n_line.step(2)
    lines[2].arrive(1)
    e_line.step(0)
    pass_weights(over0, w0)
    lines[2].arrive(2)
    e_line.step(1)
    pass_weights(over1, w1)
    lines[2].arrive(3)
    e_line.step(2)
    interleave(2)
    for copy in onward + swapped:
        copy.wait_recv()
    for line in lines + [n_line, e_line]:
        line.finish()
    send.finish()
    for copy in locals_:
        copy.wait()


def start_gather(gains, inputs, encoder, cotangent, targets, bundles, cuts):
    rows, depth = inputs.shape
    part = bundles[0].shape[0]
    any_space = pl.BlockSpec(memory_space=pl.ANY)
    vmem = pl.BlockSpec(memory_space=pltpu.VMEM)
    return pl.pallas_call(
        partial(start_kernel, cuts=cuts),
        in_specs=[vmem] * 8,
        out_specs=[vmem] + [any_space] * 8 + [vmem],
        out_shape=[
            jax.ShapeDtypeStruct((gains.shape[0], depth), F32),
            jax.ShapeDtypeStruct((8 * rows, depth), BF),
            jax.ShapeDtypeStruct((8 * rows, depth), BF),
        ]
        + [jax.ShapeDtypeStruct((2 * a.shape[0], a.shape[1]), a.dtype) for a in (inputs, inputs, cotangent, targets)]
        + [jax.ShapeDtypeStruct((4 * part, 2 * b.shape[1]), BF) for b in bundles[:2]]
        + [jax.ShapeDtypeStruct((part, 2 * bundles[2].shape[1]), BF)],
        scratch_shapes=[pltpu.VMEM((4,) + gains.shape, F32), pltpu.VMEM((rows, depth), BF)]
        + [pltpu.VMEM((2,) + b.shape, BF) for b in bundles]
        + [pltpu.VMEM((part, 2 * b.shape[1]), BF) for b in bundles[:2]]
        + [pltpu.SemaphoreType.DMA((96,)), pltpu.SemaphoreType.DMA((96,)), pltpu.SemaphoreType.DMA((16,))],
        compiler_params=pltpu.CompilerParams(collective_id=0, has_side_effects=True, vmem_limit_bytes=VMEM_LIMIT),
        name="start_gather",
    )(gains, inputs, encoder, cotangent, targets, *bundles)


def rows_kernel(n_ref, n_all, sends, arrivals, local):
    me = Peers()
    meet([me.z[1], me.z[3], me.core])
    rows = n_ref.shape[0]
    copy = pltpu.make_async_copy(n_ref, n_all.at[pl.ds((me.c * 4 + me.t) * rows, rows)], local)
    copy.start()
    line = RowLine(Pool(sends, arrivals), me, n_ref, n_all, rows)
    line.begin()
    for k in range(3):
        line.step(k)
    line.finish()
    copy.wait()


def gather_rows(normed):
    rows, depth = normed.shape
    return pl.pallas_call(
        rows_kernel,
        in_specs=[pl.BlockSpec(memory_space=pltpu.VMEM)],
        out_specs=pl.BlockSpec(memory_space=pl.ANY),
        out_shape=jax.ShapeDtypeStruct((8 * rows, depth), normed.dtype),
        scratch_shapes=[pltpu.SemaphoreType.DMA((26,)), pltpu.SemaphoreType.DMA((26,)), pltpu.SemaphoreType.DMA],
        compiler_params=pltpu.CompilerParams(collective_id=1, has_side_effects=True, vmem_limit_bytes=VMEM_LIMIT),
        name="gather_rows",
    )(normed)


def stats_kernel(stats_ref, out_ref, slots, sends, arrivals):
    me = Peers()
    meet(me.group)
    send = Sender(Pool(sends, arrivals))
    here = slots.at[me.c * 4 + me.t]
    slots[me.c * 4 + me.t] = stats_ref[...]
    copies = [send.to(peer, stats_ref, here) for peer in me.group]
    for copy in copies:
        copy.wait_recv()
    lines = stats_ref.shape[0] // 3
    top = slots[0, 0:lines]
    for i in range(1, 8):
        top = jnp.maximum(top, slots[i, 0:lines])
    total = jnp.zeros_like(top)
    picked = jnp.zeros_like(top)
    for i in range(8):
        total += slots[i, lines : 2 * lines] * jnp.exp(slots[i, 0:lines] - top)
        picked += slots[i, 2 * lines : 3 * lines]
    logsum = top + jnp.log(total)
    out_ref[0] = logsum
    out_ref[1] = logsum - picked
    send.finish()


def combine_stats(stats):
    return pl.pallas_call(
        stats_kernel,
        in_specs=[pl.BlockSpec(memory_space=pltpu.VMEM)],
        out_specs=pl.BlockSpec(memory_space=pltpu.VMEM),
        out_shape=jax.ShapeDtypeStruct((2, stats.shape[0] // 3, stats.shape[1]), F32),
        scratch_shapes=[pltpu.VMEM((8,) + stats.shape, F32), pltpu.SemaphoreType.DMA((8,)), pltpu.SemaphoreType.DMA((8,))],
        compiler_params=pltpu.CompilerParams(collective_id=2, has_side_effects=True),
        name="combine_stats",
    )(stats)


def settle_first(send, me, part_ref, other, half):
    return send.to(me.core, part_ref.at[pl.ds((1 - me.c) * half, half)], other)


def settle_second(me, part_ref, other, summed, rows):
    half = 4 * rows
    for k in range(4):
        summed[k] = (
            part_ref[pl.ds(me.c * half + k * rows, rows)].astype(F32) + other[k * rows : (k + 1) * rows].astype(F32)
        ).astype(BF)


class Planar:
    def __init__(self, send, me, part, first, second, moving, chunks):
        self.send, self.me, self.part = send, me, part
        self.first, self.second, self.moving, self.chunks = first, second, moving, chunks

    def begin(self):
        me = self.me
        self.one = []
        for start, stop, along_x in self.chunks:
            here = slice(start, stop)
            near, near_block = (me.x, me.sx) if along_x else (me.y, me.sy)
            self.one.append(
                (
                    self.send.to(near, self.part.at[me.sd, here], self.first.at[1, here]),
                    self.send.to(near, self.part.at[near_block, here], self.first.at[0, here]),
                )
            )

    def gather(self, i):
        me = self.me
        start, stop, along_x = self.chunks[i]
        here = slice(start, stop)
        self.one[i][0].wait_recv()
        self.moving[here] = (
            self.part[me.sy if along_x else me.sx, here].astype(F32) + self.first[1, here].astype(F32)
        ).astype(BF)
        return here

    def own(self, i):
        start, stop, along_x = self.chunks[i]
        here = slice(start, stop)
        self.one[i][1].wait_recv()
        return self.part[self.me.s, here].astype(F32) + self.first[0, here].astype(F32)

    def go_on(self):
        self.two = []
        for start, stop, along_x in self.chunks:
            here = slice(start, stop)
            self.two.append(
                self.send.to(self.me.y if along_x else self.me.x, self.moving.at[here], self.second.at[here])
            )

    def middle(self):
        for i in range(len(self.chunks)):
            self.gather(i)
        self.go_on()

    def end(self, store):
        for i, copy in enumerate(self.two):
            start, stop, along_x = self.chunks[i]
            here = slice(start, stop)
            copy.wait_recv()
            store(here, self.own(i) + self.second[here].astype(F32))


def halves(count, parts, step):
    middle = (count // 2 + step - 1) // step * step
    out = []
    for low, high, along_x in ((0, middle, True), (middle, count, False)):
        size = ((high - low) // parts + step - 1) // step * step
        edges = list(range(low, high, size)) + [high]
        out.append([(a, b, along_x) for a, b in zip(edges[:-1], edges[1:])])
    return [chunk for pair in zip(*out) for chunk in pair]


def middle_kernel(dn_ref, de_ref, gn_ref, own_ref, move_ref, other, summed, coming, going, total, first, sends, arrivals, *, chunks):
    me = Peers()
    meet([me.z[1], me.z[3], me.core, me.x, me.y])
    pool = Pool(sends, arrivals)
    send = Sender(pool)
    rows = summed.shape[1]
    crossing = settle_first(send, me, dn_ref, other, 4 * rows)
    plane = Planar(send, me, de_ref, first, None, move_ref, chunks)
    plane.begin()
    crossing.wait_recv()
    settle_second(me, dn_ref, other, summed, rows)
    line = SumLine(pool, me, summed, coming, going)
    line.start()
    for part in range(3):
        line.add(part)
    line.result(total)
    own = pl.ds(me.c * rows, rows)
    gn_ref[own] = total[...].astype(BF)
    share = send.to(me.core, gn_ref.at[own], gn_ref.at[own])
    for i in range(len(chunks)):
        here = plane.gather(i)
        own_ref[here] = plane.own(i).astype(BF)
    share.wait_recv()
    line.finish()
    send.finish()


def middle_scatter(dn, de):
    total, depth = dn.shape
    rows = total // 8
    groups, part, wide = de.shape
    chunks = halves(part, 3, 16)
    count = 14 + 2 * len(chunks)
    vmem = pl.BlockSpec(memory_space=pltpu.VMEM)
    return pl.pallas_call(
        partial(middle_kernel, chunks=chunks),
        in_specs=[vmem] * 2,
        out_specs=[vmem] * 3,
        out_shape=[
            jax.ShapeDtypeStruct((2 * rows, depth), BF),
            jax.ShapeDtypeStruct((part, wide), BF),
            jax.ShapeDtypeStruct((part, wide), BF),
        ],
        scratch_shapes=[
            pltpu.VMEM((4 * rows, depth), BF),
            pltpu.VMEM((4, rows, depth), BF),
            pltpu.VMEM((6, rows, depth), BF),
            pltpu.VMEM((6, rows, depth), BF),
            pltpu.VMEM((rows, depth), F32),
            pltpu.VMEM((2, part, wide), BF),
            pltpu.SemaphoreType.DMA((count,)),
            pltpu.SemaphoreType.DMA((count,)),
        ],
        compiler_params=pltpu.CompilerParams(collective_id=3, has_side_effects=True, vmem_limit_bytes=VMEM_LIMIT),
        name="middle_scatter",
    )(dn, de)


def tail_kernel(
    dn_ref, c0, c1, c2, c3, s0, s1, s2, s3, f_ref, gains_ref, eo_ref, em_ref,
    dn_out, held0, held1, held2, gain_out, e_sum, g0, g1, e_second, other, summed, coming, going, first0, second0, moving0, first1, second1, moving1,
    ab0, ab1, ab2, in0, in1, in2, out0, out1, out2, sum0, sum1, sum2, slots, plane_sum, plane_slots, sends, arrivals, *, cuts, chunks,
):
    me = Peers()
    meet(me.group + [me.x, me.y, me.d])
    pool = Pool(sends, arrivals)
    send = Sender(pool)
    rows = summed.shape[1]
    crossing = settle_first(send, me, dn_ref, other, 4 * rows)
    planes = [
        Planar(send, me, g0, first0, second0, moving0, chunks),
        Planar(send, me, g1, first1, second1, moving1, chunks),
    ]

    def collect(target, pieces):
        for i, piece in enumerate(pieces):
            target[:, :, i * piece.shape[2] : (i + 1) * piece.shape[2]] = piece[...]

    def split(value, cut):
        return [
            jnp.concatenate([value[:, 2 * a + i * (b - a) : 2 * a + (i + 1) * (b - a)] for a, b in cut], axis=1).astype(BF)
            for i in range(2)
        ]

    collect(g0, (c0, c1, c2, c3))
    planes[0].begin()
    ff_line = GradLine(pool, me, ab2, in2, out2, held2)
    lines = [GradLine(pool, me, ab0, in0, out0, held0), GradLine(pool, me, ab1, in1, out1, held1)]
    for i, half in enumerate(split(f_ref[...], cuts[2])):
        ab2[i] = half
    ff_line.start()
    crossing.wait_recv()
    settle_second(me, dn_ref, other, summed, rows)
    row_line = SumLine(pool, me, summed, coming, going)
    row_line.start()
    collect(g1, (s0, s1, s2, s3))
    planes[1].begin()
    slots[me.c * 4 + me.t] = gains_ref[...]
    gain_copies = [send.to(peer, gains_ref, slots.at[me.c * 4 + me.t]) for peer in me.group]
    ff_line.add(0)
    row_line.add(0)
    planes[0].middle()
    ff_line.add(1)
    row_line.add(1)
    planes[1].middle()
    ff_line.add(2)
    row_line.add(2)
    e_copies = [
        send.to(me.y if along_x else me.x, em_ref.at[start:stop], e_second.at[start:stop])
        for start, stop, along_x in halves(eo_ref.shape[0], 1, 16)
    ]
    for copy in gain_copies:
        copy.wait_recv()
    total = slots[0]
    for i in range(1, 8):
        total += slots[i]
    plane_sum[...] = total
    plane_slots[me.s] = total
    plane_copies = [send.to(peer, plane_sum, plane_slots.at[me.s]) for peer in (me.x, me.y, me.d)]
    for plane, cut, ab, line in ((planes[0], cuts[0], ab0, lines[0]), (planes[1], cuts[1], ab1, lines[1])):

        def store(here, value):
            for i, half in enumerate(split(value, cut)):
                ab[i, here] = half

        plane.end(store)
        line.start()
    for part in range(3):
        lines[0].add(part)
        lines[1].add(part)
    row_line.result(dn_out)
    ff_line.settle(sum2)
    for copy in e_copies:
        copy.wait_recv()
    e_sum[me.c] = (eo_ref[...].astype(F32) + e_second[...].astype(F32)).astype(BF)
    e_share = send.to(me.core, e_sum.at[me.c], e_sum.at[me.c])
    for copy in plane_copies:
        copy.wait_recv()
    gain_out[...] = plane_slots[0] + plane_slots[1] + plane_slots[2] + plane_slots[3]
    lines[0].settle(sum0)
    lines[1].settle(sum1)
    for line in (ff_line, lines[0], lines[1]):
        line.finish()
    e_share.wait_recv()
    row_line.finish()
    send.finish()


def tail_scatter(dn, grads, ff, gains, emb_own, emb_move, cuts):
    total, depth = dn.shape
    rows = total // 8
    groups, part, width = grads[0][0].shape
    width *= 4
    chunks = halves(part, 1, 16)
    vmem = pl.BlockSpec(memory_space=pltpu.VMEM)
    widths = [width // 2, width // 2, ff.shape[1] // 2]
    scratch = [
        pltpu.VMEM((groups, part, width), BF),
        pltpu.VMEM((groups, part, width), BF),
        pltpu.VMEM(emb_own.shape, BF),
        pltpu.VMEM((4 * rows, depth), BF),
        pltpu.VMEM((4, rows, depth), BF),
        pltpu.VMEM((6, rows, depth), BF),
        pltpu.VMEM((6, rows, depth), BF),
    ]
    for _ in grads:
        scratch += [pltpu.VMEM((2, part, width), BF), pltpu.VMEM((part, width), BF), pltpu.VMEM((part, width), BF)]
    for count in (2, 4, 4):
        scratch += [pltpu.VMEM((count, part, w), BF) for w in widths]
    scratch += [pltpu.VMEM((part, w), F32) for w in widths]
    scratch += [
        pltpu.VMEM((8,) + gains.shape, F32),
        pltpu.VMEM(gains.shape, F32),
        pltpu.VMEM((4,) + gains.shape, F32),
        pltpu.SemaphoreType.DMA((80,)),
        pltpu.SemaphoreType.DMA((80,)),
    ]
    return pl.pallas_call(
        partial(tail_kernel, cuts=cuts, chunks=chunks),
        in_specs=[vmem] * 13,
        out_specs=[vmem] * 6,
        out_shape=[jax.ShapeDtypeStruct((rows, depth), F32)]
        + [jax.ShapeDtypeStruct((part, w), BF) for w in widths]
        + [jax.ShapeDtypeStruct(gains.shape, F32), jax.ShapeDtypeStruct((2,) + emb_own.shape, BF)],
        scratch_shapes=scratch,
        compiler_params=pltpu.CompilerParams(collective_id=4, has_side_effects=True, vmem_limit_bytes=VMEM_LIMIT),
        name="tail_scatter",
    )(dn, *grads[0], *grads[1], ff, gains, emb_own, emb_move)


def finish_kernel(
    emb_ref, self_ref, cross_ref, ff_ref, x_ref, gh_ref, gn_ref, gain_ref, eg_ref, dx_ref, *outs
):
    half = eg_ref.shape[1] // 2
    for c in range(2):
        eg_ref[:, c * half : (c + 1) * half] = emb_ref[c, :, :half].astype(F32)
    x = x_ref[...].astype(F32)
    inverse = lax.rsqrt(jnp.mean(x * x, axis=-1, keepdims=True) + EPS)
    dx_ref[...] = gh_ref[...] + norm_back(x, inverse, gain_ref[...], gn_ref[...])
    index = 0
    for ref, count in ((self_ref, 4), (cross_ref, 4), (ff_ref, 3)):
        size = ref.shape[1] // count
        for k in range(count):
            outs[index][...] = ref[:, k * size : (k + 1) * size].astype(F32)
            index += 1


def finish(emb, own_self, own_cross, own_ff, x, grad_hidden, gn, gain, vocab):
    part, width = own_self.shape
    shapes = []
    for total, count in ((width, 4), (width, 4), (own_ff.shape[1], 3)):
        shapes += [(part, total // count)] * count
    ins = (emb, own_self, own_cross, own_ff, x, grad_hidden, gn, gain)
    vmem = pl.BlockSpec(memory_space=pltpu.VMEM)
    return pl.pallas_call(
        finish_kernel,
        in_specs=[vmem] * len(ins),
        out_specs=[vmem] * (2 + len(shapes)),
        out_shape=[jax.ShapeDtypeStruct((part, vocab), F32), jax.ShapeDtypeStruct(x.shape, F32)]
        + [jax.ShapeDtypeStruct(shape, F32) for shape in shapes],
        compiler_params=pltpu.CompilerParams(vmem_limit_bytes=VMEM_LIMIT),
        name="finish",
    )(*ins)


def normalize(hidden, gain):
    inverse = lax.rsqrt(jnp.mean(hidden * hidden, axis=-1, keepdims=True) + EPS)
    return (hidden * inverse * gain, inverse)


def norm_back(hidden, inverse, gain, upstream):
    scaled = upstream * gain
    inner = jnp.mean(scaled * hidden, axis=-1, keepdims=True)
    return inverse * scaled - hidden * (inverse * inverse * inverse) * inner


def matmul(left, right):
    return jnp.dot(left, right, preferred_element_type=F32)


def left_t(left, right):
    return jnp.einsum("ra,rb->ab", left, right, preferred_element_type=F32)


def right_t(left, right):
    return jnp.einsum("ra,ba->rb", left, right, preferred_element_type=F32)


def swap(array):
    return lax.ppermute(array, "ctx", [(0, 1), (1, 0)])


def per_device(
    inputs, encoder, prefix, targets, cotangent, gain_self, query_self, key_self, value_self, output_self,
    gain_cross, query_cross, key_cross, value_cross, output_cross, gain_hidden, gate_weight, up_weight,
    down_weight, gain_exit, embedding,
):
    tp = lax.axis_size("tp")
    ctx = lax.axis_size("ctx")
    shards = lax.axis_size("shard")
    assert tp == 4 and ctx == 2
    core = lax.axis_index("ctx")
    place = lax.axis_index("tp")
    rows, depth = inputs.shape
    group = rows * tp
    total = group * ctx
    hb = query_self.shape[1]
    width = 2 * hb
    fb = gate_weight.shape[1]
    pair = rows * ctx

    route_a = []
    route_b = []
    for c in range(2):
        for z in range(4):
            dest = c * 4 + z
            route_a.append(((z % 2) * 4 + 2 * c + z // 2, dest))
            route_b.append(((z % 2) * 4 + 2 * c + 1 - z // 2, dest))
    both = ("ctx", "tp")

    def spread_weights(parts):
        block = jnp.concatenate(parts, axis=1)
        first = lax.ppermute(block, both, route_a)
        second = lax.ppermute(block, both, route_b)
        columns = []
        start = 0
        for piece in parts:
            stop = start + piece.shape[1]
            columns += [first[:, start:stop], second[:, start:stop]]
            start = stop
        return lax.all_gather(jnp.concatenate(columns, axis=1), "shard", axis=0, tiled=True)

    def collect_weights(grad, widths):
        mine = lax.psum_scatter(grad, "shard", scatter_dimension=0, tiled=True)
        first = []
        second = []
        start = 0
        for size in widths:
            first.append(mine[:, start : start + size])
            second.append(mine[:, start + size : start + 2 * size])
            start += 2 * size
        back = lambda route: [(dest, source) for source, dest in route]
        one = lax.ppermute(jnp.concatenate(first, axis=1), both, back(route_a))
        two = lax.ppermute(jnp.concatenate(second, axis=1), both, back(route_b))
        part = (one.astype(F32) + two.astype(F32)).astype(BF)
        whole = part.astype(F32) + swap(part).astype(F32)
        outs = []
        start = 0
        for size in widths:
            outs.append(whole[:, start : start + size])
            start += size
        return outs

    def couple(own, other):
        return jnp.where(
            core == 0, jnp.concatenate([own, other], axis=0), jnp.concatenate([other, own], axis=0)
        )

    fast = shards == 4
    own_f = inputs.astype(F32)
    parts_self = [query_self, key_self, value_self, output_self.T]
    parts_cross = [query_cross, key_cross, value_cross, output_cross.T]
    parts_ff = [gate_weight, up_weight, down_weight.T]
    gain_parts = jnp.stack([gain_self, gain_cross, gain_hidden, gain_exit])
    cuts = [[(i * w, (i + 1) * w) for i in range(n)] for n, w in ((4, hb), (4, hb), (3, fb))]
    vocab_half = embedding.shape[0] // ctx
    vblock, rblock = 512, 512
    emb_mine = lax.dynamic_slice_in_dim(embedding.T, core * vocab_half, vocab_half, axis=1)
    emb_mine = jnp.pad(emb_mine, ((0, 0), (0, -vocab_half % vblock)))
    emb_t = lax.all_gather(emb_mine, "shard", axis=0, tiled=True)

    def take_pair(array):
        cut = array.reshape(ctx, group, depth)
        return lax.dynamic_slice_in_dim(cut, place * rows, rows, axis=1).reshape(pair, depth)

    if fast:
        bundles = [jnp.concatenate(parts, axis=1) for parts in (parts_self, parts_cross, parts_ff)]
        spare = -(depth // shards) % 128
        gain_block = jnp.pad(gain_parts.astype(F32), ((0, 4), (0, spare)))
        (
            gains, normed1, encoder_all, normed1_pair, x_pair, g_pair, t_pair, weights_self, weights_cross, ff_mix,
        ) = start_gather(
            gain_block, inputs, encoder, cotangent, targets.reshape(8, group // 8), bundles, cuts
        )
        hidden0 = x_pair.astype(F32)
        cotangent_pair = g_pair.astype(F32)
        targets_all = t_pair.reshape(total)
        ff_mix, emb_t = lax.optimization_barrier((ff_mix, emb_t))
        weights_ff = lax.all_gather(ff_mix, "shard", axis=0, tiled=True)
    else:
        gains = lax.all_gather(gain_parts, "shard", axis=1, tiled=True).astype(F32)
        normed1_own = normalize(own_f, gains[0])[0].astype(BF)
        normed1 = lax.all_gather(normed1_own, both, axis=0, tiled=True)
        normed1_pair = take_pair(normed1)
        encoder_all = lax.all_gather(encoder, both, axis=0, tiled=True)
        weights_self, weights_cross, weights_ff = map(spread_weights, (parts_self, parts_cross, parts_ff))
        hidden0 = couple(inputs, swap(inputs)).astype(F32)
        cotangent_pair = couple(cotangent, swap(cotangent)).astype(F32)
        targets_all = couple(targets, swap(targets))

    gain_one, gain_two, gain_three, gain_four = [gains[i] for i in range(4)]
    inverse1_own = normalize(own_f, gain_one)[1]
    query_w, key_w, value_w, out_w = [weights_self[:, i * width : (i + 1) * width] for i in range(4)]
    scale = HEAD_DIM**-0.5

    def project_q(normed, weight):
        return matmul(normed, weight).astype(BF) * jnp.asarray(scale, BF)

    positions = jnp.concatenate(
        [c * group + place * rows + jnp.arange(rows, dtype=jnp.int32) for c in range(2)]
    )
    limit = prefix[0]
    seen = jnp.maximum(positions + 1, limit)[None, :]
    causal_tiles = (((0, pair), (0, group), True), ((rows, pair), (group, total), True))
    open_tiles = (((0, pair), (0, total), False),)

    query1 = project_q(normed1_pair, query_w)
    kv1 = matmul(normed1, weights_self[:, width : 3 * width]).astype(BF)
    attended1, attended1_t, lse1 = attend(seen, query1, kv1, causal_tiles)

    def add_halves(partial_sum):
        part = partial_sum.astype(BF)
        return partial_sum + swap(part).astype(F32)

    hidden1 = hidden0 + add_halves(right_t(attended1, out_w))
    query2_w, key2_w, value2_w, out2_w = [weights_cross[:, i * width : (i + 1) * width] for i in range(4)]
    kv2 = matmul(encoder_all, weights_cross[:, width : 3 * width]).astype(BF)
    normed2, inverse2 = normalize(hidden1, gain_two)
    normed2 = normed2.astype(BF)
    query2 = project_q(normed2, query2_w)
    attended2, attended2_t, lse2 = attend(seen, query2, kv2, open_tiles)
    hidden2 = hidden1 + add_halves(right_t(attended2, out2_w))
    normed3, inverse3 = normalize(hidden2, gain_three)
    normed3 = normed3.astype(BF)
    gate_w, up_w, down_w = [weights_ff[:, i * 2 * fb : (i + 1) * 2 * fb] for i in range(3)]
    gate = matmul(normed3, gate_w)
    upper = matmul(normed3, up_w)
    active = jax.nn.gelu(gate, approximate=True)
    product = (active * upper).astype(BF)
    final = hidden2 + add_halves(right_t(product, down_w))
    normed4, inverse4 = normalize(final, gain_four)
    normed4 = normed4.astype(BF)

    def mine(array):
        return lax.dynamic_slice_in_dim(array, core * rows, rows, axis=0)

    final_own = mine(final)
    if fast:
        normed4_all = gather_rows(mine(normed4))
    else:
        normed4_all = lax.all_gather(mine(normed4), both, axis=0, tiled=True)
    local_target = (targets_all - (place * embedding.shape[0] + core * vocab_half))[None, :].astype(jnp.int32)
    stats, expo, tops = head_stats(emb_t, normed4_all, local_target, vocab_half, vblock, rblock)
    if fast:
        combined = combine_stats(stats)
        logsum = combined[0].reshape(total)
        loss = combined[1].reshape(total)
    else:
        every = lax.all_gather(stats.reshape(3, total), both, axis=0)
        top = jnp.max(every[:, 0], axis=0)
        summed = jnp.sum(every[:, 1] * jnp.exp(every[:, 0] - top[None]), axis=0)
        logsum = top + jnp.log(summed)
        loss = logsum - jnp.sum(every[:, 2], axis=0)
    exit_loss = lax.dynamic_slice_in_dim(loss, core * group, group, axis=0)
    emb_grad, grad_normed4 = head_back(
        emb_t, expo, tops, normed4_all, local_target, logsum[None, :], vocab_half, vblock, rblock
    )
    if fast:
        gn4, emb_own, emb_move = middle_scatter(grad_normed4, emb_grad.reshape(shards, depth // shards, -1))
        gn4 = gn4.astype(F32)
    else:
        emb_sum = lax.psum_scatter(emb_grad, "shard", scatter_dimension=0, tiled=True)
        emb_other = swap(emb_sum)
        gn4_own = lax.psum_scatter(grad_normed4, both, scatter_dimension=0, tiled=True)
        gn4 = couple(gn4_own, swap(gn4_own)).astype(F32)
    gain4_rows = gn4 * final * inverse4
    grad_final = cotangent_pair + norm_back(final, inverse4, gain_four, gn4)
    grad_final_b = grad_final.astype(BF)
    down_grad = left_t(grad_final_b, product).astype(BF)
    grad_product = matmul(grad_final_b, down_w)
    unused, gelu_pull = jax.vjp(partial(jax.nn.gelu, approximate=True), gate)
    grad_gate = gelu_pull(grad_product * upper)[0].astype(BF)
    grad_upper = (grad_product * active).astype(BF)
    gate_grad = left_t(normed3, grad_gate).astype(BF)
    upper_grad = left_t(normed3, grad_upper).astype(BF)
    ff_part = jnp.concatenate([gate_grad, upper_grad, down_grad], axis=1)
    gn3 = add_halves(right_t(grad_gate, gate_w) + right_t(grad_upper, up_w))
    gain3_rows = gn3 * hidden2 * inverse3
    grad_hidden2 = grad_final + norm_back(hidden2, inverse3, gain_three, gn3)
    grad_hidden2_b = grad_hidden2.astype(BF)
    out2_grad = left_t(grad_hidden2_b, attended2).astype(BF)
    grad_attended2 = matmul(grad_hidden2_b, out2_w).astype(BF)
    if fast:
        ff_mine = lax.psum_scatter(ff_part, "shard", scatter_dimension=0, tiled=True)
    grad_query2, grad_key2, grad_value2 = attend_back(
        seen, query2, kv2, grad_attended2, attended2_t, lse2, open_tiles
    )
    query2_grad = left_t(normed2, grad_query2).astype(BF)
    key2_grad = left_t(encoder_all, grad_key2).astype(BF)
    value2_grad = left_t(encoder_all, grad_value2).astype(BF)
    cross_parts = [query2_grad, key2_grad, value2_grad, out2_grad]
    encoder_part = (right_t(grad_key2, key2_w) + right_t(grad_value2, value2_w)).astype(BF)
    if fast:
        encoder_part, ff_mine = lax.optimization_barrier((encoder_part, ff_mine))
    encoder_grad = lax.psum_scatter(encoder_part, both, scatter_dimension=0, tiled=True).astype(F32)
    gn2 = add_halves(right_t(grad_query2, query2_w))
    gain2_rows = gn2 * hidden1 * inverse2
    grad_hidden1 = grad_hidden2 + norm_back(hidden1, inverse2, gain_two, gn2)
    grad_hidden1_b = grad_hidden1.astype(BF)
    out_grad = left_t(grad_hidden1_b, attended1).astype(BF)
    grad_attended1 = matmul(grad_hidden1_b, out_w).astype(BF)
    grad_query1, grad_key1, grad_value1 = attend_back(
        seen, query1, kv1, grad_attended1, attended1_t, lse1, causal_tiles
    )
    query_grad = left_t(normed1_pair, grad_query1).astype(BF)
    key_grad = left_t(normed1, grad_key1).astype(BF)
    value_grad = left_t(normed1, grad_value1).astype(BF)
    self_parts = [query_grad, key_grad, value_grad, out_grad]
    normed1_part = right_t(grad_key1, key_w) + right_t(grad_value1, value_w)
    query_part = right_t(grad_query1, query_w).reshape(ctx, rows, depth)
    cut = normed1_part.reshape(ctx, group, depth)
    old = lax.dynamic_slice_in_dim(cut, place * rows, rows, axis=1)
    cut = lax.dynamic_update_slice_in_dim(cut, old + query_part, place * rows, axis=1)
    cut = cut.reshape(total, depth).astype(BF)

    def gain_rows(gn1):
        gain1_sum = jnp.sum(gn1 * own_f * inverse1_own, axis=0)
        return jnp.stack(
            [gain1_sum] + [jnp.sum(mine(a), axis=0) for a in (gain2_rows, gain3_rows, gain4_rows)]
        )

    if fast:
        blocks = [
            [a.reshape(shards, depth // shards, a.shape[1]) for a in parts] for parts in (cross_parts, self_parts)
        ]
        gain1_part = jnp.sum(cut.astype(F32) * normed1.astype(F32), axis=0) / gain_one
        gains_part = [gain1_part] + [0.5 * jnp.sum(a, axis=0) for a in (gain2_rows, gain3_rows, gain4_rows)]
        gain_pad = jnp.stack(gains_part + [jnp.zeros_like(gain1_part)] * 4)
        gn1, cross_own, self_own, ff_own, gain_sums, emb_sums = tail_scatter(
            cut, blocks, ff_mine, gain_pad, emb_own, emb_move, [cuts[1], cuts[0], cuts[2]]
        )
        embedding_grad, inputs_grad, *weight_grads = finish(
            emb_sums, self_own, cross_own, ff_own, inputs, mine(grad_hidden1), gn1, gain_one[None],
            embedding.shape[0],
        )
    else:
        emb_halves = [jnp.where(core == 0, a, b)[:, :vocab_half] for a, b in ((emb_sum, emb_other), (emb_other, emb_sum))]
        embedding_grad = jnp.concatenate(emb_halves, axis=1).astype(F32)
        gn1 = lax.psum_scatter(cut, both, scatter_dimension=0, tiled=True).astype(F32)
        ff_grads = collect_weights(ff_part, [fb, fb, fb])
        cross_grads = collect_weights(jnp.concatenate(cross_parts, axis=1), [hb] * 4)
        self_grads = collect_weights(jnp.concatenate(self_parts, axis=1), [hb] * 4)
        gain_sums = lax.psum(gain_rows(gn1), ("shard", "ctx", "tp"))
        inputs_grad = mine(grad_hidden1) + norm_back(own_f, inverse1_own, gain_one, gn1)
        weight_grads = []
        for grads in (self_grads, cross_grads, ff_grads):
            weight_grads += grads
    part = depth // shards
    gain_grads = lax.dynamic_slice_in_dim(gain_sums, lax.axis_index("shard") * part, part, axis=1)
    return (
        final_own.astype(BF), exit_loss, inputs_grad, encoder_grad,
        gain_grads[0], *weight_grads[:3], weight_grads[3].T, gain_grads[1], *weight_grads[4:7], weight_grads[7].T,
        gain_grads[2], *weight_grads[8:10], weight_grads[10].T, gain_grads[3], embedding_grad.T,
    )


def solution(mesh):
    rows = P(("shard", "ctx", "tp"), None)
    into = P("shard", "tp")
    out = P("tp", "shard")
    gain = P("shard")
    weights = (gain, into, into, into, out, gain, into, into, into, out, gain, into, into, out, gain, out)
    return jax.shard_map(
        per_device,
        mesh=mesh,
        in_specs=(rows, rows, P("shard"), P(("shard", "ctx")), rows) + weights,
        out_specs=(rows, P(("shard", "ctx")), rows, rows) + weights,
        check_vma=False,
    )
```

```python
from functools import partial

import jax
import jax.numpy as jnp
from jax import lax
from jax.experimental import pallas as pl
from jax.experimental.pallas import tpu as pltpu
from jax.sharding import PartitionSpec as P

HEAD_DIM = 64
LN2 = 0.6931471805599453
EPS = 1e-06
MASKED = -1e30
BF = jnp.bfloat16
F32 = jnp.float32
VMEM_LIMIT = 58 * 2**20


def attend_kernel(seen_ref, q_ref, k_ref, v_ref, o_ref, ot_ref, lse_ref, vt_ref, *, tiles):
    half = lax.broadcasted_iota(jnp.int32, (2 * HEAD_DIM, 1), 0) // HEAD_DIM
    vt_ref[...] = jnp.transpose(v_ref[...])
    q_t = jnp.transpose(q_ref[...])
    for head in range(2):
        part = slice(head * HEAD_DIM, (head + 1) * HEAD_DIM)
        state = None
        for rows, keys, masked in tiles:
            qt = jnp.where(half == head, q_t[:, rows[0] : rows[1]], 0).astype(BF)
            scores = jnp.dot(k_ref[keys[0] : keys[1], :], qt, preferred_element_type=F32)
            if masked:
                key = lax.broadcasted_iota(jnp.int32, (keys[1] - keys[0], 1), 0) + keys[0]
                scores = jnp.where(key < seen_ref[:, rows[0] : rows[1]], scores, MASKED)
            top = jnp.max(scores, axis=0, keepdims=True)
            if state is not None:
                base, old_top, old_total, old_acc = state
                cut = slice(rows[0] - base, rows[1] - base)
                top = jnp.maximum(top, old_top[:, cut])
                shrink = jnp.exp(old_top[:, cut] - top)
            expo = jnp.exp(scores - top)
            total = jnp.sum(expo, axis=0, keepdims=True)
            acc = jnp.dot(vt_ref[part, keys[0] : keys[1]], expo.astype(BF), preferred_element_type=F32)
            if state is not None:
                total += old_total[:, cut] * shrink
                acc += old_acc[:, cut] * shrink
            state = (rows[0], top, total, acc)
            ot_ref[part, rows[0] : rows[1]] = acc / total
            lse_ref[0, head : head + 1, rows[0] : rows[1]] = top + jnp.log(total)
    o_ref[...] = jnp.transpose(ot_ref[...]).astype(BF)


def attend(seen, query, kv, tiles):
    rows, width = query.shape
    count = kv.shape[0]
    pair = 2 * HEAD_DIM
    pairs = width // pair
    return pl.pallas_call(
        partial(attend_kernel, tiles=tiles),
        grid=(pairs,),
        in_specs=[
            pl.BlockSpec((1, rows), lambda p: (0, 0)),
            pl.BlockSpec((rows, pair), lambda p: (0, p)),
            pl.BlockSpec((count, pair), lambda p: (0, p)),
            pl.BlockSpec((count, pair), lambda p: (0, p + pairs)),
        ],
        out_specs=[
            pl.BlockSpec((rows, pair), lambda p: (0, p)),
            pl.BlockSpec((pair, rows), lambda p: (p, 0)),
            pl.BlockSpec((1, 8, rows), lambda p: (p, 0, 0)),
        ],
        scratch_shapes=[pltpu.VMEM((pair, count), BF)],
        out_shape=(
            jax.ShapeDtypeStruct((rows, width), BF),
            jax.ShapeDtypeStruct((width, rows), F32),
            jax.ShapeDtypeStruct((pairs, 8, rows), F32),
        ),
        compiler_params=pltpu.CompilerParams(vmem_limit_bytes=VMEM_LIMIT),
        cost_estimate=pl.CostEstimate(
            flops=4 * rows * count * width, transcendentals=rows * count * width // HEAD_DIM,
            bytes_accessed=2 * count * width * 2 + 8 * rows * width,
        ),
        name="attend",
    )(seen, query, kv, kv)


def attend_back_kernel(
    seen_ref, q_ref, k_ref, v_ref, do_ref, ot_ref, lse_ref, dq_ref, dk_ref, dv_ref, dk_acc, dv_acc, dqt_acc, kt_ref, *, tiles
):
    half = lax.broadcasted_iota(jnp.int32, (2 * HEAD_DIM, 1), 0) // HEAD_DIM
    lane = lax.broadcasted_iota(jnp.int32, (1, 2 * HEAD_DIM), 1) // HEAD_DIM
    kt_ref[...] = jnp.transpose(k_ref[...])
    q_t = jnp.transpose(q_ref[...])
    do_t = jnp.transpose(do_ref[...])
    dqt_acc[...] = jnp.zeros_like(dqt_acc)
    done = []
    for head in range(2):
        part = slice(head * HEAD_DIM, (head + 1) * HEAD_DIM)
        inner_all = jnp.sum(do_t[part].astype(F32) * ot_ref[part], axis=0, keepdims=True)
        for rows, keys, masked in tiles:
            cut = slice(rows[0], rows[1])
            here = slice(keys[0], keys[1])
            qt = jnp.where(half == head, q_t[:, cut], 0).astype(BF)
            dot_t = jnp.where(half == head, do_t[:, cut], 0).astype(BF)
            q = jnp.where(lane == head, q_ref[cut, :], 0).astype(BF)
            do = jnp.where(lane == head, do_ref[cut, :], 0).astype(BF)
            scores = jnp.dot(k_ref[here, :], qt, preferred_element_type=F32)
            probs = jnp.exp(scores - lse_ref[0, head : head + 1, cut])
            if masked:
                key = lax.broadcasted_iota(jnp.int32, (keys[1] - keys[0], 1), 0) + keys[0]
                probs = jnp.where(key < seen_ref[:, cut], probs, 0.0)
            grad_probs = jnp.dot(v_ref[here, :], dot_t, preferred_element_type=F32)
            grad_scores = (probs * (grad_probs - inner_all[:, cut])).astype(BF)
            dv = jnp.dot(probs.astype(BF), do, preferred_element_type=F32)
            dk = jnp.dot(grad_scores, q, preferred_element_type=F32)
            if keys in done:
                dv_acc[here, :] += dv
                dk_acc[here, :] += dk
            else:
                dv_acc[here, :] = dv
                dk_acc[here, :] = dk
                done.append(keys)
            dqt_acc[part, cut] += jnp.dot(kt_ref[part, here], grad_scores, preferred_element_type=F32)
    dq_ref[...] = jnp.transpose(dqt_acc[...] * HEAD_DIM**-0.5).astype(BF)
    dk_ref[...] = dk_acc[...].astype(BF)
    dv_ref[...] = dv_acc[...].astype(BF)


def attend_back(seen, query, kv, grad, out_t, lse, tiles):
    rows, width = query.shape
    count = kv.shape[0]
    pair = 2 * HEAD_DIM
    pairs = width // pair
    by_column = pl.BlockSpec((rows, pair), lambda p: (0, p))
    key_spec = pl.BlockSpec((count, pair), lambda p: (0, p))
    return pl.pallas_call(
        partial(attend_back_kernel, tiles=tiles),
        grid=(pairs,),
        in_specs=[
            pl.BlockSpec((1, rows), lambda p: (0, 0)),
            by_column,
            key_spec,
            pl.BlockSpec((count, pair), lambda p: (0, p + pairs)),
            by_column,
            pl.BlockSpec((pair, rows), lambda p: (p, 0)),
            pl.BlockSpec((1, 8, rows), lambda p: (p, 0, 0)),
        ],
        out_specs=[by_column, key_spec, key_spec],
        scratch_shapes=[
            pltpu.VMEM((count, pair), F32),
            pltpu.VMEM((count, pair), F32),
            pltpu.VMEM((pair, rows), F32),
            pltpu.VMEM((pair, count), BF),
        ],
        out_shape=(
            jax.ShapeDtypeStruct((rows, width), BF),
            jax.ShapeDtypeStruct((count, width), BF),
            jax.ShapeDtypeStruct((count, width), BF),
        ),
        compiler_params=pltpu.CompilerParams(vmem_limit_bytes=VMEM_LIMIT),
        cost_estimate=pl.CostEstimate(
            flops=10 * rows * count * width, transcendentals=rows * count * width // HEAD_DIM,
            bytes_accessed=5 * count * width * 2 + 14 * rows * width,
        ),
        name="attend_back",
    )(seen, query, kv, kv, grad, out_t, lse)


def vocab_ids(step, block, vocab):
    ids = lax.broadcasted_iota(jnp.int32, (block, 1), 0) + step * block
    valid = ids < vocab
    return jnp.where(valid, ids, 2**30), valid


def head_stats_kernel(emb_ref, n_ref, target_ref, stats_ref, expo_ref, tops_ref, nt_ref, run_ref, *, vocab, block, rows, scale):
    step = pl.program_id(0)
    ids, valid = vocab_ids(step, block, vocab)
    emb = jnp.transpose(emb_ref[...])
    total = n_ref.shape[0]

    @pl.when(step == 0)
    def _():
        run_ref[0:1, :] = jnp.full((1, total), MASKED, F32)
        run_ref[1:8, :] = jnp.zeros((7, total), F32)
        for first in range(0, total, rows):
            nt_ref[:, first : first + rows] = jnp.transpose(n_ref[first : first + rows, :])

    for first in range(0, total, rows):
        columns = slice(first, first + rows)
        logits = jnp.dot(emb, nt_ref[:, columns], preferred_element_type=F32) * (scale / LN2)
        logits = jnp.where(valid, logits, MASKED)
        top = run_ref[0:1, columns]
        new_top = jnp.maximum(top, jnp.max(logits, axis=0, keepdims=True))
        expo = jnp.exp2(logits - new_top)
        expo_ref[:, columns] = expo.astype(BF)
        run_ref[0:1, columns] = new_top
        run_ref[1:2, columns] = run_ref[1:2, columns] * jnp.exp2(top - new_top) + jnp.sum(expo, axis=0, keepdims=True)
        run_ref[2:3, columns] += jnp.sum(jnp.where(ids == target_ref[:, columns], logits, 0.0), axis=0, keepdims=True)
    tops_ref[pl.ds(step, 1), :] = run_ref[0:1, :] * LN2

    @pl.when(step == pl.num_programs(0) - 1)
    def _():
        lines = total // 128
        for k in range(3):
            for i in range(lines):
                part = run_ref[k : k + 1, i * 128 : (i + 1) * 128]
                stats_ref[k * lines + i : k * lines + i + 1, :] = part if k == 1 else part * LN2


def head_stats(emb_t, normed, target, vocab, block, rows):
    total, depth = normed.shape
    steps = emb_t.shape[1] // block
    lines = (steps + 7) // 8 * 8
    return pl.pallas_call(
        partial(head_stats_kernel, vocab=vocab, block=block, rows=rows, scale=depth**-0.5),
        grid=(steps,),
        in_specs=[
            pl.BlockSpec((depth, block), lambda i: (0, i)),
            pl.BlockSpec((total, depth), lambda i: (0, 0)),
            pl.BlockSpec((1, total), lambda i: (0, 0)),
        ],
        out_specs=[
            pl.BlockSpec((3 * total // 128, 128), lambda i: (0, 0)),
            pl.BlockSpec((block, total), lambda i: (i, 0)),
            pl.BlockSpec((lines, total), lambda i: (0, 0)),
        ],
        out_shape=(
            jax.ShapeDtypeStruct((3 * total // 128, 128), F32),
            jax.ShapeDtypeStruct((steps * block, total), BF),
            jax.ShapeDtypeStruct((lines, total), F32),
        ),
        scratch_shapes=[pltpu.VMEM((depth, total), BF), pltpu.VMEM((8, total), F32)],
        compiler_params=pltpu.CompilerParams(vmem_limit_bytes=VMEM_LIMIT),
        cost_estimate=pl.CostEstimate(
            flops=2 * vocab * depth * total, transcendentals=vocab * total,
            bytes_accessed=2 * vocab * depth + 2 * depth * total + 2 * vocab * total,
        ),
        name="head_stats",
    )(emb_t, normed, target)


def head_back_kernel(
    emb_ref, expo_ref, tops_ref, n_ref, target_ref, lse_ref, de_ref, dn_ref, dnt_acc, *, vocab, block, rows, scale
):
    step = pl.program_id(0)
    ids, valid = vocab_ids(step, block, vocab)
    factor = jnp.exp(tops_ref[pl.ds(step, 1), :] - lse_ref[...])

    @pl.when(step == 0)
    def _():
        dnt_acc[...] = jnp.zeros_like(dnt_acc)

    de = None
    for first in range(0, n_ref.shape[0], rows):
        columns = slice(first, first + rows)
        probs = expo_ref[:, columns].astype(F32) * factor[:, columns]
        grad = jnp.where(ids == target_ref[:, columns], probs - 1.0, probs).astype(BF)
        term = jnp.dot(grad, n_ref[columns, :], preferred_element_type=F32)
        de = term if de is None else de + term
        dnt_acc[:, columns] += jnp.dot(emb_ref[...], grad, preferred_element_type=F32)
    de_ref[...] = jnp.transpose((de * scale).astype(BF))

    @pl.when(step == pl.num_programs(0) - 1)
    def _():
        dn_ref[...] = (jnp.transpose(dnt_acc[...]) * scale).astype(BF)


def head_back(emb_t, expo, tops, normed, target, lse, vocab, block, rows):
    total, depth = normed.shape
    steps = emb_t.shape[1] // block
    return pl.pallas_call(
        partial(head_back_kernel, vocab=vocab, block=block, rows=rows, scale=depth**-0.5),
        grid=(steps,),
        in_specs=[
            pl.BlockSpec((depth, block), lambda i: (0, i)),
            pl.BlockSpec((block, total), lambda i: (i, 0)),
            pl.BlockSpec(tops.shape, lambda i: (0, 0)),
            pl.BlockSpec((total, depth), lambda i: (0, 0)),
            pl.BlockSpec((1, total), lambda i: (0, 0)),
            pl.BlockSpec((1, total), lambda i: (0, 0)),
        ],
        out_specs=[
            pl.BlockSpec((depth, block), lambda i: (0, i)),
            pl.BlockSpec((total, depth), lambda i: (0, 0)),
        ],
        out_shape=(
            jax.ShapeDtypeStruct(emb_t.shape, BF),
            jax.ShapeDtypeStruct((total, depth), BF),
        ),
        scratch_shapes=[pltpu.VMEM((depth, total), F32)],
        compiler_params=pltpu.CompilerParams(vmem_limit_bytes=VMEM_LIMIT),
        cost_estimate=pl.CostEstimate(
            flops=4 * vocab * depth * total, transcendentals=0,
            bytes_accessed=4 * vocab * depth + 6 * depth * total + 2 * vocab * total,
        ),
        name="head_back",
    )(emb_t, expo, tops, normed, target, lse)


MESH = pl.DeviceIdType.MESH


class Peers:
    def __init__(self):
        self.s, self.c, self.t = (lax.axis_index(name) for name in ("shard", "ctx", "tp"))
        s, c, t = self.s, self.c, self.t
        self.sx = s + 1 - 2 * lax.rem(s, 2)
        self.sy = lax.rem(s + 2, 4)
        self.sd = lax.rem(self.sx + 2, 4)
        self.x = (self.sx, c, t)
        self.y = (self.sy, c, t)
        self.d = (self.sd, c, t)
        self.core = (s, 1 - c, t)
        self.z = [(s, c, lax.rem(t + k, 4)) for k in range(4)]
        self.z_other = [(s, 1 - c, lax.rem(t + k, 4)) for k in range(4)]
        self.group = self.z[1:] + self.z_other


def meet(peers):
    barrier = pltpu.get_barrier_semaphore()
    for peer in peers:
        pl.semaphore_signal(barrier, inc=1, device_id=peer, device_id_type=MESH)
    pl.semaphore_wait(barrier, len(peers))


class Pool:
    def __init__(self, sends, arrivals):
        self.sends, self.arrivals, self.count = sends, arrivals, 0

    def take(self, count):
        first = self.count
        self.count += count
        return first

    def copy(self, index, peer, source, target):
        return pltpu.make_async_remote_copy(
            src_ref=source, dst_ref=target, send_sem=self.sends.at[index],
            recv_sem=self.arrivals.at[index], device_id=peer, device_id_type=MESH,
        )


class Sender:
    def __init__(self, pool):
        self.pool, self.all = pool, []

    def to(self, peer, source, target):
        copy = self.pool.copy(self.pool.take(1), peer, source, target)
        self.all.append(copy)
        copy.start()
        return copy

    def finish(self):
        for copy in self.all:
            copy.wait_send()


class RowLine:
    def __init__(self, pool, me, own, everyone, rows, pieces=2):
        self.pool, self.me, self.own, self.everyone = pool, me, own, everyone
        self.rows, self.pieces, self.sub = rows, pieces, rows // pieces
        self.first = pool.take(13 * pieces)

    def block(self, chip, piece):
        return self.everyone.at[pl.ds((self.me.c * 4 + chip) * self.rows + piece * self.sub, self.sub)]

    def source(self, own, chip, piece):
        return self.own.at[pl.ds(piece * self.sub, self.sub)] if own else self.block(chip, piece)

    def make(self, slot, piece, peer, chip, own=False):
        index = self.first + slot * self.pieces + piece
        return self.pool.copy(index, peer, self.source(own, chip, piece), self.block(chip, piece))

    def right(self, k, piece):
        return self.make(k, piece, self.me.z[1], self.me.t - k, k == 0)

    def left(self, k, piece):
        return self.make(3 + k, piece, self.me.z[3], self.me.t + k, k == 0)

    def across(self, slot, piece, chip, own=False):
        return self.make(6 + slot, piece, self.me.core, chip, own)

    def begin(self):
        t = self.me.t
        for p in range(self.pieces):
            pl.when(t < 3)(lambda: self.right(0, p).start())
            pl.when(t > 0)(lambda: self.left(0, p).start())
        for p in range(self.pieces):
            self.across(0, p, t, True).start()

    def step(self, k):
        t = self.me.t
        for p in range(self.pieces):

            @pl.when(t > k)
            def _():
                chip = t - 1 - k
                self.make(k, p, self.me.z[1], chip).wait_recv()
                if k < 2:
                    pl.when(t < 3)(lambda: self.right(k + 1, p).start())
                self.across(1 + k, p, chip).start()

            @pl.when(t + k < 3)
            def _():
                chip = t + 1 + k
                self.make(3 + k, p, self.me.z[3], chip).wait_recv()
                if k < 2:
                    pl.when(t > 0)(lambda: self.left(k + 1, p).start())
                self.across(4 + k, p, chip).start()

    def finish(self):
        t = self.me.t
        for p in range(self.pieces):
            pl.when(t < 3)(lambda: self.right(0, p).wait_send())
            pl.when(t > 0)(lambda: self.left(0, p).wait_send())
            self.across(0, p, t, True).wait()
            for k in range(3):

                @pl.when(t > k)
                def _():
                    if k < 2:
                        pl.when(t < 3)(lambda: self.right(k + 1, p).wait_send())
                    self.across(1 + k, p, t - 1 - k).wait()

                @pl.when(t + k < 3)
                def _():
                    if k < 2:
                        pl.when(t > 0)(lambda: self.left(k + 1, p).wait_send())
                    self.across(4 + k, p, t + 1 + k).wait()


class BlockLine:
    def __init__(self, pool, me, own, take, pieces=2):
        self.pool, self.me, self.own, self.take = pool, me, own, take
        self.pieces, self.sub = pieces, own.shape[0] // pieces
        self.first = pool.take(4 * pieces)
        self.where = [(me.c + 1, 1 - me.c), (3 * me.c, me.c)]

    def make(self, lane, i, piece, peer):
        here = self.take.at[self.where[i][1], pl.ds(piece * self.sub, self.sub)]
        return self.pool.copy(self.first + (2 * lane + i) * self.pieces + piece, peer, here, here)

    def right(self, i, piece):
        return self.make(0, i, piece, self.me.z[1])

    def left(self, i, piece):
        return self.make(1, i, piece, self.me.z[3])

    def begin(self):
        t = self.me.t
        for i, (block, slot) in enumerate(self.where):

            @pl.when(t == block)
            def _():
                self.take[slot] = self.own[...]
                for p in range(self.pieces):
                    pl.when(t < 3)(lambda: self.right(i, p).start())
                    pl.when(t > 0)(lambda: self.left(i, p).start())

    def arrive(self, distance):
        t = self.me.t
        for i, (block, slot) in enumerate(self.where):

            @pl.when(t - block == distance)
            def _():
                for p in range(self.pieces):
                    self.right(i, p).wait_recv()
                    pl.when(t < 3)(lambda: self.right(i, p).start())

            @pl.when(block - t == distance)
            def _():
                for p in range(self.pieces):
                    self.left(i, p).wait_recv()
                    pl.when(t > 0)(lambda: self.left(i, p).start())

    def finish(self):
        t = self.me.t
        for i, (block, slot) in enumerate(self.where):
            for p in range(self.pieces):
                pl.when((t >= block) & (t < 3))(lambda: self.right(i, p).wait_send())
                pl.when((t <= block) & (t > 0))(lambda: self.left(i, p).wait_send())


class SumLine:
    def __init__(self, pool, me, own, coming, going, pieces=2):
        self.pool, self.me, self.own, self.coming, self.going = pool, me, own, coming, going
        self.pieces, self.sub = pieces, own.shape[1] // pieces
        self.first = pool.take(6 * pieces)

    def copy(self, slot, piece, source):
        here = pl.ds(piece * self.sub, self.sub)
        peer = self.me.z[1] if slot < 3 else self.me.z[3]
        return self.pool.copy(
            self.first + slot * self.pieces + piece, peer, source.at[here], self.coming.at[slot, here]
        )

    def dest(self, slot):
        return 3 - slot if slot < 3 else slot - 3

    def direct(self, slot):
        return self.me.t == (0 if slot < 3 else 3)

    def start(self):
        for slot in (0, 3, 1, 4, 2, 5):

            @pl.when(self.direct(slot))
            def _():
                for p in range(self.pieces):
                    self.copy(slot, p, self.own.at[self.dest(slot)]).start()

    passing = ((0, 1), (3, 2), (1, 1), (4, 2), (0, 2), (3, 1))

    def add(self, part):
        for slot, chip in self.passing[2 * part : 2 * part + 2]:

            @pl.when(self.me.t == chip)
            def _():
                for p in range(self.pieces):
                    here = pl.ds(p * self.sub, self.sub)
                    self.copy(slot, p, self.going.at[slot]).wait_recv()
                    self.going[slot, here] = (
                        self.own[self.dest(slot), here].astype(F32) + self.coming[slot, here].astype(F32)
                    ).astype(BF)
                    self.copy(slot, p, self.going.at[slot]).start()

    def result(self, out):
        t = self.me.t
        for slot in range(6):

            @pl.when(t == self.dest(slot))
            def _():
                for p in range(self.pieces):
                    self.copy(slot, p, self.going.at[slot]).wait_recv()

        out[...] = self.own[t].astype(F32)

        @pl.when(t > 0)
        def _():
            out[...] += self.coming[3 - t].astype(F32)

        @pl.when(t < 3)
        def _():
            out[...] += self.coming[3 + t].astype(F32)

    def finish(self):
        for slot in range(6):

            @pl.when(self.direct(slot))
            def _():
                for p in range(self.pieces):
                    self.copy(slot, p, self.own.at[self.dest(slot)]).wait_send()

        for slot, chip in self.passing:

            @pl.when(self.me.t == chip)
            def _():
                for p in range(self.pieces):
                    self.copy(slot, p, self.going.at[slot]).wait_send()


class GradLine:
    def __init__(self, pool, me, own, coming, going, shared, pieces=2):
        self.pool, self.me, self.own, self.coming, self.going, self.shared = pool, me, own, coming, going, shared
        self.pieces, self.sub = pieces, own.shape[1] // pieces
        self.first = pool.take(4 * pieces + 1)
        self.home = me.c == me.t // 2

    def here(self, piece):
        return pl.ds(piece * self.sub, self.sub)

    def copy(self, slot, source, piece):
        peer = self.me.z[1] if slot < 2 else self.me.z[3]
        here = self.here(piece)
        return self.pool.copy(
            self.first + slot * self.pieces + piece, peer, source.at[here], self.coming.at[slot, here]
        )

    def index(self, slot):
        return (1, 0, 0, 1)[slot]

    def block(self, slot):
        return 2 * self.me.c + self.index(slot)

    def direct(self, slot):
        t = self.me.t
        return (t == 0) & (self.block(slot) > 0) if slot < 2 else (t == 3) & (self.block(slot) < 3)

    def start(self):
        for slot in (0, 2, 1, 3):
            for p in range(self.pieces):
                pl.when(self.direct(slot))(lambda: self.copy(slot, self.own.at[self.index(slot)], p).start())

    passing = ((0, 1), (2, 2), (1, 1), (3, 2), (0, 2), (2, 1))

    def adds(self, slot, chip):
        return (self.me.t == chip) & ((chip < self.block(slot)) if slot < 2 else (chip > self.block(slot)))

    def add(self, part):
        for slot, chip in self.passing[2 * part : 2 * part + 2]:

            @pl.when(self.adds(slot, chip))
            def _():
                for p in range(self.pieces):
                    here = self.here(p)
                    self.copy(slot, self.going.at[slot], p).wait_recv()
                    self.going[slot, here] = (
                        self.own[self.index(slot), here].astype(F32) + self.coming[slot, here].astype(F32)
                    ).astype(BF)
                    self.copy(slot, self.going.at[slot], p).start()

    def share(self):
        return self.pool.copy(self.first + 4 * self.pieces, self.me.core, self.shared, self.shared)

    def settle(self, total):
        t = self.me.t

        for slot in range(4):
            ends = (t == self.block(slot)) & (t > 0 if slot < 2 else t < 3)
            for p in range(self.pieces):
                pl.when(ends)(lambda: self.copy(slot, self.going.at[slot], p).wait_recv())

        @pl.when(self.home)
        def _():
            j = lax.rem(t, 2)
            total[...] = self.own[j].astype(F32)

            @pl.when(t > 0)
            def _():
                total[...] += self.coming[1 - j].astype(F32)

            @pl.when(t < 3)
            def _():
                total[...] += self.coming[2 + j].astype(F32)

            self.shared[...] = total[...].astype(BF)
            self.share().start()

    def finish(self):
        for slot in range(4):
            for p in range(self.pieces):
                pl.when(self.direct(slot))(lambda: self.copy(slot, self.own.at[self.index(slot)], p).wait_send())
        for slot, chip in self.passing:
            for p in range(self.pieces):
                pl.when(self.adds(slot, chip))(lambda: self.copy(slot, self.going.at[slot], p).wait_send())
        pl.when(self.home)(lambda: self.share().wait_send())
        pl.when(jnp.logical_not(self.home))(lambda: self.share().wait_recv())


def start_kernel(
    gains_ref, x_ref, e_ref, g_ref, t_ref, b0, b1, b2, gains_out, n_all, e_all, n_pair, x_pair, g_pair, t_pair, w0, w1, mix2,
    gain_slots, n_ref, take0, take1, take2, mix0, mix1, sends, arrivals, local, *, cuts,
):
    me = Peers()
    meet([me.z[1], me.z[3], me.core, me.x, me.y, me.d])
    pool = Pool(sends, arrivals)
    send = Sender(pool)
    rows = x_ref.shape[0]
    locals_ = []

    def copy_here(source, target):
        copy = pltpu.make_async_copy(source, target, local.at[len(locals_)])
        copy.start()
        locals_.append(copy)

    gain_slots[me.s] = gains_ref[...]
    gain_copies = [send.to(peer, gains_ref, gain_slots.at[me.s]) for peer in (me.x, me.y, me.d)]
    bundles = [(b0, take0, mix0), (b1, take1, mix1), (b2, take2, mix2)]
    lines = [BlockLine(pool, me, block, take) for block, take, mix in bundles]

    def interleave(i):
        block, take, mix = bundles[i]
        first = take[0]
        second = take[1]
        columns = []
        for start, stop in cuts[i]:
            columns += [first[:, start:stop], second[:, start:stop]]
        mix[...] = jnp.concatenate(columns, axis=1)

    depth = b0.shape[0]
    half = depth // 2
    mine = pl.ds(me.s * depth, depth)

    def share(i, w):
        mix = bundles[i][2]
        copy_here(mix, w.at[mine])
        return send.to(me.x, mix, w.at[mine]), send.to(me.y, mix, w.at[mine])

    onward = []

    def pass_on(to_x, to_y, x_part, y_part):
        to_x.wait_recv()
        onward.append(send.to(me.y, x_part, x_part))
        to_y.wait_recv()
        onward.append(send.to(me.x, y_part, y_part))

    def pass_weights(over, w):
        pass_on(*over, w.at[pl.ds(me.sx * depth, half)], w.at[pl.ds(me.sy * depth + half, half)])

    lines[0].begin()
    lines[1].begin()
    for copy in gain_copies:
        copy.wait_recv()
    width = x_ref.shape[1] // 4
    gains = jnp.concatenate([gain_slots[i][:, :width] for i in range(4)], axis=1)
    gains_out[...] = gains
    n_ref[...] = normalize(x_ref[...].astype(F32), gains[0:1])[0].astype(BF)
    n_line = RowLine(pool, me, n_ref, n_all, rows)
    e_line = RowLine(pool, me, e_ref, e_all, rows)
    n_line.begin()
    copy_here(n_ref, n_all.at[pl.ds((me.c * 4 + me.t) * rows, rows)])
    copy_here(e_ref, e_all.at[pl.ds((me.c * 4 + me.t) * rows, rows)])
    swapped = []
    for ref, pair in ((n_ref, n_pair), (x_ref, x_pair), (g_ref, g_pair), (t_ref, t_pair)):
        where = pair.at[pl.ds(me.c * ref.shape[0], ref.shape[0])]
        swapped.append(send.to(me.core, ref, where))
        copy_here(ref, where)
    lines[0].arrive(1)
    lines[1].arrive(1)
    lines[0].arrive(2)
    lines[1].arrive(2)
    n_line.step(0)
    lines[0].arrive(3)
    interleave(0)
    over0 = share(0, w0)
    lines[1].arrive(3)
    interleave(1)
    over1 = share(1, w1)
    lines[2].begin()
    e_line.begin()
    n_line.step(1)
    n_line.step(2)
    lines[2].arrive(1)
    e_line.step(0)
    pass_weights(over0, w0)
    lines[2].arrive(2)
    e_line.step(1)
    pass_weights(over1, w1)
    lines[2].arrive(3)
    e_line.step(2)
    interleave(2)
    for copy in onward + swapped:
        copy.wait_recv()
    for line in lines + [n_line, e_line]:
        line.finish()
    send.finish()
    for copy in locals_:
        copy.wait()


def start_gather(gains, inputs, encoder, cotangent, targets, bundles, cuts):
    rows, depth = inputs.shape
    part = bundles[0].shape[0]
    any_space = pl.BlockSpec(memory_space=pl.ANY)
    vmem = pl.BlockSpec(memory_space=pltpu.VMEM)
    return pl.pallas_call(
        partial(start_kernel, cuts=cuts),
        in_specs=[vmem] * 8,
        out_specs=[vmem] + [any_space] * 8 + [vmem],
        out_shape=[
            jax.ShapeDtypeStruct((gains.shape[0], depth), F32),
            jax.ShapeDtypeStruct((8 * rows, depth), BF),
            jax.ShapeDtypeStruct((8 * rows, depth), BF),
        ]
        + [jax.ShapeDtypeStruct((2 * a.shape[0], a.shape[1]), a.dtype) for a in (inputs, inputs, cotangent, targets)]
        + [jax.ShapeDtypeStruct((4 * part, 2 * b.shape[1]), BF) for b in bundles[:2]]
        + [jax.ShapeDtypeStruct((part, 2 * bundles[2].shape[1]), BF)],
        scratch_shapes=[pltpu.VMEM((4,) + gains.shape, F32), pltpu.VMEM((rows, depth), BF)]
        + [pltpu.VMEM((2,) + b.shape, BF) for b in bundles]
        + [pltpu.VMEM((part, 2 * b.shape[1]), BF) for b in bundles[:2]]
        + [pltpu.SemaphoreType.DMA((96,)), pltpu.SemaphoreType.DMA((96,)), pltpu.SemaphoreType.DMA((16,))],
        compiler_params=pltpu.CompilerParams(collective_id=0, has_side_effects=True, vmem_limit_bytes=VMEM_LIMIT),
        name="start_gather",
    )(gains, inputs, encoder, cotangent, targets, *bundles)


def rows_kernel(n_ref, n_all, sends, arrivals, local):
    me = Peers()
    meet([me.z[1], me.z[3], me.core])
    rows = n_ref.shape[0]
    copy = pltpu.make_async_copy(n_ref, n_all.at[pl.ds((me.c * 4 + me.t) * rows, rows)], local)
    copy.start()
    line = RowLine(Pool(sends, arrivals), me, n_ref, n_all, rows)
    line.begin()
    for k in range(3):
        line.step(k)
    line.finish()
    copy.wait()


def gather_rows(normed):
    rows, depth = normed.shape
    return pl.pallas_call(
        rows_kernel,
        in_specs=[pl.BlockSpec(memory_space=pltpu.VMEM)],
        out_specs=pl.BlockSpec(memory_space=pl.ANY),
        out_shape=jax.ShapeDtypeStruct((8 * rows, depth), normed.dtype),
        scratch_shapes=[pltpu.SemaphoreType.DMA((26,)), pltpu.SemaphoreType.DMA((26,)), pltpu.SemaphoreType.DMA],
        compiler_params=pltpu.CompilerParams(collective_id=1, has_side_effects=True, vmem_limit_bytes=VMEM_LIMIT),
        name="gather_rows",
    )(normed)


def stats_kernel(stats_ref, out_ref, slots, sends, arrivals):
    me = Peers()
    meet(me.group)
    send = Sender(Pool(sends, arrivals))
    here = slots.at[me.c * 4 + me.t]
    slots[me.c * 4 + me.t] = stats_ref[...]
    copies = [send.to(peer, stats_ref, here) for peer in me.group]
    for copy in copies:
        copy.wait_recv()
    lines = stats_ref.shape[0] // 3
    top = slots[0, 0:lines]
    for i in range(1, 8):
        top = jnp.maximum(top, slots[i, 0:lines])
    total = jnp.zeros_like(top)
    picked = jnp.zeros_like(top)
    for i in range(8):
        total += slots[i, lines : 2 * lines] * jnp.exp(slots[i, 0:lines] - top)
        picked += slots[i, 2 * lines : 3 * lines]
    logsum = top + jnp.log(total)
    out_ref[0] = logsum
    out_ref[1] = logsum - picked
    send.finish()


def combine_stats(stats):
    return pl.pallas_call(
        stats_kernel,
        in_specs=[pl.BlockSpec(memory_space=pltpu.VMEM)],
        out_specs=pl.BlockSpec(memory_space=pltpu.VMEM),
        out_shape=jax.ShapeDtypeStruct((2, stats.shape[0] // 3, stats.shape[1]), F32),
        scratch_shapes=[pltpu.VMEM((8,) + stats.shape, F32), pltpu.SemaphoreType.DMA((8,)), pltpu.SemaphoreType.DMA((8,))],
        compiler_params=pltpu.CompilerParams(collective_id=2, has_side_effects=True),
        name="combine_stats",
    )(stats)


def settle_first(send, me, part_ref, other, half):
    return send.to(me.core, part_ref.at[pl.ds((1 - me.c) * half, half)], other)


def settle_second(me, part_ref, other, summed, rows):
    half = 4 * rows
    for k in range(4):
        summed[k] = (
            part_ref[pl.ds(me.c * half + k * rows, rows)].astype(F32) + other[k * rows : (k + 1) * rows].astype(F32)
        ).astype(BF)


class Planar:
    def __init__(self, send, me, part, first, second, moving, chunks):
        self.send, self.me, self.part = send, me, part
        self.first, self.second, self.moving, self.chunks = first, second, moving, chunks

    def begin(self):
        me = self.me
        self.one = []
        for start, stop, along_x in self.chunks:
            here = slice(start, stop)
            near, near_block = (me.x, me.sx) if along_x else (me.y, me.sy)
            self.one.append(
                (
                    self.send.to(near, self.part.at[me.sd, here], self.first.at[1, here]),
                    self.send.to(near, self.part.at[near_block, here], self.first.at[0, here]),
                )
            )

    def gather(self, i):
        me = self.me
        start, stop, along_x = self.chunks[i]
        here = slice(start, stop)
        self.one[i][0].wait_recv()
        self.moving[here] = (
            self.part[me.sy if along_x else me.sx, here].astype(F32) + self.first[1, here].astype(F32)
        ).astype(BF)
        return here

    def own(self, i):
        start, stop, along_x = self.chunks[i]
        here = slice(start, stop)
        self.one[i][1].wait_recv()
        return self.part[self.me.s, here].astype(F32) + self.first[0, here].astype(F32)

    def go_on(self):
        self.two = []
        for start, stop, along_x in self.chunks:
            here = slice(start, stop)
            self.two.append(
                self.send.to(self.me.y if along_x else self.me.x, self.moving.at[here], self.second.at[here])
            )

    def middle(self):
        for i in range(len(self.chunks)):
            self.gather(i)
        self.go_on()

    def end(self, store):
        for i, copy in enumerate(self.two):
            start, stop, along_x = self.chunks[i]
            here = slice(start, stop)
            copy.wait_recv()
            store(here, self.own(i) + self.second[here].astype(F32))


def halves(count, parts, step):
    middle = (count // 2 + step - 1) // step * step
    out = []
    for low, high, along_x in ((0, middle, True), (middle, count, False)):
        size = ((high - low) // parts + step - 1) // step * step
        edges = list(range(low, high, size)) + [high]
        out.append([(a, b, along_x) for a, b in zip(edges[:-1], edges[1:])])
    return [chunk for pair in zip(*out) for chunk in pair]


def middle_kernel(dn_ref, de_ref, gn_ref, own_ref, move_ref, other, summed, coming, going, total, first, sends, arrivals, *, chunks):
    me = Peers()
    meet([me.z[1], me.z[3], me.core, me.x, me.y])
    pool = Pool(sends, arrivals)
    send = Sender(pool)
    rows = summed.shape[1]
    crossing = settle_first(send, me, dn_ref, other, 4 * rows)
    plane = Planar(send, me, de_ref, first, None, move_ref, chunks)
    plane.begin()
    crossing.wait_recv()
    settle_second(me, dn_ref, other, summed, rows)
    line = SumLine(pool, me, summed, coming, going)
    line.start()
    for part in range(3):
        line.add(part)
    line.result(total)
    own = pl.ds(me.c * rows, rows)
    gn_ref[own] = total[...].astype(BF)
    share = send.to(me.core, gn_ref.at[own], gn_ref.at[own])
    for i in range(len(chunks)):
        here = plane.gather(i)
        own_ref[here] = plane.own(i).astype(BF)
    share.wait_recv()
    line.finish()
    send.finish()


def middle_scatter(dn, de):
    total, depth = dn.shape
    rows = total // 8
    groups, part, wide = de.shape
    chunks = halves(part, 3, 16)
    count = 14 + 2 * len(chunks)
    vmem = pl.BlockSpec(memory_space=pltpu.VMEM)
    return pl.pallas_call(
        partial(middle_kernel, chunks=chunks),
        in_specs=[vmem] * 2,
        out_specs=[vmem] * 3,
        out_shape=[
            jax.ShapeDtypeStruct((2 * rows, depth), BF),
            jax.ShapeDtypeStruct((part, wide), BF),
            jax.ShapeDtypeStruct((part, wide), BF),
        ],
        scratch_shapes=[
            pltpu.VMEM((4 * rows, depth), BF),
            pltpu.VMEM((4, rows, depth), BF),
            pltpu.VMEM((6, rows, depth), BF),
            pltpu.VMEM((6, rows, depth), BF),
            pltpu.VMEM((rows, depth), F32),
            pltpu.VMEM((2, part, wide), BF),
            pltpu.SemaphoreType.DMA((count,)),
            pltpu.SemaphoreType.DMA((count,)),
        ],
        compiler_params=pltpu.CompilerParams(collective_id=3, has_side_effects=True, vmem_limit_bytes=VMEM_LIMIT),
        name="middle_scatter",
    )(dn, de)


def tail_kernel(
    dn_ref, c0, c1, c2, c3, s0, s1, s2, s3, f_ref, gains_ref, eo_ref, em_ref,
    dn_out, held0, held1, held2, gain_out, e_sum, g0, g1, e_second, other, summed, coming, going, first0, second0, moving0, first1, second1, moving1,
    ab0, ab1, ab2, in0, in1, in2, out0, out1, out2, sum0, sum1, sum2, slots, plane_sum, plane_slots, sends, arrivals, *, cuts, chunks,
):
    me = Peers()
    meet(me.group + [me.x, me.y, me.d])
    pool = Pool(sends, arrivals)
    send = Sender(pool)
    rows = summed.shape[1]
    crossing = settle_first(send, me, dn_ref, other, 4 * rows)
    planes = [
        Planar(send, me, g0, first0, second0, moving0, chunks),
        Planar(send, me, g1, first1, second1, moving1, chunks),
    ]

    def collect(target, pieces):
        for i, piece in enumerate(pieces):
            target[:, :, i * piece.shape[2] : (i + 1) * piece.shape[2]] = piece[...]

    def split(value, cut):
        return [
            jnp.concatenate([value[:, 2 * a + i * (b - a) : 2 * a + (i + 1) * (b - a)] for a, b in cut], axis=1).astype(BF)
            for i in range(2)
        ]

    collect(g0, (c0, c1, c2, c3))
    planes[0].begin()
    ff_line = GradLine(pool, me, ab2, in2, out2, held2)
    lines = [GradLine(pool, me, ab0, in0, out0, held0), GradLine(pool, me, ab1, in1, out1, held1)]
    for i, half in enumerate(split(f_ref[...], cuts[2])):
        ab2[i] = half
    ff_line.start()
    crossing.wait_recv()
    settle_second(me, dn_ref, other, summed, rows)
    row_line = SumLine(pool, me, summed, coming, going)
    row_line.start()
    collect(g1, (s0, s1, s2, s3))
    planes[1].begin()
    slots[me.c * 4 + me.t] = gains_ref[...]
    gain_copies = [send.to(peer, gains_ref, slots.at[me.c * 4 + me.t]) for peer in me.group]
    ff_line.add(0)
    row_line.add(0)
    planes[0].middle()
    ff_line.add(1)
    row_line.add(1)
    planes[1].middle()
    ff_line.add(2)
    row_line.add(2)
    e_copies = [
        send.to(me.y if along_x else me.x, em_ref.at[start:stop], e_second.at[start:stop])
        for start, stop, along_x in halves(eo_ref.shape[0], 1, 16)
    ]
    for copy in gain_copies:
        copy.wait_recv()
    total = slots[0]
    for i in range(1, 8):
        total += slots[i]
    plane_sum[...] = total
    plane_slots[me.s] = total
    plane_copies = [send.to(peer, plane_sum, plane_slots.at[me.s]) for peer in (me.x, me.y, me.d)]
    for plane, cut, ab, line in ((planes[0], cuts[0], ab0, lines[0]), (planes[1], cuts[1], ab1, lines[1])):

        def store(here, value):
            for i, half in enumerate(split(value, cut)):
                ab[i, here] = half

        plane.end(store)
        line.start()
    for part in range(3):
        lines[0].add(part)
        lines[1].add(part)
    row_line.result(dn_out)
    ff_line.settle(sum2)
    for copy in e_copies:
        copy.wait_recv()
    e_sum[me.c] = (eo_ref[...].astype(F32) + e_second[...].astype(F32)).astype(BF)
    e_share = send.to(me.core, e_sum.at[me.c], e_sum.at[me.c])
    for copy in plane_copies:
        copy.wait_recv()
    gain_out[...] = plane_slots[0] + plane_slots[1] + plane_slots[2] + plane_slots[3]
    lines[0].settle(sum0)
    lines[1].settle(sum1)
    for line in (ff_line, lines[0], lines[1]):
        line.finish()
    e_share.wait_recv()
    row_line.finish()
    send.finish()


def tail_scatter(dn, grads, ff, gains, emb_own, emb_move, cuts):
    total, depth = dn.shape
    rows = total // 8
    groups, part, width = grads[0][0].shape
    width *= 4
    chunks = halves(part, 1, 16)
    vmem = pl.BlockSpec(memory_space=pltpu.VMEM)
    widths = [width // 2, width // 2, ff.shape[1] // 2]
    scratch = [
        pltpu.VMEM((groups, part, width), BF),
        pltpu.VMEM((groups, part, width), BF),
        pltpu.VMEM(emb_own.shape, BF),
        pltpu.VMEM((4 * rows, depth), BF),
        pltpu.VMEM((4, rows, depth), BF),
        pltpu.VMEM((6, rows, depth), BF),
        pltpu.VMEM((6, rows, depth), BF),
    ]
    for _ in grads:
        scratch += [pltpu.VMEM((2, part, width), BF), pltpu.VMEM((part, width), BF), pltpu.VMEM((part, width), BF)]
    for count in (2, 4, 4):
        scratch += [pltpu.VMEM((count, part, w), BF) for w in widths]
    scratch += [pltpu.VMEM((part, w), F32) for w in widths]
    scratch += [
        pltpu.VMEM((8,) + gains.shape, F32),
        pltpu.VMEM(gains.shape, F32),
        pltpu.VMEM((4,) + gains.shape, F32),
        pltpu.SemaphoreType.DMA((80,)),
        pltpu.SemaphoreType.DMA((80,)),
    ]
    return pl.pallas_call(
        partial(tail_kernel, cuts=cuts, chunks=chunks),
        in_specs=[vmem] * 13,
        out_specs=[vmem] * 6,
        out_shape=[jax.ShapeDtypeStruct((rows, depth), F32)]
        + [jax.ShapeDtypeStruct((part, w), BF) for w in widths]
        + [jax.ShapeDtypeStruct(gains.shape, F32), jax.ShapeDtypeStruct((2,) + emb_own.shape, BF)],
        scratch_shapes=scratch,
        compiler_params=pltpu.CompilerParams(collective_id=4, has_side_effects=True, vmem_limit_bytes=VMEM_LIMIT),
        name="tail_scatter",
    )(dn, *grads[0], *grads[1], ff, gains, emb_own, emb_move)


def finish_kernel(
    emb_ref, self_ref, cross_ref, ff_ref, x_ref, gh_ref, gn_ref, gain_ref, eg_ref, dx_ref, *outs
):
    half = eg_ref.shape[1] // 2
    for c in range(2):
        eg_ref[:, c * half : (c + 1) * half] = emb_ref[c, :, :half].astype(F32)
    x = x_ref[...].astype(F32)
    inverse = lax.rsqrt(jnp.mean(x * x, axis=-1, keepdims=True) + EPS)
    dx_ref[...] = gh_ref[...] + norm_back(x, inverse, gain_ref[...], gn_ref[...])
    index = 0
    for ref, count in ((self_ref, 4), (cross_ref, 4), (ff_ref, 3)):
        size = ref.shape[1] // count
        for k in range(count):
            outs[index][...] = ref[:, k * size : (k + 1) * size].astype(F32)
            index += 1


def finish(emb, own_self, own_cross, own_ff, x, grad_hidden, gn, gain, vocab):
    part, width = own_self.shape
    shapes = []
    for total, count in ((width, 4), (width, 4), (own_ff.shape[1], 3)):
        shapes += [(part, total // count)] * count
    ins = (emb, own_self, own_cross, own_ff, x, grad_hidden, gn, gain)
    vmem = pl.BlockSpec(memory_space=pltpu.VMEM)
    return pl.pallas_call(
        finish_kernel,
        in_specs=[vmem] * len(ins),
        out_specs=[vmem] * (2 + len(shapes)),
        out_shape=[jax.ShapeDtypeStruct((part, vocab), F32), jax.ShapeDtypeStruct(x.shape, F32)]
        + [jax.ShapeDtypeStruct(shape, F32) for shape in shapes],
        compiler_params=pltpu.CompilerParams(vmem_limit_bytes=VMEM_LIMIT),
        name="finish",
    )(*ins)


def normalize(hidden, gain):
    inverse = lax.rsqrt(jnp.mean(hidden * hidden, axis=-1, keepdims=True) + EPS)
    return (hidden * inverse * gain, inverse)


def norm_back(hidden, inverse, gain, upstream):
    scaled = upstream * gain
    inner = jnp.mean(scaled * hidden, axis=-1, keepdims=True)
    return inverse * scaled - hidden * (inverse * inverse * inverse) * inner


def matmul(left, right):
    return jnp.dot(left, right, preferred_element_type=F32)


def left_t(left, right):
    return jnp.einsum("ra,rb->ab", left, right, preferred_element_type=F32)


def right_t(left, right):
    return jnp.einsum("ra,ba->rb", left, right, preferred_element_type=F32)


def swap(array):
    return lax.ppermute(array, "ctx", [(0, 1), (1, 0)])


def per_device(
    inputs, encoder, prefix, targets, cotangent, gain_self, query_self, key_self, value_self, output_self,
    gain_cross, query_cross, key_cross, value_cross, output_cross, gain_hidden, gate_weight, up_weight,
    down_weight, gain_exit, embedding,
):
    tp = lax.axis_size("tp")
    ctx = lax.axis_size("ctx")
    shards = lax.axis_size("shard")
    assert tp == 4 and ctx == 2
    core = lax.axis_index("ctx")
    place = lax.axis_index("tp")
    rows, depth = inputs.shape
    group = rows * tp
    total = group * ctx
    hb = query_self.shape[1]
    width = 2 * hb
    fb = gate_weight.shape[1]
    pair = rows * ctx

    route_a = []
    route_b = []
    for c in range(2):
        for z in range(4):
            dest = c * 4 + z
            route_a.append(((z % 2) * 4 + 2 * c + z // 2, dest))
            route_b.append(((z % 2) * 4 + 2 * c + 1 - z // 2, dest))
    both = ("ctx", "tp")

    def spread_weights(parts):
        block = jnp.concatenate(parts, axis=1)
        first = lax.ppermute(block, both, route_a)
        second = lax.ppermute(block, both, route_b)
        columns = []
        start = 0
        for piece in parts:
            stop = start + piece.shape[1]
            columns += [first[:, start:stop], second[:, start:stop]]
            start = stop
        return lax.all_gather(jnp.concatenate(columns, axis=1), "shard", axis=0, tiled=True)

    def collect_weights(grad, widths):
        mine = lax.psum_scatter(grad, "shard", scatter_dimension=0, tiled=True)
        first = []
        second = []
        start = 0
        for size in widths:
            first.append(mine[:, start : start + size])
            second.append(mine[:, start + size : start + 2 * size])
            start += 2 * size
        back = lambda route: [(dest, source) for source, dest in route]
        one = lax.ppermute(jnp.concatenate(first, axis=1), both, back(route_a))
        two = lax.ppermute(jnp.concatenate(second, axis=1), both, back(route_b))
        part = (one.astype(F32) + two.astype(F32)).astype(BF)
        whole = part.astype(F32) + swap(part).astype(F32)
        outs = []
        start = 0
        for size in widths:
            outs.append(whole[:, start : start + size])
            start += size
        return outs

    def couple(own, other):
        return jnp.where(
            core == 0, jnp.concatenate([own, other], axis=0), jnp.concatenate([other, own], axis=0)
        )

    fast = shards == 4
    own_f = inputs.astype(F32)
    parts_self = [query_self, key_self, value_self, output_self.T]
    parts_cross = [query_cross, key_cross, value_cross, output_cross.T]
    parts_ff = [gate_weight, up_weight, down_weight.T]
    gain_parts = jnp.stack([gain_self, gain_cross, gain_hidden, gain_exit])
    cuts = [[(i * w, (i + 1) * w) for i in range(n)] for n, w in ((4, hb), (4, hb), (3, fb))]
    vocab_half = embedding.shape[0] // ctx
    vblock, rblock = 512, 512
    emb_mine = lax.dynamic_slice_in_dim(embedding.T, core * vocab_half, vocab_half, axis=1)
    emb_mine = jnp.pad(emb_mine, ((0, 0), (0, -vocab_half % vblock)))
    emb_t = lax.all_gather(emb_mine, "shard", axis=0, tiled=True)

    def take_pair(array):
        cut = array.reshape(ctx, group, depth)
        return lax.dynamic_slice_in_dim(cut, place * rows, rows, axis=1).reshape(pair, depth)

    if fast:
        bundles = [jnp.concatenate(parts, axis=1) for parts in (parts_self, parts_cross, parts_ff)]
        spare = -(depth // shards) % 128
        gain_block = jnp.pad(gain_parts.astype(F32), ((0, 4), (0, spare)))
        (
            gains, normed1, encoder_all, normed1_pair, x_pair, g_pair, t_pair, weights_self, weights_cross, ff_mix,
        ) = start_gather(
            gain_block, inputs, encoder, cotangent, targets.reshape(8, group // 8), bundles, cuts
        )
        hidden0 = x_pair.astype(F32)
        cotangent_pair = g_pair.astype(F32)
        targets_all = t_pair.reshape(total)
        ff_mix, emb_t = lax.optimization_barrier((ff_mix, emb_t))
        weights_ff = lax.all_gather(ff_mix, "shard", axis=0, tiled=True)
    else:
        gains = lax.all_gather(gain_parts, "shard", axis=1, tiled=True).astype(F32)
        normed1_own = normalize(own_f, gains[0])[0].astype(BF)
        normed1 = lax.all_gather(normed1_own, both, axis=0, tiled=True)
        normed1_pair = take_pair(normed1)
        encoder_all = lax.all_gather(encoder, both, axis=0, tiled=True)
        weights_self, weights_cross, weights_ff = map(spread_weights, (parts_self, parts_cross, parts_ff))
        hidden0 = couple(inputs, swap(inputs)).astype(F32)
        cotangent_pair = couple(cotangent, swap(cotangent)).astype(F32)
        targets_all = couple(targets, swap(targets))

    gain_one, gain_two, gain_three, gain_four = [gains[i] for i in range(4)]
    inverse1_own = normalize(own_f, gain_one)[1]
    query_w, key_w, value_w, out_w = [weights_self[:, i * width : (i + 1) * width] for i in range(4)]
    scale = HEAD_DIM**-0.5

    def project_q(normed, weight):
        return matmul(normed, weight).astype(BF) * jnp.asarray(scale, BF)

    positions = jnp.concatenate(
        [c * group + place * rows + jnp.arange(rows, dtype=jnp.int32) for c in range(2)]
    )
    limit = prefix[0]
    seen = jnp.maximum(positions + 1, limit)[None, :]
    causal_tiles = (((0, pair), (0, group), True), ((rows, pair), (group, total), True))
    open_tiles = (((0, pair), (0, total), False),)

    query1 = project_q(normed1_pair, query_w)
    kv1 = matmul(normed1, weights_self[:, width : 3 * width]).astype(BF)
    attended1, attended1_t, lse1 = attend(seen, query1, kv1, causal_tiles)

    def add_halves(partial_sum):
        part = partial_sum.astype(BF)
        return partial_sum + swap(part).astype(F32)

    hidden1 = hidden0 + add_halves(right_t(attended1, out_w))
    query2_w, key2_w, value2_w, out2_w = [weights_cross[:, i * width : (i + 1) * width] for i in range(4)]
    kv2 = matmul(encoder_all, weights_cross[:, width : 3 * width]).astype(BF)
    normed2, inverse2 = normalize(hidden1, gain_two)
    normed2 = normed2.astype(BF)
    query2 = project_q(normed2, query2_w)
    attended2, attended2_t, lse2 = attend(seen, query2, kv2, open_tiles)
    hidden2 = hidden1 + add_halves(right_t(attended2, out2_w))
    normed3, inverse3 = normalize(hidden2, gain_three)
    normed3 = normed3.astype(BF)
    gate_w, up_w, down_w = [weights_ff[:, i * 2 * fb : (i + 1) * 2 * fb] for i in range(3)]
    gate = matmul(normed3, gate_w)
    upper = matmul(normed3, up_w)
    active = jax.nn.gelu(gate, approximate=True)
    product = (active * upper).astype(BF)
    final = hidden2 + add_halves(right_t(product, down_w))
    normed4, inverse4 = normalize(final, gain_four)
    normed4 = normed4.astype(BF)

    def mine(array):
        return lax.dynamic_slice_in_dim(array, core * rows, rows, axis=0)

    final_own = mine(final)
    if fast:
        normed4_all = gather_rows(mine(normed4))
    else:
        normed4_all = lax.all_gather(mine(normed4), both, axis=0, tiled=True)
    local_target = (targets_all - (place * embedding.shape[0] + core * vocab_half))[None, :].astype(jnp.int32)
    stats, expo, tops = head_stats(emb_t, normed4_all, local_target, vocab_half, vblock, rblock)
    if fast:
        combined = combine_stats(stats)
        logsum = combined[0].reshape(total)
        loss = combined[1].reshape(total)
    else:
        every = lax.all_gather(stats.reshape(3, total), both, axis=0)
        top = jnp.max(every[:, 0], axis=0)
        summed = jnp.sum(every[:, 1] * jnp.exp(every[:, 0] - top[None]), axis=0)
        logsum = top + jnp.log(summed)
        loss = logsum - jnp.sum(every[:, 2], axis=0)
    exit_loss = lax.dynamic_slice_in_dim(loss, core * group, group, axis=0)
    emb_grad, grad_normed4 = head_back(
        emb_t, expo, tops, normed4_all, local_target, logsum[None, :], vocab_half, vblock, rblock
    )
    if fast:
        gn4, emb_own, emb_move = middle_scatter(grad_normed4, emb_grad.reshape(shards, depth // shards, -1))
        gn4 = gn4.astype(F32)
    else:
        emb_sum = lax.psum_scatter(emb_grad, "shard", scatter_dimension=0, tiled=True)
        emb_other = swap(emb_sum)
        gn4_own = lax.psum_scatter(grad_normed4, both, scatter_dimension=0, tiled=True)
        gn4 = couple(gn4_own, swap(gn4_own)).astype(F32)
    gain4_rows = gn4 * final * inverse4
    grad_final = cotangent_pair + norm_back(final, inverse4, gain_four, gn4)
    grad_final_b = grad_final.astype(BF)
    down_grad = left_t(grad_final_b, product).astype(BF)
    grad_product = matmul(grad_final_b, down_w)
    unused, gelu_pull = jax.vjp(partial(jax.nn.gelu, approximate=True), gate)
    grad_gate = gelu_pull(grad_product * upper)[0].astype(BF)
    grad_upper = (grad_product * active).astype(BF)
    gate_grad = left_t(normed3, grad_gate).astype(BF)
    upper_grad = left_t(normed3, grad_upper).astype(BF)
    ff_part = jnp.concatenate([gate_grad, upper_grad, down_grad], axis=1)
    gn3 = add_halves(right_t(grad_gate, gate_w) + right_t(grad_upper, up_w))
    gain3_rows = gn3 * hidden2 * inverse3
    grad_hidden2 = grad_final + norm_back(hidden2, inverse3, gain_three, gn3)
    grad_hidden2_b = grad_hidden2.astype(BF)
    out2_grad = left_t(grad_hidden2_b, attended2).astype(BF)
    grad_attended2 = matmul(grad_hidden2_b, out2_w).astype(BF)
    if fast:
        ff_mine = lax.psum_scatter(ff_part, "shard", scatter_dimension=0, tiled=True)
    grad_query2, grad_key2, grad_value2 = attend_back(
        seen, query2, kv2, grad_attended2, attended2_t, lse2, open_tiles
    )
    query2_grad = left_t(normed2, grad_query2).astype(BF)
    key2_grad = left_t(encoder_all, grad_key2).astype(BF)
    value2_grad = left_t(encoder_all, grad_value2).astype(BF)
    cross_parts = [query2_grad, key2_grad, value2_grad, out2_grad]
    encoder_part = (right_t(grad_key2, key2_w) + right_t(grad_value2, value2_w)).astype(BF)
    if fast:
        encoder_part, ff_mine = lax.optimization_barrier((encoder_part, ff_mine))
    encoder_grad = lax.psum_scatter(encoder_part, both, scatter_dimension=0, tiled=True).astype(F32)
    gn2 = add_halves(right_t(grad_query2, query2_w))
    gain2_rows = gn2 * hidden1 * inverse2
    grad_hidden1 = grad_hidden2 + norm_back(hidden1, inverse2, gain_two, gn2)
    grad_hidden1_b = grad_hidden1.astype(BF)
    out_grad = left_t(grad_hidden1_b, attended1).astype(BF)
    grad_attended1 = matmul(grad_hidden1_b, out_w).astype(BF)
    grad_query1, grad_key1, grad_value1 = attend_back(
        seen, query1, kv1, grad_attended1, attended1_t, lse1, causal_tiles
    )
    query_grad = left_t(normed1_pair, grad_query1).astype(BF)
    key_grad = left_t(normed1, grad_key1).astype(BF)
    value_grad = left_t(normed1, grad_value1).astype(BF)
    self_parts = [query_grad, key_grad, value_grad, out_grad]
    normed1_part = right_t(grad_key1, key_w) + right_t(grad_value1, value_w)
    query_part = right_t(grad_query1, query_w).reshape(ctx, rows, depth)
    cut = normed1_part.reshape(ctx, group, depth)
    old = lax.dynamic_slice_in_dim(cut, place * rows, rows, axis=1)
    cut = lax.dynamic_update_slice_in_dim(cut, old + query_part, place * rows, axis=1)
    cut = cut.reshape(total, depth).astype(BF)

    def gain_rows(gn1):
        gain1_sum = jnp.sum(gn1 * own_f * inverse1_own, axis=0)
        return jnp.stack(
            [gain1_sum] + [jnp.sum(mine(a), axis=0) for a in (gain2_rows, gain3_rows, gain4_rows)]
        )

    if fast:
        blocks = [
            [a.reshape(shards, depth // shards, a.shape[1]) for a in parts] for parts in (cross_parts, self_parts)
        ]
        gain1_part = jnp.sum(cut.astype(F32) * normed1.astype(F32), axis=0) / gain_one
        gains_part = [gain1_part] + [0.5 * jnp.sum(a, axis=0) for a in (gain2_rows, gain3_rows, gain4_rows)]
        gain_pad = jnp.stack(gains_part + [jnp.zeros_like(gain1_part)] * 4)
        gn1, cross_own, self_own, ff_own, gain_sums, emb_sums = tail_scatter(
            cut, blocks, ff_mine, gain_pad, emb_own, emb_move, [cuts[1], cuts[0], cuts[2]]
        )
        embedding_grad, inputs_grad, *weight_grads = finish(
            emb_sums, self_own, cross_own, ff_own, inputs, mine(grad_hidden1), gn1, gain_one[None],
            embedding.shape[0],
        )
    else:
        emb_halves = [jnp.where(core == 0, a, b)[:, :vocab_half] for a, b in ((emb_sum, emb_other), (emb_other, emb_sum))]
        embedding_grad = jnp.concatenate(emb_halves, axis=1).astype(F32)
        gn1 = lax.psum_scatter(cut, both, scatter_dimension=0, tiled=True).astype(F32)
        ff_grads = collect_weights(ff_part, [fb, fb, fb])
        cross_grads = collect_weights(jnp.concatenate(cross_parts, axis=1), [hb] * 4)
        self_grads = collect_weights(jnp.concatenate(self_parts, axis=1), [hb] * 4)
        gain_sums = lax.psum(gain_rows(gn1), ("shard", "ctx", "tp"))
        inputs_grad = mine(grad_hidden1) + norm_back(own_f, inverse1_own, gain_one, gn1)
        weight_grads = []
        for grads in (self_grads, cross_grads, ff_grads):
            weight_grads += grads
    part = depth // shards
    gain_grads = lax.dynamic_slice_in_dim(gain_sums, lax.axis_index("shard") * part, part, axis=1)
    return (
        final_own.astype(BF), exit_loss, inputs_grad, encoder_grad,
        gain_grads[0], *weight_grads[:3], weight_grads[3].T, gain_grads[1], *weight_grads[4:7], weight_grads[7].T,
        gain_grads[2], *weight_grads[8:10], weight_grads[10].T, gain_grads[3], embedding_grad.T,
    )


def solution(mesh):
    rows = P(("shard", "ctx", "tp"), None)
    into = P("shard", "tp")
    out = P("tp", "shard")
    gain = P("shard")
    weights = (gain, into, into, into, out, gain, into, into, into, out, gain, into, into, out, gain, out)
    return jax.shard_map(
        per_device,
        mesh=mesh,
        in_specs=(rows, rows, P("shard"), P(("shard", "ctx")), rows) + weights,
        out_specs=(rows, P(("shard", "ctx")), rows, rows) + weights,
        check_vma=False,
    )
```
